32 devices in a mesh: blk: 4 (over y, x), dp: 8 (over z, core).
Axes of the slice: x: 2, y: 2, z: 4, core: 2. Of those that a mesh axis runs over, the one named last changes fastest.
Arguments:
- item_ids: int32 [8, 2048], P('dp', 'blk'), may hold values from 0 to 2047
- pos_buckets: int32 [8, 2048], P('dp', 'blk'), may hold values from 0 to 63
- time_buckets: int32 [8, 2048], P('dp', 'blk'), may hold values from 0 to 63
- item_table: bfloat16 [2048, 512], P('dp'), may hold values from -6 to 6
- proj_in: float32 [512, 2048], P(('blk', 'dp')), may hold values from -0.25 to 0.25
- proj_out: float32 [512, 512], P(('blk', 'dp')), may hold values from -0.375 to 0.375
- small_params: float32 [6, 512], P(None, ('blk', 'dp')), may hold values from -4 to 4, as said below
- out_grad: bfloat16 [8, 2048, 512], P('dp', 'blk'), may hold values from -6 to 6
- moment_in: float32 [512, 2048], P(('blk', 'dp')), may hold values from -384 to 384
- second_in: float32 [512, 2048], P(('blk', 'dp')), may hold values from 4096 to 16384
- moment_out: float32 [512, 512], P(('blk', 'dp')), may hold values from -384 to 384
- second_out: float32 [512, 512], P(('blk', 'dp')), may hold values from 4096 to 16384
- moment_small: float32 [6, 512], P(None, ('blk', 'dp')), may hold values from -384 to 384
- second_small: float32 [6, 512], P(None, ('blk', 'dp')), may hold values from 4096 to 16384
Outputs:
- layer_out: bfloat16 [8, 2048, 512], P('dp', 'blk')
- input_grad: float32 [8, 2048, 512], P('dp', 'blk')
- table_grad: float32 [2048, 512], P(('blk', 'dp'))
- item_counts: float32 [2048], P(('blk', 'dp'))
- log_q: float32 [2048], P(('blk', 'dp'))
- new_moment_in: float32 [512, 2048], P(('blk', 'dp'))
- new_second_in: float32 [512, 2048], P(('blk', 'dp'))
- new_proj_in: float32 [512, 2048], P(('blk', 'dp'))
- new_moment_out: float32 [512, 512], P(('blk', 'dp'))
- new_second_out: float32 [512, 512], P(('blk', 'dp'))
- new_proj_out: float32 [512, 512], P(('blk', 'dp'))
- new_moment_small: float32 [6, 512], P(None, ('blk', 'dp'))
- new_second_small: float32 [6, 512], P(None, ('blk', 'dp'))
- new_small: float32 [6, 512], P(None, ('blk', 'dp'))
The draws below stay inside these ranges and needn't reach their ends.
Inputs may be any that keep to these rules, and one draw needn't show every extreme that they name: `small_params`: rows 0 and 2 lie near one, rows 1 and 3 near zero, rows 4 and 5 of order one.
All inputs are finite; a program needn't handle non-finite values.
Results may differ from the reference program's by a relative error of at most 0.012.
Values may be sent and summed in bfloat16 or wider, within the bound.
A program may use at most 128 MiB of HBM per device.

```python
import math
import jax
import jax.numpy as jnp
import numpy as np
from jax import lax

D = 512
H = 8
HEAD = 64
NB = 64
LEN = 2048
SEQS = 8
ITEMS = 2048


def draw_small_params(key, part):
    key_gain = jax.random.fold_in(key, 11)
    key_shift = jax.random.fold_in(key, 12)
    key_table = jax.random.fold_in(key, 13)
    gain_rows = jax.random.uniform(key_gain, (2, D), jnp.float32, 0.7, 1.3)
    shift_rows = jnp.clip(0.2 * jax.random.normal(key_shift, (2, D), jnp.float32), -0.8, 0.8)
    bias_tables = jnp.clip(jax.random.normal(key_table, (2, D), jnp.float32), -4.0, 4.0)
    return jnp.stack([gain_rows[0], shift_rows[0], gain_rows[1], shift_rows[1], bias_tables[0], bias_tables[1]])


def set_ends(drawn, rng, least, high):
    spot = [jax.random.randint(jax.random.fold_in(rng, axis), (), 0, length) for axis, length in enumerate(drawn.shape)]
    main_axis = drawn.shape.index(max(drawn.shape))
    beside = spot[:main_axis] + [(spot[main_axis] + 1) % drawn.shape[main_axis]] + spot[main_axis + 1:]
    return drawn.at[tuple(spot)].set(least).at[tuple(beside)].set(high)


def block_levels(own_key, dims, cuts, smallest, top_value):
    loudness = 1.0
    for position, blocks in cuts:
        draws = jax.random.uniform(jax.random.fold_in(jax.random.fold_in(own_key, 6), position), (blocks,), jnp.float32, smallest / len(cuts), top_value / len(cuts))
        loudness = loudness * jnp.repeat(jnp.exp(draws), dims[position] // blocks).reshape((-1,) + (1,) * (len(dims) - 1 - position))
    return loudness


def rank_table(number_of, skew):
    portions = [(1 << 20) // math.isqrt(standing ** skew) + 1 for standing in range(1, number_of + 1)]
    width = 1 + sum(portions) // (1 << 30)
    return np.cumsum(np.array([max(1, weight // width) for weight in portions]))


def ranked(stream_key, dims, amount, lean):
    table = rank_table(amount, lean)
    ticket = jax.random.randint(jax.random.fold_in(stream_key, 1), dims, 0, int(table[amount - 1]))
    rank = jnp.searchsorted(jnp.asarray(table, jnp.int32), ticket, side="right")
    return jax.random.permutation(jax.random.fold_in(stream_key, 2), amount)[rank].astype(jnp.int32)


def scatter_about(key, dims, spread, bound, pieces=(), kind=jnp.bfloat16):
    drawn = jax.random.normal(key, dims, jnp.float32) * spread
    if len(pieces) > 0:
        drawn = block_levels(key, dims, pieces, -0.22, 0.18) * drawn
    return jnp.clip(drawn, min=-bound, max=bound).astype(kind)


def setup_inputs(seed: int = 0) -> dict:
    key_of = jax.random.split(jax.random.key(seed), 15)
    item_ids = set_ends(ranked(key_of[0], (SEQS, LEN), ITEMS, 2), jax.random.fold_in(key_of[0], 3), 0, ITEMS - 1).astype(jnp.int32)
    pos_buckets = set_ends(jax.random.randint(key_of[1], (SEQS, LEN), 0, NB), jax.random.fold_in(key_of[1], 1), 0, NB - 1).astype(jnp.int32)
    time_buckets = set_ends(jax.random.randint(key_of[2], (SEQS, LEN), 0, NB), jax.random.fold_in(key_of[2], 1), 0, NB - 1).astype(jnp.int32)
    item_table = scatter_about(key_of[3], (ITEMS, D), 1.0, 6.0, ((0, 8),))
    proj_in = scatter_about(key_of[4], (D, 4 * D), D ** -0.5, 0.25, ((0, 32),), jnp.float32)
    proj_out = scatter_about(key_of[5], (D, D), (D // 2) ** -0.5, 0.375, ((0, 32),), jnp.float32)
    small_params = draw_small_params(jax.random.fold_in(key_of[14], 71), 0)
    out_grad = scatter_about(key_of[7], (SEQS, LEN, D), 1.0, 6.0, ((0, 8), (1, 4)))
    moment_in = scatter_about(key_of[8], (D, 4 * D), (0.5 * (SEQS * LEN) ** 0.5), 384.0, ((0, 32),), jnp.float32)
    second_in = jnp.clip(jnp.exp(math.log(16384.0) - 1.3862944 * jax.random.uniform(key_of[9], (D, 4 * D), jnp.float32) ** block_levels(key_of[9], (D, 4 * D), ((0, 32),), -0.2, 0.2)), 4096.0, 16384.0)
    moment_out = scatter_about(key_of[10], (D, D), (0.5 * (SEQS * LEN) ** 0.5), 384.0, ((0, 32),), jnp.float32)
    second_out = jnp.clip(jnp.exp(math.log(16384.0) - 1.3862944 * jax.random.uniform(key_of[11], (D, D), jnp.float32) ** block_levels(key_of[11], (D, D), ((0, 32),), -0.2, 0.2)), 4096.0, 16384.0)
    moment_small = scatter_about(key_of[12], (6, D), (0.5 * (SEQS * LEN) ** 0.5), 384.0, ((1, 32),), jnp.float32)
    second_small = jnp.clip(jnp.exp(math.log(16384.0) - 1.3862944 * jax.random.uniform(key_of[13], (6, D), jnp.float32) ** block_levels(key_of[13], (6, D), ((1, 32),), -0.2, 0.2)), 4096.0, 16384.0)
    return {"item_ids": item_ids, "pos_buckets": pos_buckets, "time_buckets": time_buckets, "item_table": item_table, "proj_in": proj_in, "proj_out": proj_out, "small_params": small_params, "out_grad": out_grad, "moment_in": moment_in, "second_in": second_in, "moment_out": moment_out, "second_out": second_out, "moment_small": moment_small, "second_small": second_small}


@jax.custom_vjp
def low(v):
    return lax.optimization_barrier(v.astype(jnp.bfloat16)).astype(jnp.float32)

@jax.custom_vjp
def low_back(v):
    return v

def low_keep(v):
    return (low(v), None)

def low_pass(kept, grad):
    return (grad,)

def back_keep(v):
    return (v, None)

def back_low(kept, grad):
    return (low(grad),)
low.defvjp(low_keep, low_pass)
low_back.defvjp(back_keep, back_low)
norm_eps = 1e-05
beta_first = 0.5
beta_second = 0.5
adam_eps = 1e-08
weight_decay = 0.01
rate_in = 0.05
rate_out = 0.06
rate_small = 0.3
step_number = 3
highest = lax.Precision.HIGHEST

def layer_norm(values, gain, shift):
    centered = values - lax.optimization_barrier(jnp.mean(values, axis=-1, keepdims=True))
    variance = lax.optimization_barrier(jnp.mean(centered * centered, axis=-1, keepdims=True))
    return centered * lax.rsqrt(variance + norm_eps) * gain + shift

def sequence_layer(embedded, weight_in, weight_out, small, pos_row, time_row):
    copy_in = low(weight_in)
    copy_out = low(weight_out)
    copy_small = low(small)
    normed = low(layer_norm(embedded, copy_small[0], copy_small[1]))
    projected = low_back(jnp.dot(normed, copy_in, precision=highest))
    activated = jax.nn.silu(projected)
    gate_u = activated[:, :D]
    rounded = low(activated[:, D:])
    values = rounded[:, :D].reshape(LEN, H, HEAD)
    queries = rounded[:, D:2 * D].reshape(LEN, H, HEAD)
    keys_all = rounded[:, 2 * D:].reshape(LEN, H, HEAD)
    pos_table = copy_small[4].reshape(H, NB)
    time_table = copy_small[5].reshape(H, NB)
    key_bias = pos_table[:, pos_row]
    query_bias = time_table[:, time_row]
    positions = jnp.arange(LEN, dtype=jnp.int32)
    rows_blk = math.gcd(LEN, 512)
    count_blk = LEN // rows_blk

    def attend_block(operands):
        query_blk, bias_blk, place_blk = operands
        scores = jnp.einsum('ihd,jhd->hij', query_blk, keys_all, precision=highest) * HEAD ** (-0.5)
        scores = low_back(scores + bias_blk[:, :, None] + key_bias[:, None, :])
        allowed = place_blk[:, None] >= positions[None, :]
        weights = low(jnp.where(allowed[None], jax.nn.silu(scores) / LEN, 0.0))
        return jnp.einsum('hij,jhd->ihd', weights, values, precision=highest)
    mixed = lax.map(jax.checkpoint(attend_block), (queries.reshape(count_blk, rows_blk, H, HEAD), query_bias.reshape(H, count_blk, rows_blk).transpose(1, 0, 2), positions.reshape(count_blk, rows_blk)))
    attended = low_back(mixed.reshape(LEN, D))
    normed_two = layer_norm(attended, copy_small[2], copy_small[3])
    gated = low(normed_two * gate_u)
    return embedded + jnp.dot(gated, copy_out, precision=highest)

def adam_update(weight, grad, moment, second, rate):
    new_moment = beta_first * moment + (1.0 - beta_first) * grad
    new_second = beta_second * second + (1.0 - beta_second) * grad * grad
    moment_hat = new_moment / (1.0 - beta_first ** step_number)
    second_hat = new_second / (1.0 - beta_second ** step_number)
    new_weight = weight - rate * (moment_hat / (jnp.sqrt(second_hat) + adam_eps) + weight_decay * weight)
    return (new_moment, new_second, new_weight)

def reference(item_ids, pos_buckets, time_buckets, item_table, proj_in, proj_out, small_params, out_grad, moment_in, second_in, moment_out, second_out, moment_small, second_small):
    table_float = item_table.astype(jnp.float32)

    def one_history(carried, operands):
        ids_row, pos_row, time_row, grad_row = operands
        embedded = table_float[ids_row]

        def forward(embed_arg, weight_in, weight_out, small):
            return sequence_layer(embed_arg, weight_in, weight_out, small, pos_row, time_row)
        result, pullback = jax.vjp(forward, embedded, proj_in, proj_out, small_params)
        grad_embed, grad_in, grad_out, grad_small = pullback(grad_row.astype(jnp.float32))
        carried = (carried[0] + grad_in, carried[1] + grad_out, carried[2] + grad_small)
        return (carried, (result.astype(jnp.bfloat16), grad_embed))
    zeros_init = (jnp.zeros((D, 4 * D), jnp.float32), jnp.zeros((D, D), jnp.float32), jnp.zeros((6, D), jnp.float32))
    (grad_in, grad_out, grad_small), (layer_out, input_grad) = lax.scan(one_history, zeros_init, (item_ids, pos_buckets, time_buckets, out_grad))
    flat_ids = item_ids.reshape(-1)
    table_grad = jnp.zeros((ITEMS, D), jnp.float32).at[flat_ids].add(low(input_grad).reshape(-1, D))
    item_counts = jnp.zeros((ITEMS,), jnp.float32).at[flat_ids].add(1.0)
    log_q = jnp.log(jnp.maximum(item_counts, 1.0) / (SEQS * LEN))
    new_moment_in, new_second_in, new_proj_in = adam_update(proj_in, grad_in, moment_in, second_in, rate_in)
    new_moment_out, new_second_out, new_proj_out = adam_update(proj_out, grad_out, moment_out, second_out, rate_out)
    new_moment_small, new_second_small, new_small = adam_update(small_params, grad_small, moment_small, second_small, rate_small)
    return (layer_out, input_grad, table_grad, item_counts, log_q, new_moment_in, new_second_in, new_proj_in, new_moment_out, new_second_out, new_proj_out, new_moment_small, new_second_small, new_small)
```

```python
import functools
import math

import jax
import jax.numpy as jnp
from jax import lax
from jax.experimental import pallas as pl
from jax.experimental.pallas import tpu as pltpu
from jax.sharding import PartitionSpec as P

D = 512
H = 8
HEAD = 64
NB = 64


norm_eps = 1e-05
beta_first = 0.5
beta_second = 0.5
adam_eps = 1e-08
weight_decay = 0.01
rate_in = 0.05
rate_out = 0.06
rate_small = 0.3
step_number = 3


def standardize(values):
    centered = values - jnp.mean(values, axis=-1, keepdims=True)
    inverse = lax.rsqrt(jnp.mean(centered * centered, axis=-1, keepdims=True) + norm_eps)
    return (centered * inverse, inverse)


def norm_back(grad_hat, normal_hat, inverse):
    mean_grad = jnp.mean(grad_hat, axis=-1, keepdims=True)
    mean_cross = jnp.mean(grad_hat * normal_hat, axis=-1, keepdims=True)
    return (grad_hat - mean_grad - normal_hat * mean_cross) * inverse


def silu_slope(values):
    logistic = jax.nn.sigmoid(values)
    return logistic * (1.0 + values * (1.0 - logistic))


def adam_update(weight, grad, moment, second, rate):
    new_moment = beta_first * moment + (1.0 - beta_first) * grad
    new_second = beta_second * second + (1.0 - beta_second) * grad * grad
    moment_hat = new_moment / (1.0 - beta_first**step_number)
    second_hat = new_second / (1.0 - beta_second**step_number)
    new_weight = weight - rate * (
        moment_hat / (jnp.sqrt(second_hat) + adam_eps) + weight_decay * weight
    )
    return (new_moment, new_second, new_weight)


def by_events(
    item_ids,
    pos_buckets,
    time_buckets,
    item_table,
    proj_in,
    proj_out,
    small_params,
    out_grad,
    moment_in,
    second_in,
    moment_out,
    second_out,
    moment_small,
    second_small,
):
    seq_count, group = item_ids.shape
    length = group * lax.axis_size("blk")
    devices = lax.axis_size("blk") * lax.axis_size("dp")
    items = item_table.shape[0] * lax.axis_size("dp")
    tokens = seq_count * group
    scale = HEAD ** (-0.5)
    copy_in, copy_out, copy_small = (
        lax.all_gather(proj_in.astype(jnp.bfloat16), ("blk", "dp"), axis=0, tiled=True),
        lax.all_gather(proj_out.astype(jnp.bfloat16), ("blk", "dp"), axis=0, tiled=True),
        lax.all_gather(small_params.astype(jnp.bfloat16), ("blk", "dp"), axis=1, tiled=True),
    )
    small_float = copy_small.astype(jnp.float32)
    flat_ids = item_ids.reshape(tokens)
    portion = lax.all_gather(item_table, "dp", axis=0, tiled=True)
    hot = (flat_ids[:, None] == jnp.arange(portion.shape[0], dtype=jnp.int32)[None, :]).astype(
        jnp.bfloat16
    )
    embedded = jnp.dot(hot, portion, preferred_element_type=jnp.float32)
    hat_one, inverse_one = standardize(embedded)
    normed = (hat_one * small_float[0] + small_float[1]).astype(jnp.bfloat16)
    projected = jnp.dot(normed, copy_in, preferred_element_type=jnp.float32)
    activated = jax.nn.silu(projected)
    gate_u = activated[:, :D]
    rounded = activated[:, D:].astype(jnp.bfloat16)
    values = rounded[:, :D].reshape(seq_count, group, H, HEAD)
    queries = rounded[:, D : 2 * D].reshape(seq_count, group, H, HEAD)
    keys_own = rounded[:, 2 * D :].reshape(seq_count, group, H, HEAD)
    pos_table = small_float[4].reshape(H, NB)
    time_table = small_float[5].reshape(H, NB)
    buckets = jnp.arange(NB, dtype=jnp.int32)
    time_hot = (time_buckets[:, :, None] == buckets).astype(jnp.float32)
    query_bias = jnp.einsum("scb,hb->shc", time_hot, time_table)
    query_first = lax.axis_index("blk") * group
    query_pos = query_first + jnp.arange(group, dtype=jnp.int32)
    query_last = query_first + group - 1
    pos_sent = pos_buckets.astype(jnp.bfloat16)

    def tile_scores(key_blk, bucket_blk, key_start):
        pos_hot = (bucket_blk.astype(jnp.int32)[:, :, None] == buckets).astype(jnp.float32)
        key_bias = jnp.einsum("sjb,hb->shj", pos_hot, pos_table)
        raw_scores = (
            jnp.einsum("sihd,sjhd->shij", queries, key_blk, preferred_element_type=jnp.float32)
            * scale
        )
        raw_scores = raw_scores + query_bias[:, :, :, None] + key_bias[:, :, None, :]
        key_pos = key_start + jnp.arange(key_blk.shape[1], dtype=jnp.int32)
        allowed = (query_pos[:, None] >= key_pos[None, :])[None, None]
        return (raw_scores, allowed, pos_hot)

    attend_init = jnp.zeros((seq_count, group, H, HEAD), jnp.float32)
    running = attend_init
    key_part = lax.all_gather(keys_own, "blk", axis=1, tiled=True)
    value_part = lax.all_gather(values, "blk", axis=1, tiled=True)
    bucket_part = lax.all_gather(pos_sent, "blk", axis=1, tiled=True)
    span = key_part.shape[1]
    rows_blk = math.gcd(span, 512)

    def fold_step(carried, block_idx):
        key_start = block_idx * rows_blk
        key_blk = lax.dynamic_slice_in_dim(key_part, key_start, rows_blk, 1)
        value_blk = lax.dynamic_slice_in_dim(value_part, key_start, rows_blk, 1)
        bucket_blk = lax.dynamic_slice_in_dim(bucket_part, key_start, rows_blk, 1)

        def fold_compute(current):
            raw_scores, allowed, pos_hot = tile_scores(key_blk, bucket_blk, key_start)
            weights = jnp.where(allowed, jax.nn.silu(raw_scores) / length, 0.0).astype(jnp.bfloat16)
            return current + jnp.einsum(
                "shij,sjhd->sihd", weights, value_blk, preferred_element_type=jnp.float32
            )

        return (
            lax.cond(key_start <= query_last, fold_compute, lambda current: current, carried),
            None,
        )

    running, _ = lax.scan(fold_step, running, jnp.arange(span // rows_blk, dtype=jnp.int32))
    attended = running
    attended = attended.reshape(tokens, D)
    hat_two, inverse_two = standardize(attended)
    normed_two = hat_two * small_float[2] + small_float[3]
    gated = (normed_two * gate_u).astype(jnp.bfloat16)
    result = embedded + jnp.dot(gated, copy_out, preferred_element_type=jnp.float32)
    layer_out = result.astype(jnp.bfloat16).reshape(seq_count, group, D)
    cotangent = out_grad.reshape(tokens, D)
    grad_out_weight = jnp.einsum("td,te->de", gated, cotangent, preferred_element_type=jnp.float32)
    grad_gated = jnp.einsum("te,de->td", cotangent, copy_out, preferred_element_type=jnp.float32)
    grad_u = grad_gated * normed_two
    grad_norm_two = grad_gated * gate_u
    grad_gain_two = jnp.sum(grad_norm_two * hat_two, axis=0)
    grad_shift_two = jnp.sum(grad_norm_two, axis=0)
    grad_attended = norm_back(grad_norm_two * small_float[2], hat_two, inverse_two).astype(
        jnp.bfloat16
    )
    grad_attended = grad_attended.reshape(seq_count, group, H, HEAD)
    key_whole, value_whole, bucket_whole = (
        lax.all_gather(keys_own, "blk", axis=1, tiled=True),
        lax.all_gather(values, "blk", axis=1, tiled=True),
        lax.all_gather(pos_sent, "blk", axis=1, tiled=True),
    )
    rows_back = math.gcd(length, 512)

    def back_step(carried, block_idx):
        grad_query, grad_pos, grad_qbias = carried
        key_start = block_idx * rows_back
        key_blk = lax.dynamic_slice_in_dim(key_whole, key_start, rows_back, 1)
        value_blk = lax.dynamic_slice_in_dim(value_whole, key_start, rows_back, 1)
        bucket_blk = lax.dynamic_slice_in_dim(bucket_whole, key_start, rows_back, 1)

        def back_compute(operand):
            raw_scores, allowed, pos_hot = tile_scores(key_blk, bucket_blk, key_start)
            grad_weights = jnp.einsum(
                "sihd,sjhd->shij", grad_attended, value_blk, preferred_element_type=jnp.float32
            )
            grad_raw = jnp.where(
                allowed, grad_weights / length * silu_slope(raw_scores), 0.0
            ).astype(jnp.bfloat16)
            grad_raw_float = grad_raw.astype(jnp.float32)
            part_query = (
                jnp.einsum("shij,sjhd->sihd", grad_raw, key_blk, preferred_element_type=jnp.float32)
                * scale
            )
            part_pos = jnp.einsum("shj,sjb->hb", jnp.sum(grad_raw_float, axis=2), pos_hot)
            part_qbias = jnp.sum(grad_raw_float, axis=3)
            weights = jnp.where(allowed, jax.nn.silu(raw_scores) / length, 0.0).astype(jnp.bfloat16)
            part_key = (
                jnp.einsum("shij,sihd->sjhd", grad_raw, queries, preferred_element_type=jnp.float32)
                * scale
            )
            part_value = jnp.einsum(
                "shij,sihd->sjhd", weights, grad_attended, preferred_element_type=jnp.float32
            )
            paired = jnp.concatenate(
                [
                    part_key.reshape(seq_count, rows_back, D),
                    part_value.reshape(seq_count, rows_back, D),
                ],
                axis=-1,
            )
            return (part_query, part_pos, part_qbias, paired)

        def skip_tile(operand):
            empty = (
                jnp.zeros((seq_count, group, H, HEAD), jnp.float32),
                jnp.zeros((H, NB), jnp.float32),
                jnp.zeros((seq_count, H, group), jnp.float32),
            )
            return empty + (jnp.zeros((seq_count, rows_back, 2 * D), jnp.float32),)

        parts = lax.cond(key_start <= query_last, back_compute, skip_tile, 0)
        summed = (grad_query + parts[0], grad_pos + parts[1], grad_qbias + parts[2])
        return (summed, parts[3])

    back_init = (
        jnp.zeros((seq_count, group, H, HEAD), jnp.float32),
        jnp.zeros((H, NB), jnp.float32),
        jnp.zeros((seq_count, H, group), jnp.float32),
    )
    (grad_query, grad_pos_table, grad_qbias), stacked = lax.scan(
        back_step, back_init, jnp.arange(length // rows_back, dtype=jnp.int32)
    )
    kv_terms = stacked.transpose(1, 0, 2, 3).reshape(seq_count, length, 2 * D)
    kv_own = lax.psum_scatter(kv_terms, "blk", scatter_dimension=1, tiled=True)
    grad_key = kv_own[:, :, :D].reshape(tokens, D)
    grad_value = kv_own[:, :, D:].reshape(tokens, D)
    grad_time_table = jnp.einsum("shc,scb->hb", grad_qbias, time_hot)
    grad_acts = jnp.concatenate(
        [grad_u, grad_value, grad_query.reshape(tokens, D), grad_key], axis=-1
    )
    grad_pre = (grad_acts * silu_slope(projected)).astype(jnp.bfloat16)
    grad_in_weight = jnp.einsum("td,tf->df", normed, grad_pre, preferred_element_type=jnp.float32)
    grad_normed = jnp.einsum("tf,df->td", grad_pre, copy_in, preferred_element_type=jnp.float32)
    grad_gain_one = jnp.sum(grad_normed * hat_one, axis=0)
    grad_shift_one = jnp.sum(grad_normed, axis=0)
    grad_embed = cotangent.astype(jnp.float32) + norm_back(
        grad_normed * small_float[0], hat_one, inverse_one
    )
    input_grad = grad_embed.reshape(seq_count, group, D)
    grad_small = jnp.stack(
        [
            grad_gain_one,
            grad_shift_one,
            grad_gain_two,
            grad_shift_two,
            grad_pos_table.reshape(D),
            grad_time_table.reshape(D),
        ]
    )
    counts_local = jnp.sum(
        (flat_ids[:, None] == jnp.arange(items, dtype=jnp.int32)[None, :]).astype(jnp.float32),
        axis=0,
    )
    shard_in, shard_out, shard_small, item_counts = (
        lax.psum_scatter(grad_in_weight, ("blk", "dp"), scatter_dimension=0, tiled=True),
        lax.psum_scatter(grad_out_weight, ("blk", "dp"), scatter_dimension=0, tiled=True),
        lax.psum_scatter(grad_small, ("blk", "dp"), scatter_dimension=1, tiled=True),
        lax.psum_scatter(counts_local, ("blk", "dp"), scatter_dimension=0, tiled=True),
    )
    grad_rounded = grad_embed.astype(jnp.bfloat16)
    hot = (
        flat_ids[:, None]
        == jnp.arange(items // devices * lax.axis_size(("blk", "dp")), dtype=jnp.int32)[None, :]
    ).astype(jnp.bfloat16)
    table_grad = lax.psum_scatter(
        jnp.einsum("tr,td->rd", hot, grad_rounded, preferred_element_type=jnp.float32),
        ("blk", "dp"),
        scatter_dimension=0,
        tiled=True,
    )
    log_q = jnp.log(jnp.maximum(item_counts, 1.0) / (seq_count * lax.axis_size("dp") * length))
    new_moment_in, new_second_in, new_proj_in = adam_update(
        proj_in, shard_in, moment_in, second_in, rate_in
    )
    new_moment_out, new_second_out, new_proj_out = adam_update(
        proj_out, shard_out, moment_out, second_out, rate_out
    )
    new_moment_small, new_second_small, new_small = adam_update(
        small_params, shard_small, moment_small, second_small, rate_small
    )
    return (
        layer_out,
        input_grad,
        table_grad,
        item_counts,
        log_q,
        new_moment_in,
        new_second_in,
        new_proj_in,
        new_moment_out,
        new_second_out,
        new_proj_out,
        new_moment_small,
        new_second_small,
        new_small,
    )


MESH = pl.DeviceIdType.MESH
F32, BF16, I32 = jnp.float32, jnp.bfloat16, jnp.int32
LANES = 128
NN = (((1,), (0,)), ((), ()))
NT = (((1,), (1,)), ((), ()))
TN = (((0,), (0,)), ((), ()))


def mm(lhs, rhs, dims=NN):
    return lax.dot_general(lhs, rhs, dims, preferred_element_type=F32)


def iota(shape, dim):
    return lax.broadcasted_iota(I32, shape, dim)


def at(index, size):
    return pl.ds(pl.multiple_of(index * size, size), size)


def fused_kernel(sizes, *refs):
    nb, nz, group, items, weight_rows, tokens = sizes
    nd = nz * 2
    length = nb * group
    part = D // nb
    rows_table = items // (nb * nd)
    (
        ids_in, pos_in, time_in, table_in, proj_in, proj_out, small_in, out_grad_in,
        moment_in, second_in, moment_out, second_out, moment_small, second_small,
        layer_out, input_grad, table_grad, counts_out, logq_out,
        new_m_in, new_s_in, new_w_in, new_m_out, new_s_out, new_w_out,
        new_m_small, new_s_small, new_w_small,
        send, recv, local,
        index, column, padded, table, weight, weight_send, outw, small, small_all, cot,
        embedded, normed, projected, gate, value, query, key, attended,
        grad_gated, stats, fix, gated_send, gated_got, grad_att, dq, dk, dv,
        grad_pre, part_send, part_got, stats_one, ig_send, ig_got, bias_sum, gain_sum,
        table_sum, table_core, table_z, table_zgot, table_own, table_got,
        gi_sum, gi_core, gi_z, gi_zgot, gi_own, gi_got,
        go_sum, go_core, go_z, go_zgot, little, little_core, little_z, little_zgot, little_all,
    ) = refs
    b = lax.axis_index("blk")
    d = lax.axis_index("dp")
    z, core = d // 2, d % 2
    other = 1 - core

    counter = [0]

    def slots(count):
        base = counter[0]
        counter[0] += count
        return base

    def copy(src, dst, slot, target):
        return pltpu.make_async_remote_copy(
            src_ref=src, dst_ref=dst, send_sem=send.at[slot], recv_sem=recv.at[slot],
            device_id={"blk": target[0], "dp": target[1]}, device_id_type=MESH,
        )

    def blk_peer(k):
        return (lax.rem(b + k, nb), d)

    def blk_from(k):
        return lax.rem(b + nb - k, nb)

    def z_to(k):
        return lax.rem(z + k, nz)

    def z_from(k):
        return lax.rem(z + nz - k, nz)

    def z_peer(k):
        return (b, z_to(k) * 2 + core)

    core_peer = (b, z * 2 + other)

    pending = []

    def push(src, dst, slot, target):
        made = copy(src, dst, slot, target)
        made.start()
        pending.append((src, dst, slot, target))

    def arrive(dst, slot):
        copy(dst, dst, slot, core_peer).wait_recv()

    table_load = pltpu.make_async_copy(table_in, table.at[d], local.at[0])
    table_load.start()
    cot_load = pltpu.make_async_copy(out_grad_in, cot.at[b], local.at[1])
    cot_load.start()

    index[b] = jnp.concatenate(
        [ids_in[...], pos_in[...], time_in[...], jnp.zeros((5, group), I32)], axis=0
    )
    own_rows = proj_in[...].astype(BF16)
    for q in range(nb):
        weight_send[q] = jnp.concatenate(
            [own_rows[:, s * D + q * part : s * D + (q + 1) * part] for s in range(4)], axis=1
        )
    weight[b, d] = weight_send[b]
    outw[b, d] = proj_out[...].astype(BF16)
    width = small_in.shape[1]
    spread = (iota((width, LANES), 1) == iota((width, LANES), 0) + d * width).astype(F32)
    small_pad = jnp.concatenate([small_in[...], jnp.zeros((10, width), F32)], axis=0)
    small[b, d] = mm(small_pad.astype(BF16), spread.astype(BF16)).astype(BF16)

    barrier = pltpu.get_barrier_semaphore()
    peers = [blk_peer(k) for k in range(1, nb)] + [z_peer(k) for k in range(1, nz)] + [core_peer]
    for target in peers:
        pl.semaphore_signal(
            barrier, inc=1, device_id={"blk": target[0], "dp": target[1]}, device_id_type=MESH
        )
    pl.semaphore_wait(barrier, len(peers))

    s_index, s_w, s_s, s_o = slots(nb), slots(nb), slots(nb), slots(nb)
    for k in range(1, nb):
        to = blk_peer(k)
        push(index.at[b], index.at[b], s_index + k, to)
        push(weight_send.at[to[0]], weight.at[b, d], s_w + k, to)
        push(small.at[b, d], small.at[b, d], s_s + k, to)
        push(outw.at[b, d], outw.at[b, d], s_o + k, to)
    table_load.wait()
    s_tz, s_tx, s_tc = slots(nz), slots(nz * nb), slots(nz * nb)
    for k in range(1, nz):
        push(table.at[d, b], table.at[d, b], s_tz + k, z_peer(k))
    push(table.at[d], table.at[d], s_tc, core_peer)
    s_wz, s_wc = slots(nz * 3), slots(nz * 3)
    gathered = (weight, small, outw)
    firsts = (s_w, s_s, s_o)
    for n, (buffer, first) in enumerate(zip(gathered, firsts)):
        for k in range(1, nb):
            arrive(buffer.at[blk_from(k), d], first + k)
        for k in range(1, nz):
            push(buffer.at[:, d], buffer.at[:, d], s_wz + n * nz + k, z_peer(k))
        push(buffer.at[:, d], buffer.at[:, d], s_wc + n * nz, core_peer)
    for k in range(1, nz):
        shard = z_from(k) * 2 + core
        arrive(table.at[shard, b], s_tz + k)
        for m in range(1, nb):
            push(table.at[shard, b], table.at[shard, b], s_tx + k * nb + m, blk_peer(m))
        push(table.at[shard, b], table.at[shard, b], s_tc + k * nb, core_peer)
    for n, buffer in enumerate(gathered):
        for k in range(1, nz):
            shard = z_from(k) * 2 + core
            arrive(buffer.at[:, shard], s_wz + n * nz + k)
            push(buffer.at[:, shard], buffer.at[:, shard], s_wc + n * nz + k, core_peer)
    for k in range(1, nz):
        shard = z_from(k) * 2 + core
        for m in range(1, nb):
            arrive(table.at[shard, blk_from(m)], s_tx + k * nb + m)
            push(table.at[shard, blk_from(m)], table.at[shard, blk_from(m)], s_tc + k * nb + m, core_peer)
    cot_load.wait()
    s_g = slots(nb)
    for k in range(1, nb):
        push(cot.at[b], cot.at[b], s_g + k, blk_peer(k))

    for k in range(1, nb):
        arrive(index.at[blk_from(k)], s_index + k)
    padded[...] = jnp.zeros(padded.shape, F32)

    def to_column(e, carry):
        padded[0:8, :] = index[e].astype(F32)
        column[at(e, group), :] = jnp.transpose(padded[...]).astype(I32)
        return carry

    lax.fori_loop(0, nb, to_column, 0)

    for n, buffer in enumerate(gathered):
        for k in range(0, nz):
            arrive(buffer.at[:, z_from(k) * 2 + other], s_wc + n * nz + k)
    arrive(table.at[z * 2 + other], s_tc)
    for k in range(1, nz):
        shard = z_from(k) * 2 + other
        arrive(table.at[shard, b], s_tc + k * nb)
        for m in range(1, nb):
            arrive(table.at[shard, blk_from(m)], s_tc + k * nb + m)

    for q in range(nb):
        total = small[q, 0].astype(F32)
        for r in range(1, nd):
            total = total + small[q, r].astype(F32)
        small_all[q] = total
    gain_one = jnp.concatenate([small_all[q][0:1] for q in range(nb)], axis=1)
    shift_one = jnp.concatenate([small_all[q][1:2] for q in range(nb)], axis=1)
    mine = small_all[b]
    gain_one_own = mine[0:1]
    gain_two, shift_two = mine[2:3], mine[3:4]
    pos_row, time_row = mine[4:5], mine[5:6]
    lane = iota((1, LANES), 1)
    low = lane < NB
    pos_rows = (0.5 * pltpu.roll(pos_row, NB, 1), 0.5 * pos_row)
    time_rows = (0.5 * time_row, 0.5 * pltpu.roll(time_row, NB, 1))
    masks = (low, lane >= NB)

    step = 256

    def embed(t, carry):
        rows = at(t, step)
        picked = column[rows, 0:1]
        hot = jnp.where(iota((step, items), 1) == picked, 1.0, 0.0).astype(BF16)
        found = mm(hot, table[...].reshape(items, D))
        embedded[rows, :] = found.astype(BF16)
        mean = jnp.mean(found, axis=1, keepdims=True)
        centered = found - mean
        inverse = lax.rsqrt(jnp.mean(centered * centered, axis=1, keepdims=True) + norm_eps)
        fix[rows, :] = jnp.where(lane == 0, mean, inverse)
        ready = (centered * inverse * gain_one + shift_one).astype(BF16)
        normed[rows, :] = ready
        raw = mm(ready, weight[...].reshape(D, 4 * part))
        projected[rows, :] = raw
        act = raw * (0.5 + 0.5 * jnp.tanh(0.5 * raw))
        gate[rows, :] = act[:, 0:part]
        value[rows, :] = act[:, part : 2 * part].astype(BF16)
        queries = act[:, 2 * part : 3 * part].astype(BF16).astype(F32) * (0.5 * HEAD**-0.5)
        keys = act[:, 3 * part :].astype(BF16)
        time_hot = jnp.where(lane == column[rows, 2:3], 1.0, 0.0)
        pos_hot = jnp.where(lane == column[rows, 1:2] + NB, 1.0, 0.0)
        for h in range(2):
            query[h, rows, 0:LANES] = jnp.where(masks[h], queries, 0.0).astype(BF16)
            query[h, rows, LANES:] = jnp.where(low, time_hot, pos_rows[h]).astype(BF16)
            key[h, rows, 0:LANES] = keys
            key[h, rows, LANES:] = jnp.where(low, time_rows[h], pos_hot).astype(BF16)
        return carry

    lax.fori_loop(0, length // step, embed, 0)
    out_rows = outw[b].reshape(part, D)
    for k in range(1, nb):
        arrive(cot.at[blk_from(k)], s_g + k)

    s_st = slots(nb * nb)
    inv_length = 1.0 / length

    def forward(r, carry):
        i = nb - 1 - r
        rows = at(i, group)
        dq[...] = jnp.zeros(dq.shape, F32)

        def tile(j, masked):
            cols = at(j, group)
            for h in range(2):
                x = mm(query[h, rows, :], key[h, cols, :], NT)
                w = x + x * jnp.tanh(x)
                if masked:
                    w = jnp.where(iota(w.shape, 0) >= iota(w.shape, 1), w, 0.0)
                dq[h, :, 0:LANES] += mm(w.astype(BF16), value[cols, :])

        def full(j, inner):
            tile(j, False)
            return inner

        lax.fori_loop(0, i, full, 0)
        tile(i, True)
        att = jnp.where(low, dq[0, :, 0:LANES], dq[1, :, 0:LANES]) * inv_length
        attended[rows, :] = att
        gg = mm(cot[i], out_rows, NT)
        grad_gated[rows, :] = gg
        g = gg * gate[rows, :] * gain_two
        mean = jnp.mean(att, axis=1, keepdims=True)
        centered = att - mean
        square = jnp.sum(centered * centered, axis=1, keepdims=True)
        sum_g = jnp.sum(g, axis=1, keepdims=True)
        sum_ga = jnp.sum(g * centered, axis=1, keepdims=True)
        packed = jnp.where(
            lane == 0, mean, jnp.where(lane == 1, square, jnp.where(lane == 2, sum_g, sum_ga))
        )
        stats[b, i] = jnp.transpose(packed)[0:8]
        for k in range(1, nb):
            copy(stats.at[b, i], stats.at[b, i], s_st + i * nb + k, blk_peer(k)).start()
        return carry

    lax.fori_loop(0, nb, forward, 0)

    s_ps, s_s1 = slots(nb * nb), slots(nb * nb)
    dk[...] = jnp.zeros(dk.shape, F32)
    dv[...] = jnp.zeros(dv.shape, F32)
    bias_sum[...] = jnp.zeros(bias_sum.shape, F32)
    gain_sum[...] = jnp.zeros(gain_sum.shape, F32)

    def backward(r, carry):
        i = nb - 1 - r
        rows = at(i, group)
        for k in range(1, nb):
            arrive(stats.at[blk_from(k), i], s_st + i * nb + k)
        every = [stats[q, i] for q in range(nb)]
        mean = sum(s[0:1] for s in every) * (1.0 / nb)
        square = sum(s[1:2] + part * (s[0:1] - mean) * (s[0:1] - mean) for s in every)
        inverse = lax.rsqrt(square * (1.0 / D) + norm_eps)
        mean_g = sum(s[2:3] for s in every) * (1.0 / D)
        cross = inverse * sum(s[3:4] + (s[0:1] - mean) * s[2:3] for s in every) * (1.0 / D)
        padded[0:1, :] = mean
        padded[1:2, :] = inverse
        padded[2:3, :] = mean_g
        padded[3:4, :] = cross
        turned = jnp.transpose(padded[...])
        inverse = turned[:, 1:2]
        hat = (attended[rows, :] - turned[:, 0:1]) * inverse
        normal = hat * gain_two + shift_two
        gated_send[i] = (normal * gate[rows, :]).astype(BF16)
        gg = grad_gated[rows, :]
        grad_u = gg * normal
        grad_norm = gg * gate[rows, :]
        gain_sum[2:3, :] += jnp.sum(grad_norm * hat, axis=0, keepdims=True)
        gain_sum[3:4, :] += jnp.sum(grad_norm, axis=0, keepdims=True)
        ga = (grad_norm * gain_two - turned[:, 2:3] - hat * turned[:, 3:4]) * inverse
        for h in range(2):
            grad_att[h] = jnp.where(masks[h], ga, 0.0).astype(BF16)
        dq[...] = jnp.zeros(dq.shape, F32)

        def tile(j, masked):
            cols = at(j, group)
            for h in range(2):
                x = mm(key[h, cols, :], query[h, rows, :], NT)
                t = jnp.tanh(x)
                u = 1.0 + t
                w = x * u
                slope = u * (1.0 + x * (1.0 - t))
                if masked:
                    allowed = iota(w.shape, 0) <= iota(w.shape, 1)
                    w = jnp.where(allowed, w, 0.0)
                    slope = jnp.where(allowed, slope, 0.0)
                dw = mm(value[cols, :], grad_att[h], NT)
                graw = (dw * slope).astype(BF16)
                dv[j] += mm(w.astype(BF16), grad_att[h])
                back = mm(graw, query[h, rows, :])
                dk[j] += back[:, 0:LANES]
                bias_sum[h : h + 1, :] += jnp.sum(back[:, LANES:], axis=0, keepdims=True)
                dq[h] += mm(graw, key[h, cols, :], TN)

        def full(j, inner):
            tile(j, False)
            return inner

        lax.fori_loop(0, i, full, 0)
        tile(i, True)
        for h in range(2):
            bias_sum[2 + h : 3 + h, :] += jnp.sum(dq[h, :, LANES:], axis=0, keepdims=True)
        grad_q = jnp.where(low, dq[0, :, 0:LANES], dq[1, :, 0:LANES]) * (
            0.5 * inv_length * HEAD**-0.5
        )
        raw = projected[rows, :]
        logistic = 0.5 + 0.5 * jnp.tanh(0.5 * raw)
        slope = logistic * (1.0 + raw * (1.0 - logistic))
        acts = jnp.concatenate([grad_u, dv[i] * inv_length, grad_q, dk[i] * inv_length], axis=1)
        pre = (acts * slope).astype(BF16)
        grad_pre[rows, :] = pre
        partial = mm(pre, weight[...].reshape(D, 4 * part), NT)
        scaled = partial * gain_one
        first = jnp.sum(scaled, axis=1, keepdims=True)
        mean_one, inverse_one = fix[rows, 0:1], fix[rows, 1:2]
        hat_one = (embedded[rows, :].astype(F32) - mean_one) * inverse_one
        second = jnp.sum(scaled * hat_one, axis=1, keepdims=True)
        stats_one[b, i] = jnp.transpose(jnp.where(lane == 0, first, second))[0:8]
        for q in range(nb):
            part_send[q, i] = partial[:, q * part : (q + 1) * part].astype(BF16)
        for k in range(1, nb):
            to = blk_peer(k)
            copy(part_send.at[to[0], i], part_got.at[b, i], s_ps + i * nb + k, to).start()
            copy(stats_one.at[b, i], stats_one.at[b, i], s_s1 + i * nb + k, to).start()
        part_got[b, i] = part_send[b, i]
        return carry

    lax.fori_loop(0, nb, backward, 0)

    s_gt = slots(nb)
    for k in range(1, nb):
        to = blk_peer(k)
        push(gated_send.at[to[0]], gated_got.at[b], s_gt + k, to)
    gated_got[b] = gated_send[b]

    def core_stage(total, landing, base):
        for k in range(nz):
            push(total.at[:, k * 2 + other], landing.at[k], base + k, core_peer)

    def core_sum(total, landing, outgoing, base):
        for k in range(nz):
            arrive(landing.at[k], base + k)
            outgoing[k] = (total[:, k * 2 + core].astype(F32) + landing[k].astype(F32)).astype(BF16)

    def z_stage(outgoing, landing, base):
        for k in range(1, nz):
            push(outgoing.at[z_to(k)], landing.at[k], base + k, z_peer(k))

    def z_sum(outgoing, landing, base):
        total = outgoing[z].astype(F32)
        for k in range(1, nz):
            arrive(landing.at[k], base + k)
            total = total + landing[k].astype(F32)
        return total

    s_gic, s_giz, s_gix = slots(nz), slots(nz), slots(nb)
    s_goc, s_goz = slots(nz), slots(nz)

    gated_all = gated_send[...].reshape(length, part)
    go_sum[...] = mm(gated_all, cot[...].reshape(length, D), TN).astype(BF16).reshape(go_sum.shape)
    core_stage(go_sum, go_core, s_goc)

    def weight_grad(t, carry):
        cols = at(t, LANES)
        got = mm(normed[:, cols], grad_pre[...], TN).astype(BF16)
        gi_sum[t] = got.reshape(gi_sum.shape[1:])
        return carry

    lax.fori_loop(0, nb, weight_grad, 0)
    core_stage(gi_sum, gi_core, s_gic)

    s_ig = slots(nb)

    def input_part(r, carry):
        i = nb - 1 - r
        rows = at(i, group)
        for k in range(1, nb):
            arrive(part_got.at[blk_from(k), i], s_ps + i * nb + k)
            arrive(stats_one.at[blk_from(k), i], s_s1 + i * nb + k)
        total = sum(part_got[q, i].astype(F32) for q in range(nb))
        row = sum(stats_one[q, i] for q in range(nb)) * (1.0 / D)
        padded[0:8, :] = row
        turned = jnp.transpose(padded[...])
        mean_one, inverse_one = fix[rows, 0:1], fix[rows, 1:2]
        mycols = at(b, part)
        hat_one = (embedded[rows, mycols].astype(F32) - mean_one) * inverse_one
        gain_sum[0:1, :] += jnp.sum(total * hat_one, axis=0, keepdims=True)
        gain_sum[1:2, :] += jnp.sum(total, axis=0, keepdims=True)
        back = (total * gain_one_own - turned[:, 0:1] - hat_one * turned[:, 1:2]) * inverse_one
        ig_send[i] = (cot[i, :, mycols].astype(F32) + back).astype(BF16)
        return carry

    lax.fori_loop(0, nb, input_part, 0)
    for k in range(1, nb):
        to = blk_peer(k)
        push(ig_send.at[to[0]], ig_got.at[b], s_ig + k, to)
    ig_got[b] = ig_send[b]

    s_tgc, s_tgz, s_tgx = slots(nz), slots(nz), slots(nb)

    def table_part(t, carry):
        picked = jnp.concatenate([index[e][0:1] for e in range(nb)], axis=1)
        hot = jnp.where(iota((step, length), 0) + t * step == picked, 1.0, 0.0).astype(BF16)
        got = mm(hot, ig_send[...].reshape(length, part)).astype(BF16)
        table_sum[t // (items // nb // step), at(t % (items // nb // step), step // rows_table)] = (
            got.reshape(step // rows_table, rows_table, part)
        )
        return carry

    lax.fori_loop(0, items // step, table_part, 0)
    core_stage(table_sum, table_core, s_tgc)

    s_lc, s_lz = slots(1), slots(nz)
    own_items = items // nb

    def count(t, carry):
        picked = column[at(t, step), 0:1]
        hit = jnp.where(iota((step, own_items), 1) + b * own_items == picked, 1.0, 0.0)
        return carry + jnp.sum(hit, axis=0, keepdims=True)

    counted = lax.fori_loop(0, length // step, count, jnp.zeros((1, own_items), F32))
    time_grad = jnp.where(low, bias_sum[0:1, :], pltpu.roll(bias_sum[1:2, :], NB, 1))
    pos_grad = jnp.where(low, pltpu.roll(bias_sum[2:3, :], NB, 1), bias_sum[3:4, :])
    halved = 0.5 * inv_length
    little[...] = jnp.zeros(little.shape, F32)
    little[0:4, :] = gain_sum[0:4, :]
    little[4:5, :] = pos_grad * halved
    little[5:6, :] = time_grad * halved
    for q in range(own_items // LANES):
        little[8 + q : 9 + q, :] = counted[:, q * LANES : (q + 1) * LANES]
    push(little, little_core, s_lc, core_peer)

    core_sum(go_sum, go_core, go_z, s_goc)
    z_stage(go_z, go_zgot, s_goz)
    core_sum(gi_sum, gi_core, gi_z, s_gic)
    z_stage(gi_z, gi_zgot, s_giz)
    arrive(little_core, s_lc)
    little_z[...] = little[...] + little_core[...]
    for k in range(1, nz):
        push(little_z, little_zgot.at[k], s_lz + k, z_peer(k))
    core_sum(table_sum, table_core, table_z, s_tgc)
    z_stage(table_z, table_zgot, s_tgz)

    for k in range(1, nb):
        arrive(gated_got.at[blk_from(k)], s_gt + k)
    result = embedded[at(b, group), :].astype(F32)
    for q in range(nb):
        result = result + mm(gated_got[q], outw[q].reshape(part, D))
    layer_out[...] = result.astype(BF16)

    gi_own[...] = z_sum(gi_z, gi_zgot, s_giz)
    for k in range(1, nb):
        to = blk_peer(k)
        push(gi_own.at[to[0]], gi_got.at[b], s_gix + k, to)
    gi_got[b] = gi_own[b]
    table_own[...] = z_sum(table_z, table_zgot, s_tgz)
    for k in range(1, nb):
        to = blk_peer(k)
        push(table_own.at[to[0]], table_got.at[b], s_tgx + k, to)
    table_got[b] = table_own[b]

    grad_out = z_sum(go_z, go_zgot, s_goz)[0]
    new_m_out[...], new_s_out[...], new_w_out[...] = adam_update(
        proj_out[...], grad_out, moment_out[...], second_out[...], rate_out
    )
    totals = little_z[...]
    for k in range(1, nz):
        arrive(little_zgot.at[k], s_lz + k)
        totals = totals + little_zgot[k]
    little_all[...] = totals
    shifted = pltpu.roll(little_all[0:8, :], lax.rem(LANES - d * width, LANES), 1)[0:6, 0:width]
    new_m_small[...], new_s_small[...], new_w_small[...] = adam_update(
        small_in[...], shifted, moment_small[...], second_small[...], rate_small
    )
    per_row = LANES // rows_table
    count_row = little_all[pl.ds(8 + d // per_row, 1), :]
    count_row = pltpu.roll(
        jnp.broadcast_to(count_row, (8, LANES)),
        lax.rem(LANES - lax.rem(d, per_row) * rows_table, LANES), 1,
    )[0:1, 0:rows_table]
    counts_out[...] = count_row
    logq_out[...] = jnp.log(jnp.maximum(count_row, 1.0) * (1.0 / tokens))

    for k in range(1, nb):
        arrive(gi_got.at[blk_from(k)], s_gix + k)
    grad_in = jnp.concatenate(
        [gi_got[q][:, s * part : (s + 1) * part] for s in range(4) for q in range(nb)], axis=1
    )
    new_m_in[...], new_s_in[...], new_w_in[...] = adam_update(
        proj_in[...], grad_in, moment_in[...], second_in[...], rate_in
    )
    for k in range(1, nb):
        arrive(ig_got.at[blk_from(k)], s_ig + k)
    for q in range(nb):
        input_grad[:, q * part : (q + 1) * part] = ig_got[q].astype(F32)
    for k in range(1, nb):
        arrive(table_got.at[blk_from(k)], s_tgx + k)
    for q in range(nb):
        table_grad[:, q * part : (q + 1) * part] = table_got[q]

    for args in pending:
        copy(*args).wait_send()

    def drain(i, carry):
        for k in range(1, nb):
            to = blk_peer(k)
            copy(stats.at[b, i], stats.at[b, i], s_st + i * nb + k, to).wait_send()
            copy(part_send.at[to[0], i], part_got.at[b, i], s_ps + i * nb + k, to).wait_send()
            copy(stats_one.at[b, i], stats_one.at[b, i], s_s1 + i * nb + k, to).wait_send()
        return carry

    lax.fori_loop(0, nb, drain, 0)
    assert counter[0] <= send.shape[0], counter[0]


def fused(sizes, args):
    nb, nz, group, items, weight_rows, tokens = sizes
    nd = nz * 2
    length = nb * group
    part = D // nb
    rows_table = items // (nb * nd)
    (
        item_ids, pos_buckets, time_buckets, item_table, proj_in, proj_out, small_params, out_grad,
        moment_in, second_in, moment_out, second_out, moment_small, second_small,
    ) = args
    width = small_params.shape[1]
    shape = jax.ShapeDtypeStruct
    outs = [
        shape((group, D), BF16), shape((group, D), F32), shape((rows_table, D), F32),
        shape((1, rows_table), F32), shape((1, rows_table), F32),
        *[shape(proj_in.shape, F32)] * 3, *[shape(proj_out.shape, F32)] * 3,
        *[shape(small_params.shape, F32)] * 3,
    ]
    vm = pltpu.VMEM
    scratch = [
        pltpu.SemaphoreType.DMA((192,)), pltpu.SemaphoreType.DMA((192,)), pltpu.SemaphoreType.DMA((2,)),
        vm((nb, 8, group), I32),
        vm((length, LANES), I32),
        vm((LANES, group), F32),
        vm((nd, nb, rows_table, D), BF16),
        vm((nb, nd, weight_rows, 4 * part), BF16),
        vm((nb, weight_rows, 4 * part), BF16),
        vm((nb, nd, weight_rows, D), BF16),
        vm((nb, nd, 16, LANES), BF16),
        vm((nb, 16, LANES), F32),
        vm((nb, group, D), BF16),
        vm((length, D), BF16),
        vm((length, D), BF16),
        vm((length, 4 * part), F32),
        vm((length, part), F32),
        vm((length, part), BF16),
        vm((2, length, 2 * LANES), BF16),
        vm((2, length, 2 * LANES), BF16),
        vm((length, part), F32),
        vm((length, part), F32),
        vm((nb, nb, 8, group), F32),
        vm((length, LANES), F32),
        vm((nb, group, part), BF16),
        vm((nb, group, part), BF16),
        vm((2, group, part), BF16),
        vm((2, group, 2 * LANES), F32),
        vm((nb, group, part), F32),
        vm((nb, group, part), F32),
        vm((length, 4 * part), BF16),
        vm((nb, nb, group, part), BF16),
        vm((nb, nb, group, part), BF16),
        vm((nb, nb, 8, group), F32),
        vm((nb, group, part), BF16),
        vm((nb, group, part), BF16),
        vm((8, LANES), F32),
        vm((8, LANES), F32),
        vm((nb, nd, rows_table, part), BF16),
        vm((nz, nb, rows_table, part), BF16),
        vm((nz, nb, rows_table, part), BF16),
        vm((nz, nb, rows_table, part), BF16),
        vm((nb, rows_table, part), F32),
        vm((nb, rows_table, part), F32),
        vm((nb, nd, weight_rows, 4 * part), BF16),
        vm((nz, nb, weight_rows, 4 * part), BF16),
        vm((nz, nb, weight_rows, 4 * part), BF16),
        vm((nz, nb, weight_rows, 4 * part), BF16),
        vm((nb, weight_rows, 4 * part), F32),
        vm((nb, weight_rows, 4 * part), F32),
        vm((1, nd, weight_rows, D), BF16),
        vm((nz, 1, weight_rows, D), BF16),
        vm((nz, 1, weight_rows, D), BF16),
        vm((nz, 1, weight_rows, D), BF16),
        vm((16, LANES), F32), vm((16, LANES), F32), vm((16, LANES), F32), vm((nz, 16, LANES), F32),
        vm((16, LANES), F32),
    ]
    whole, far = pl.BlockSpec(memory_space=pltpu.VMEM), pl.BlockSpec(memory_space=pl.ANY)
    got = pl.pallas_call(
        functools.partial(fused_kernel, sizes),
        out_shape=outs,
        in_specs=[whole] * 3 + [far] + [whole] * 3 + [far] + [whole] * 6,
        out_specs=[whole] * len(outs),
        scratch_shapes=scratch,
        compiler_params=pltpu.CompilerParams(
            collective_id=0, has_side_effects=True, vmem_limit_bytes=60 * 2**20
        ),
        name="hstu_step",
    )(
        item_ids, pos_buckets, time_buckets,
        item_table.reshape(nb, item_table.shape[0] // nb, D),
        proj_in, proj_out, small_params, out_grad.reshape(group, D),
        moment_in, second_in, moment_out, second_out, moment_small, second_small,
    )
    return (
        got[0].reshape(out_grad.shape), got[1].reshape(out_grad.shape), got[2],
        got[3].reshape(rows_table), got[4].reshape(rows_table), *got[5:],
    )


def per_device(*args):
    item_ids, item_table, proj_in, small_params = args[0], args[3], args[4], args[6]
    seq_count, group = item_ids.shape
    nb, nd = lax.axis_size("blk"), lax.axis_size("dp")
    items = item_table.shape[0] * nd
    by_heads = (
        seq_count == 1 and nd % 2 == 0 and D // nb == LANES and group % 256 == 0
        and items <= 2048 and items // (nb * nd) % 16 == 0 and proj_in.shape[0] % 16 == 0
        and small_params.shape[1] * nd == LANES
    )
    if by_heads:
        sizes = (nb, nd // 2, group, items, proj_in.shape[0], nd * nb * group)
        return fused(sizes, args)
    return by_events(*args)


def solution(mesh):
    placed = (
        P("dp", "blk"),
        P("dp", "blk"),
        P("dp", "blk"),
        P("dp", None),
        P(("blk", "dp"), None),
        P(("blk", "dp"), None),
        P(None, ("blk", "dp")),
        P("dp", "blk", None),
        P(("blk", "dp"), None),
        P(("blk", "dp"), None),
        P(("blk", "dp"), None),
        P(("blk", "dp"), None),
        P(None, ("blk", "dp")),
        P(None, ("blk", "dp")),
    )
    return jax.shard_map(
        per_device,
        mesh=mesh,
        in_specs=placed,
        out_specs=(
            P("dp", "blk", None),
            P("dp", "blk", None),
            P(("blk", "dp"), None),
            P(("blk", "dp")),
            P(("blk", "dp")),
            P(("blk", "dp"), None),
            P(("blk", "dp"), None),
            P(("blk", "dp"), None),
            P(("blk", "dp"), None),
            P(("blk", "dp"), None),
            P(("blk", "dp"), None),
            P(None, ("blk", "dp")),
            P(None, ("blk", "dp")),
            P(None, ("blk", "dp")),
        ),
        check_vma=False,
    )
```

```python
import functools
import math

import jax
import jax.numpy as jnp
from jax import lax
from jax.experimental import pallas as pl
from jax.experimental.pallas import tpu as pltpu
from jax.sharding import PartitionSpec as P

D = 512
H = 8
HEAD = 64
NB = 64


norm_eps = 1e-05
beta_first = 0.5
beta_second = 0.5
adam_eps = 1e-08
weight_decay = 0.01
rate_in = 0.05
rate_out = 0.06
rate_small = 0.3
step_number = 3


def standardize(values):
    centered = values - jnp.mean(values, axis=-1, keepdims=True)
    inverse = lax.rsqrt(jnp.mean(centered * centered, axis=-1, keepdims=True) + norm_eps)
    return (centered * inverse, inverse)


def norm_back(grad_hat, normal_hat, inverse):
    mean_grad = jnp.mean(grad_hat, axis=-1, keepdims=True)
    mean_cross = jnp.mean(grad_hat * normal_hat, axis=-1, keepdims=True)
    return (grad_hat - mean_grad - normal_hat * mean_cross) * inverse


def silu_slope(values):
    logistic = jax.nn.sigmoid(values)
    return logistic * (1.0 + values * (1.0 - logistic))


def adam_update(weight, grad, moment, second, rate):
    new_moment = beta_first * moment + (1.0 - beta_first) * grad
    new_second = beta_second * second + (1.0 - beta_second) * grad * grad
    moment_hat = new_moment / (1.0 - beta_first**step_number)
    second_hat = new_second / (1.0 - beta_second**step_number)
    new_weight = weight - rate * (
        moment_hat / (jnp.sqrt(second_hat) + adam_eps) + weight_decay * weight
    )
    return (new_moment, new_second, new_weight)


def by_events(
    item_ids,
    pos_buckets,
    time_buckets,
    item_table,
    proj_in,
    proj_out,
    small_params,
    out_grad,
    moment_in,
    second_in,
    moment_out,
    second_out,
    moment_small,
    second_small,
):
    seq_count, group = item_ids.shape
    length = group * lax.axis_size("blk")
    devices = lax.axis_size("blk") * lax.axis_size("dp")
    items = item_table.shape[0] * lax.axis_size("dp")
    tokens = seq_count * group
    scale = HEAD ** (-0.5)
    copy_in, copy_out, copy_small = (
        lax.all_gather(proj_in.astype(jnp.bfloat16), ("blk", "dp"), axis=0, tiled=True),
        lax.all_gather(proj_out.astype(jnp.bfloat16), ("blk", "dp"), axis=0, tiled=True),
        lax.all_gather(small_params.astype(jnp.bfloat16), ("blk", "dp"), axis=1, tiled=True),
    )
    small_float = copy_small.astype(jnp.float32)
    flat_ids = item_ids.reshape(tokens)
    portion = lax.all_gather(item_table, "dp", axis=0, tiled=True)
    hot = (flat_ids[:, None] == jnp.arange(portion.shape[0], dtype=jnp.int32)[None, :]).astype(
        jnp.bfloat16
    )
    embedded = jnp.dot(hot, portion, preferred_element_type=jnp.float32)
    hat_one, inverse_one = standardize(embedded)
    normed = (hat_one * small_float[0] + small_float[1]).astype(jnp.bfloat16)
    projected = jnp.dot(normed, copy_in, preferred_element_type=jnp.float32)
    activated = jax.nn.silu(projected)
    gate_u = activated[:, :D]
    rounded = activated[:, D:].astype(jnp.bfloat16)
    values = rounded[:, :D].reshape(seq_count, group, H, HEAD)
    queries = rounded[:, D : 2 * D].reshape(seq_count, group, H, HEAD)
    keys_own = rounded[:, 2 * D :].reshape(seq_count, group, H, HEAD)
    pos_table = small_float[4].reshape(H, NB)
    time_table = small_float[5].reshape(H, NB)
    buckets = jnp.arange(NB, dtype=jnp.int32)
    time_hot = (time_buckets[:, :, None] == buckets).astype(jnp.float32)
    query_bias = jnp.einsum("scb,hb->shc", time_hot, time_table)
    query_first = lax.axis_index("blk") * group
    query_pos = query_first + jnp.arange(group, dtype=jnp.int32)
    query_last = query_first + group - 1
    pos_sent = pos_buckets.astype(jnp.bfloat16)

    def tile_scores(key_blk, bucket_blk, key_start):
        pos_hot = (bucket_blk.astype(jnp.int32)[:, :, None] == buckets).astype(jnp.float32)
        key_bias = jnp.einsum("sjb,hb->shj", pos_hot, pos_table)
        raw_scores = (
            jnp.einsum("sihd,sjhd->shij", queries, key_blk, preferred_element_type=jnp.float32)
            * scale
        )
        raw_scores = raw_scores + query_bias[:, :, :, None] + key_bias[:, :, None, :]
        key_pos = key_start + jnp.arange(key_blk.shape[1], dtype=jnp.int32)
        allowed = (query_pos[:, None] >= key_pos[None, :])[None, None]
        return (raw_scores, allowed, pos_hot)

    attend_init = jnp.zeros((seq_count, group, H, HEAD), jnp.float32)
    running = attend_init
    key_part = lax.all_gather(keys_own, "blk", axis=1, tiled=True)
    value_part = lax.all_gather(values, "blk", axis=1, tiled=True)
    bucket_part = lax.all_gather(pos_sent, "blk", axis=1, tiled=True)
    span = key_part.shape[1]
    rows_blk = math.gcd(span, 512)

    def fold_step(carried, block_idx):
        key_start = block_idx * rows_blk
        key_blk = lax.dynamic_slice_in_dim(key_part, key_start, rows_blk, 1)
        value_blk = lax.dynamic_slice_in_dim(value_part, key_start, rows_blk, 1)
        bucket_blk = lax.dynamic_slice_in_dim(bucket_part, key_start, rows_blk, 1)

        def fold_compute(current):
            raw_scores, allowed, pos_hot = tile_scores(key_blk, bucket_blk, key_start)
            weights = jnp.where(allowed, jax.nn.silu(raw_scores) / length, 0.0).astype(jnp.bfloat16)
            return current + jnp.einsum(
                "shij,sjhd->sihd", weights, value_blk, preferred_element_type=jnp.float32
            )

        return (
            lax.cond(key_start <= query_last, fold_compute, lambda current: current, carried),
            None,
        )

    running, _ = lax.scan(fold_step, running, jnp.arange(span // rows_blk, dtype=jnp.int32))
    attended = running
    attended = attended.reshape(tokens, D)
    hat_two, inverse_two = standardize(attended)
    normed_two = hat_two * small_float[2] + small_float[3]
    gated = (normed_two * gate_u).astype(jnp.bfloat16)
    result = embedded + jnp.dot(gated, copy_out, preferred_element_type=jnp.float32)
    layer_out = result.astype(jnp.bfloat16).reshape(seq_count, group, D)
    cotangent = out_grad.reshape(tokens, D)
    grad_out_weight = jnp.einsum("td,te->de", gated, cotangent, preferred_element_type=jnp.float32)
    grad_gated = jnp.einsum("te,de->td", cotangent, copy_out, preferred_element_type=jnp.float32)
    grad_u = grad_gated * normed_two
    grad_norm_two = grad_gated * gate_u
    grad_gain_two = jnp.sum(grad_norm_two * hat_two, axis=0)
    grad_shift_two = jnp.sum(grad_norm_two, axis=0)
    grad_attended = norm_back(grad_norm_two * small_float[2], hat_two, inverse_two).astype(
        jnp.bfloat16
    )
    grad_attended = grad_attended.reshape(seq_count, group, H, HEAD)
    key_whole, value_whole, bucket_whole = (
        lax.all_gather(keys_own, "blk", axis=1, tiled=True),
        lax.all_gather(values, "blk", axis=1, tiled=True),
        lax.all_gather(pos_sent, "blk", axis=1, tiled=True),
    )
    rows_back = math.gcd(length, 512)

    def back_step(carried, block_idx):
        grad_query, grad_pos, grad_qbias = carried
        key_start = block_idx * rows_back
        key_blk = lax.dynamic_slice_in_dim(key_whole, key_start, rows_back, 1)
        value_blk = lax.dynamic_slice_in_dim(value_whole, key_start, rows_back, 1)
        bucket_blk = lax.dynamic_slice_in_dim(bucket_whole, key_start, rows_back, 1)

        def back_compute(operand):
            raw_scores, allowed, pos_hot = tile_scores(key_blk, bucket_blk, key_start)
            grad_weights = jnp.einsum(
                "sihd,sjhd->shij", grad_attended, value_blk, preferred_element_type=jnp.float32
            )
            grad_raw = jnp.where(
                allowed, grad_weights / length * silu_slope(raw_scores), 0.0
            ).astype(jnp.bfloat16)
            grad_raw_float = grad_raw.astype(jnp.float32)
            part_query = (
                jnp.einsum("shij,sjhd->sihd", grad_raw, key_blk, preferred_element_type=jnp.float32)
                * scale
            )
            part_pos = jnp.einsum("shj,sjb->hb", jnp.sum(grad_raw_float, axis=2), pos_hot)
            part_qbias = jnp.sum(grad_raw_float, axis=3)
            weights = jnp.where(allowed, jax.nn.silu(raw_scores) / length, 0.0).astype(jnp.bfloat16)
            part_key = (
                jnp.einsum("shij,sihd->sjhd", grad_raw, queries, preferred_element_type=jnp.float32)
                * scale
            )
            part_value = jnp.einsum(
                "shij,sihd->sjhd", weights, grad_attended, preferred_element_type=jnp.float32
            )
            paired = jnp.concatenate(
                [
                    part_key.reshape(seq_count, rows_back, D),
                    part_value.reshape(seq_count, rows_back, D),
                ],
                axis=-1,
            )
            return (part_query, part_pos, part_qbias, paired)

        def skip_tile(operand):
            empty = (
                jnp.zeros((seq_count, group, H, HEAD), jnp.float32),
                jnp.zeros((H, NB), jnp.float32),
                jnp.zeros((seq_count, H, group), jnp.float32),
            )
            return empty + (jnp.zeros((seq_count, rows_back, 2 * D), jnp.float32),)

        parts = lax.cond(key_start <= query_last, back_compute, skip_tile, 0)
        summed = (grad_query + parts[0], grad_pos + parts[1], grad_qbias + parts[2])
        return (summed, parts[3])

    back_init = (
        jnp.zeros((seq_count, group, H, HEAD), jnp.float32),
        jnp.zeros((H, NB), jnp.float32),
        jnp.zeros((seq_count, H, group), jnp.float32),
    )
    (grad_query, grad_pos_table, grad_qbias), stacked = lax.scan(
        back_step, back_init, jnp.arange(length // rows_back, dtype=jnp.int32)
    )
    kv_terms = stacked.transpose(1, 0, 2, 3).reshape(seq_count, length, 2 * D)
    kv_own = lax.psum_scatter(kv_terms, "blk", scatter_dimension=1, tiled=True)
    grad_key = kv_own[:, :, :D].reshape(tokens, D)
    grad_value = kv_own[:, :, D:].reshape(tokens, D)
    grad_time_table = jnp.einsum("shc,scb->hb", grad_qbias, time_hot)
    grad_acts = jnp.concatenate(
        [grad_u, grad_value, grad_query.reshape(tokens, D), grad_key], axis=-1
    )
    grad_pre = (grad_acts * silu_slope(projected)).astype(jnp.bfloat16)
    grad_in_weight = jnp.einsum("td,tf->df", normed, grad_pre, preferred_element_type=jnp.float32)
    grad_normed = jnp.einsum("tf,df->td", grad_pre, copy_in, preferred_element_type=jnp.float32)
    grad_gain_one = jnp.sum(grad_normed * hat_one, axis=0)
    grad_shift_one = jnp.sum(grad_normed, axis=0)
    grad_embed = cotangent.astype(jnp.float32) + norm_back(
        grad_normed * small_float[0], hat_one, inverse_one
    )
    input_grad = grad_embed.reshape(seq_count, group, D)
    grad_small = jnp.stack(
        [
            grad_gain_one,
            grad_shift_one,
            grad_gain_two,
            grad_shift_two,
            grad_pos_table.reshape(D),
            grad_time_table.reshape(D),
        ]
    )
    counts_local = jnp.sum(
        (flat_ids[:, None] == jnp.arange(items, dtype=jnp.int32)[None, :]).astype(jnp.float32),
        axis=0,
    )
    shard_in, shard_out, shard_small, item_counts = (
        lax.psum_scatter(grad_in_weight, ("blk", "dp"), scatter_dimension=0, tiled=True),
        lax.psum_scatter(grad_out_weight, ("blk", "dp"), scatter_dimension=0, tiled=True),
        lax.psum_scatter(grad_small, ("blk", "dp"), scatter_dimension=1, tiled=True),
        lax.psum_scatter(counts_local, ("blk", "dp"), scatter_dimension=0, tiled=True),
    )
    grad_rounded = grad_embed.astype(jnp.bfloat16)
    hot = (
        flat_ids[:, None]
        == jnp.arange(items // devices * lax.axis_size(("blk", "dp")), dtype=jnp.int32)[None, :]
    ).astype(jnp.bfloat16)
    table_grad = lax.psum_scatter(
        jnp.einsum("tr,td->rd", hot, grad_rounded, preferred_element_type=jnp.float32),
        ("blk", "dp"),
        scatter_dimension=0,
        tiled=True,
    )
    log_q = jnp.log(jnp.maximum(item_counts, 1.0) / (seq_count * lax.axis_size("dp") * length))
    new_moment_in, new_second_in, new_proj_in = adam_update(
        proj_in, shard_in, moment_in, second_in, rate_in
    )
    new_moment_out, new_second_out, new_proj_out = adam_update(
        proj_out, shard_out, moment_out, second_out, rate_out
    )
    new_moment_small, new_second_small, new_small = adam_update(
        small_params, shard_small, moment_small, second_small, rate_small
    )
    return (
        layer_out,
        input_grad,
        table_grad,
        item_counts,
        log_q,
        new_moment_in,
        new_second_in,
        new_proj_in,
        new_moment_out,
        new_second_out,
        new_proj_out,
        new_moment_small,
        new_second_small,
        new_small,
    )


MESH = pl.DeviceIdType.MESH
F32, BF16, I32 = jnp.float32, jnp.bfloat16, jnp.int32
LANES = 128
NN = (((1,), (0,)), ((), ()))
NT = (((1,), (1,)), ((), ()))
TN = (((0,), (0,)), ((), ()))


def mm(lhs, rhs, dims=NN):
    return lax.dot_general(lhs, rhs, dims, preferred_element_type=F32)


def iota(shape, dim):
    return lax.broadcasted_iota(I32, shape, dim)


def at(index, size):
    return pl.ds(pl.multiple_of(index * size, size), size)


def fused_kernel(sizes, *refs):
    nb, nz, group, items, weight_rows, tokens = sizes
    nd = nz * 2
    length = nb * group
    part = D // nb
    rows_table = items // (nb * nd)
    (
        ids_in, pos_in, time_in, table_in, proj_in, proj_out, small_in, out_grad_in,
        layer_out, input_out, table_out, grad_in_out, grad_out_out, little_out,
        send, recv, local,
        index, column, padded, table, weight, weight_send, outw, small_send, small, small_all, cot,
        embedded, normed, projected, gate, value, query, key, attended,
        grad_gated, stats, fix, gated_send, gated_got, grad_att, dq, dk, dv,
        grad_pre, part_send, part_got, stats_one, ig_send, ig_got, bias_sum, gain_sum,
        table_sum, table_core, table_z, table_zgot, table_own, table_got,
        gi_sum, gi_core, gi_z, gi_zgot, gi_own, gi_got,
        go_sum, go_core, go_z, go_zgot, little, little_core, little_z, little_zgot,
    ) = refs
    b = lax.axis_index("blk")
    d = lax.axis_index("dp")
    z, core = d // 2, d % 2
    other = 1 - core

    counter = [0]

    def slots(count):
        base = counter[0]
        counter[0] += count
        return base

    def copy(src, dst, slot, target, landing=None):
        return pltpu.make_async_remote_copy(
            src_ref=src, dst_ref=dst, send_sem=send.at[slot],
            recv_sem=recv.at[slot if landing is None else landing],
            device_id={"blk": target[0], "dp": target[1]}, device_id_type=MESH,
        )

    def blk_peer(k):
        return (lax.rem(b + k, nb), d)

    def blk_from(k):
        return lax.rem(b + nb - k, nb)

    def z_to(k):
        return lax.rem(z + k, nz)

    def z_from(k):
        return lax.rem(z + nz - k, nz)

    def z_peer(k):
        return (b, z_to(k) * 2 + core)

    core_peer = (b, z * 2 + other)

    pending = []

    def push(src, dst, slot, target, landing=None, where=None):
        def start():
            copy(src, dst, slot, target, landing).start()

        if where is None:
            start()
        else:
            pl.when(where)(start)
        pending.append((where, src, dst, slot, target))

    near = (z + 1 - 2 * (z % 2), 2 - z // 2, 3 * (1 - z // 2))

    def chain_start(ref, base):
        for n, (beside, there) in enumerate(((z - 1, z > 0), (z + 1, z < nz - 1))):
            to = jnp.clip(beside, 0, nz - 1)
            push(ref, ref, base + n, (b, to * 2 + core), base + z, there)

    def chain_next(ref, base, n):
        arrive(ref, base + near[n])
        beyond = jnp.where(near[n] < z, z + 1, z - 1)
        there = jnp.logical_and(beyond >= 0, beyond < nz)
        to = jnp.clip(beyond, 0, nz - 1)
        push(ref, ref, base + 2 + n, (b, to * 2 + core), base + near[n], there)

    def arrive(dst, slot):
        copy(dst, dst, slot, core_peer).wait_recv()

    table_load = pltpu.make_async_copy(table_in, table.at[d], local.at[0])
    table_load.start()
    cot_load = pltpu.make_async_copy(out_grad_in, cot.at[b], local.at[1])
    cot_load.start()

    index[b] = jnp.concatenate(
        [ids_in[...], pos_in[...], time_in[...], jnp.zeros((5, group), I32)], axis=0
    )
    own_rows = proj_in[...].astype(BF16)
    for q in range(nb):
        weight_send[q] = jnp.concatenate(
            [own_rows[:, s * D + q * part : s * D + (q + 1) * part] for s in range(4)], axis=1
        )
    weight[b, d] = weight_send[b]
    outw[b, d] = proj_out[...].astype(BF16)
    width = small_in.shape[1]
    spread = (iota((width, LANES), 1) == iota((width, LANES), 0) + b * width).astype(F32)
    small_pad = jnp.concatenate([small_in[...], jnp.zeros((10, width), F32)], axis=0)
    small_send[b] = mm(small_pad.astype(BF16), spread.astype(BF16)).astype(BF16)

    barrier = pltpu.get_barrier_semaphore()
    peers = [blk_peer(k) for k in range(1, nb)] + [z_peer(k) for k in range(1, nz)] + [core_peer]
    for target in peers:
        pl.semaphore_signal(
            barrier, inc=1, device_id={"blk": target[0], "dp": target[1]}, device_id_type=MESH
        )
    pl.semaphore_wait(barrier, len(peers))

    s_index, s_w, s_s = slots(nb), slots(nb), slots(nb)
    for k in range(1, nb):
        to = blk_peer(k)
        push(index.at[b], index.at[b], s_index + k, to)
        push(weight_send.at[to[0]], weight.at[b, d], s_w + k, to)
        push(small_send.at[b], small_send.at[b], s_s + k, to)
    table_load.wait()
    s_tz, s_tx, s_tc = slots(nz + 2), slots(nz * nb), slots(nz * nb)
    chain_start(table.at[d, b], s_tz)
    push(table.at[d], table.at[d], s_tc, core_peer, s_tc + z * nb)
    cot_load.wait()
    s_g = slots(6)
    x_peer, y_peer = (b // 2 * 2 + 1 - b % 2, d), (lax.rem(b + 2, nb), d)
    halves = (slice(0, group // 2), slice(group // 2, group))
    sides = (x_peer, y_peer)

    def cot_half(owner, n):
        return cot.at[owner, halves[n]]

    def own_half(n):
        for m in range(2):
            push(cot_half(b, n), cot_half(b, n), s_g + 2 * n + m, sides[m])

    s_wz, s_wc = slots(3 * (nz + 2)), slots(3 * nz)

    def shard_of(n, slot):
        return (weight.at[:, slot], small.at[slot], outw.at[b, slot])[n]

    def shard_start(n):
        for k in range(1, nz):
            push(shard_of(n, d), shard_of(n, d), s_wz + n * (nz + 2) + k, z_peer(k), s_wz + n * (nz + 2) + z)
        push(shard_of(n, d), shard_of(n, d), s_wc + n * nz, core_peer, s_wc + n * nz + z)

    def shard_next(n, m):
        ref = shard_of(n, near[m] * 2 + core)
        arrive(ref, s_wz + n * (nz + 2) + near[m])
        push(ref, ref, s_wc + n * nz + 1 + m, core_peer, s_wc + n * nz + near[m])

    for k in range(1, nb):
        arrive(weight.at[blk_from(k), d], s_w + k)
    shard_start(0)
    for k in range(1, nb):
        arrive(small_send.at[blk_from(k)], s_s + k)
    small[d] = sum(small_send[q].astype(F32) for q in range(nb)).astype(BF16)
    shard_start(1)

    for k in range(1, nb):
        arrive(index.at[blk_from(k)], s_index + k)
    padded[...] = jnp.zeros(padded.shape, F32)

    def to_column(e, carry):
        padded[0:8, :] = index[e].astype(F32)
        column[at(e, group), :] = jnp.transpose(padded[...]).astype(I32)
        return carry

    lax.fori_loop(0, nb, to_column, 0)

    step = 256

    def table_over_z(n):
        shard = near[n] * 2 + core
        chain_next(table.at[shard, b], s_tz, n)
        for m in range(1, nb):
            push(
                table.at[shard, b], table.at[shard, b], s_tx + n * nb + m, blk_peer(m),
                s_tx + near[n] * nb + m,
            )
        push(
            table.at[shard, b], table.at[shard, b], s_tc + (n + 1) * nb, core_peer,
            s_tc + near[n] * nb,
        )

    def table_over_blk(n):
        shard = near[n] * 2 + core
        for m in range(1, nb):
            quarter = table.at[shard, blk_from(m)]
            arrive(quarter, s_tx + near[n] * nb + m)
            push(quarter, quarter, s_tc + (n + 1) * nb + m, core_peer, s_tc + near[n] * nb + m)

    def table_over_core(n):
        shard = near[n] * 2 + other
        arrive(table.at[shard, b], s_tc + near[n] * nb)
        for m in range(1, nb):
            arrive(table.at[shard, blk_from(m)], s_tc + near[n] * nb + m)

    def picked_rows(rows, at_z):
        picked = column[rows, 0:1] - at_z * (items // nz)
        hot = jnp.where(iota((step, items // nz), 1) == picked, 1.0, 0.0).astype(BF16)
        return mm(hot, table[pl.ds(at_z * 2, 2)].reshape(items // nz, D)).astype(BF16)

    def look_up(at_z, first):
        def body(t, carry):
            rows = at(t, step)
            found = picked_rows(rows, at_z)
            embedded[rows, :] = found if first else embedded[rows, :] + found
            return carry

        lax.fori_loop(0, length // step, body, 0)

    def pass_on(n):
        arrive(cot_half(sides[n][0], n), s_g + 2 * n + n)
        push(cot_half(sides[n][0], n), cot_half(sides[n][0], n), s_g + 4 + n, sides[1 - n])

    table_over_z(0)
    table_over_z(1)
    arrive(table.at[z * 2 + other], s_tc + z * nb)
    look_up(z, True)
    table_over_z(2)
    own_half(0)
    own_half(1)
    for n in range(2):
        for m in range(nz - 1):
            shard_next(n, m)
    table_over_blk(0)
    table_over_blk(1)
    table_over_core(0)
    shard_start(2)
    look_up(near[0], False)
    table_over_blk(2)
    table_over_core(1)
    look_up(near[1], False)
    pass_on(0)
    table_over_core(2)

    def shards_over_core(n):
        for m in (z, *near):
            arrive(shard_of(n, m * 2 + other), s_wc + n * nz + m)

    shards_over_core(0)
    shards_over_core(1)

    lane = iota((1, LANES), 1)
    for q in range(nb):
        total = jnp.zeros((16, LANES), F32)
        for r in range(nd):
            turned = pltpu.roll(small[r].astype(F32), (r - q) * width % LANES, 1)
            total = jnp.where(lane // width == r, turned, total)
        small_all[q] = total
    gain_one = jnp.concatenate([small_all[q][0:1] for q in range(nb)], axis=1)
    shift_one = jnp.concatenate([small_all[q][1:2] for q in range(nb)], axis=1)
    mine = small_all[b]
    gain_one_own = mine[0:1]
    gain_two, shift_two = mine[2:3], mine[3:4]
    pos_row, time_row = mine[4:5], mine[5:6]
    low = lane < NB
    pos_rows = (0.5 * pltpu.roll(pos_row, NB, 1), 0.5 * pos_row)
    time_rows = (0.5 * time_row, 0.5 * pltpu.roll(time_row, NB, 1))
    masks = (low, lane >= NB)

    def embed(t, carry):
        rows = at(t, step)
        found = embedded[rows, :] + picked_rows(rows, near[2])
        embedded[rows, :] = found
        found = found.astype(F32)
        mean = jnp.mean(found, axis=1, keepdims=True)
        centered = found - mean
        inverse = lax.rsqrt(jnp.mean(centered * centered, axis=1, keepdims=True) + norm_eps)
        fix[rows, :] = jnp.where(lane == 0, mean, inverse)
        ready = (centered * inverse * gain_one + shift_one).astype(BF16)
        normed[rows, :] = ready
        raw = mm(ready, weight[...].reshape(D, 4 * part))
        projected[rows, :] = raw
        act = raw * (0.5 + 0.5 * jnp.tanh(0.5 * raw))
        gate[rows, :] = act[:, 0:part]
        value[rows, :] = act[:, part : 2 * part].astype(BF16)
        queries = act[:, 2 * part : 3 * part].astype(BF16).astype(F32) * (0.5 * HEAD**-0.5)
        keys = act[:, 3 * part :].astype(BF16)
        time_hot = jnp.where(lane == column[rows, 2:3], 1.0, 0.0)
        pos_hot = jnp.where(lane == column[rows, 1:2] + NB, 1.0, 0.0)
        for h in range(2):
            query[h, rows, 0:LANES] = jnp.where(masks[h], queries, 0.0).astype(BF16)
            query[h, rows, LANES:] = jnp.where(low, time_hot, pos_rows[h]).astype(BF16)
            key[h, rows, 0:LANES] = keys
            key[h, rows, LANES:] = jnp.where(low, time_rows[h], pos_hot).astype(BF16)
        return carry

    lax.fori_loop(0, length // step // 2, embed, 0)
    pass_on(1)
    for m in range(nz - 1):
        shard_next(2, m)
    lax.fori_loop(length // step // 2, length // step, embed, 0)
    shards_over_core(2)
    out_rows = outw[b].reshape(part, D)

    s_st = slots(nb * nb)
    inv_length = 1.0 / length

    def forward(r, carry):
        i = nb - 1 - r
        rows = at(i, group)
        dq[...] = jnp.zeros(dq.shape, F32)

        def tile(j, masked):
            cols = at(j, group)
            for h in range(2):
                x = mm(query[h, rows, :], key[h, cols, :], NT)
                w = x + x * jnp.tanh(x)
                if masked:
                    w = jnp.where(iota(w.shape, 0) >= iota(w.shape, 1), w, 0.0)
                dq[h, :, 0:LANES] += mm(w.astype(BF16), value[cols, :])

        def full(j, inner):
            tile(j, False)
            return inner

        lax.fori_loop(0, i, full, 0)
        tile(i, True)
        att = jnp.where(low, dq[0, :, 0:LANES], dq[1, :, 0:LANES]) * inv_length
        attended[rows, :] = att

        @pl.when(r == 0)
        def cotangents():
            cross = nb - 1 - b
            for n in range(2):
                arrive(cot_half(sides[n][0], 1 - n), s_g + 2 * (1 - n) + n)
                arrive(cot_half(cross, n), s_g + 4 + n)

        gg = mm(cot[i], out_rows, NT)
        grad_gated[rows, :] = gg
        g = gg * gate[rows, :] * gain_two
        mean = jnp.mean(att, axis=1, keepdims=True)
        centered = att - mean
        square = jnp.sum(centered * centered, axis=1, keepdims=True)
        sum_g = jnp.sum(g, axis=1, keepdims=True)
        sum_ga = jnp.sum(g * centered, axis=1, keepdims=True)
        packed = jnp.where(
            lane == 0, mean, jnp.where(lane == 1, square, jnp.where(lane == 2, sum_g, sum_ga))
        )
        stats[b, i] = jnp.transpose(packed)[0:8]
        for k in range(1, nb):
            copy(stats.at[b, i], stats.at[b, i], s_st + i * nb + k, blk_peer(k)).start()
        return carry

    lax.fori_loop(0, nb, forward, 0)

    s_ox = slots(nb)
    for k in range(1, nb):
        push(outw.at[b], outw.at[b], s_ox + k, blk_peer(k))

    s_ps, s_s1 = slots(nb * nb), slots(nb * nb)
    dk[...] = jnp.zeros(dk.shape, F32)
    dv[...] = jnp.zeros(dv.shape, F32)
    bias_sum[...] = jnp.zeros(bias_sum.shape, F32)
    gain_sum[...] = jnp.zeros(gain_sum.shape, F32)

    def backward(r, carry):
        i = nb - 1 - r
        rows = at(i, group)
        for k in range(1, nb):
            arrive(stats.at[blk_from(k), i], s_st + i * nb + k)
        every = [stats[q, i] for q in range(nb)]
        mean = sum(s[0:1] for s in every) * (1.0 / nb)
        square = sum(s[1:2] + part * (s[0:1] - mean) * (s[0:1] - mean) for s in every)
        inverse = lax.rsqrt(square * (1.0 / D) + norm_eps)
        mean_g = sum(s[2:3] for s in every) * (1.0 / D)
        cross = inverse * sum(s[3:4] + (s[0:1] - mean) * s[2:3] for s in every) * (1.0 / D)
        padded[0:1, :] = mean
        padded[1:2, :] = inverse
        padded[2:3, :] = mean_g
        padded[3:4, :] = cross
        turned = jnp.transpose(padded[...])
        inverse = turned[:, 1:2]
        hat = (attended[rows, :] - turned[:, 0:1]) * inverse
        normal = hat * gain_two + shift_two
        gated_send[i] = (normal * gate[rows, :]).astype(BF16)
        gg = grad_gated[rows, :]
        grad_u = gg * normal
        grad_norm = gg * gate[rows, :]
        gain_sum[2:3, :] += jnp.sum(grad_norm * hat, axis=0, keepdims=True)
        gain_sum[3:4, :] += jnp.sum(grad_norm, axis=0, keepdims=True)
        ga = (grad_norm * gain_two - turned[:, 2:3] - hat * turned[:, 3:4]) * inverse
        for h in range(2):
            grad_att[h] = jnp.where(masks[h], ga, 0.0).astype(BF16)
        dq[...] = jnp.zeros(dq.shape, F32)

        def tile(j, masked):
            cols = at(j, group)
            for h in range(2):
                x = mm(key[h, cols, :], query[h, rows, :], NT)
                t = jnp.tanh(x)
                u = 1.0 + t
                w = x * u
                slope = u * (1.0 + x * (1.0 - t))
                if masked:
                    allowed = iota(w.shape, 0) <= iota(w.shape, 1)
                    w = jnp.where(allowed, w, 0.0)
                    slope = jnp.where(allowed, slope, 0.0)
                dw = mm(value[cols, :], grad_att[h], NT)
                graw = (dw * slope).astype(BF16)
                dv[j] += mm(w.astype(BF16), grad_att[h])
                back = mm(graw, query[h, rows, :])
                dk[j] += back[:, 0:LANES]
                bias_sum[h : h + 1, :] += jnp.sum(back[:, LANES:], axis=0, keepdims=True)
                dq[h] += mm(graw, key[h, cols, :], TN)

        def full(j, inner):
            tile(j, False)
            return inner

        lax.fori_loop(0, i, full, 0)
        tile(i, True)
        for h in range(2):
            bias_sum[2 + h : 3 + h, :] += jnp.sum(dq[h, :, LANES:], axis=0, keepdims=True)
        grad_q = jnp.where(low, dq[0, :, 0:LANES], dq[1, :, 0:LANES]) * (
            0.5 * inv_length * HEAD**-0.5
        )
        raw = projected[rows, :]
        logistic = 0.5 + 0.5 * jnp.tanh(0.5 * raw)
        slope = logistic * (1.0 + raw * (1.0 - logistic))
        acts = jnp.concatenate([grad_u, dv[i] * inv_length, grad_q, dk[i] * inv_length], axis=1)
        pre = (acts * slope).astype(BF16)
        grad_pre[rows, :] = pre
        partial = mm(pre, weight[...].reshape(D, 4 * part), NT)
        scaled = partial * gain_one
        first = jnp.sum(scaled, axis=1, keepdims=True)
        mean_one, inverse_one = fix[rows, 0:1], fix[rows, 1:2]
        hat_one = (embedded[rows, :].astype(F32) - mean_one) * inverse_one
        second = jnp.sum(scaled * hat_one, axis=1, keepdims=True)
        stats_one[b, i] = jnp.transpose(jnp.where(lane == 0, first, second))[0:8]
        for q in range(nb):
            part_send[q, i] = partial[:, q * part : (q + 1) * part].astype(BF16)
        for k in range(1, nb):
            to = blk_peer(k)
            copy(part_send.at[to[0], i], part_got.at[b, i], s_ps + i * nb + k, to).start()
            copy(stats_one.at[b, i], stats_one.at[b, i], s_s1 + i * nb + k, to).start()
        part_got[b, i] = part_send[b, i]
        return carry

    lax.fori_loop(0, nb, backward, 0)

    s_gt = slots(nb)
    for k in range(1, nb):
        to = blk_peer(k)
        push(gated_send.at[to[0]], gated_got.at[b], s_gt + k, to)
    gated_got[b] = gated_send[b]

    def core_stage(total, landing, base):
        for k in range(nz):
            push(total.at[:, k * 2 + other], landing.at[k], base + k, core_peer)

    def core_sum(total, landing, outgoing, base):
        for k in range(nz):
            arrive(landing.at[k], base + k)
            outgoing[k] = (total[:, k * 2 + core].astype(F32) + landing[k].astype(F32)).astype(BF16)

    def z_stage(outgoing, landing, base):
        for k in range(1, nz):
            push(outgoing.at[z_to(k)], landing.at[k], base + k, z_peer(k))

    def z_sum(outgoing, landing, base):
        total = outgoing[z].astype(F32)
        for k in range(1, nz):
            arrive(landing.at[k], base + k)
            total = total + landing[k].astype(F32)
        return total

    s_gic, s_giz, s_gix = slots(nz), slots(nz), slots(nb)
    s_goc, s_goz = slots(nz), slots(nz)

    gated_all = gated_send[...].reshape(length, part)
    go_sum[...] = mm(gated_all, cot[...].reshape(length, D), TN).astype(BF16).reshape(go_sum.shape)
    core_stage(go_sum, go_core, s_goc)

    def weight_grad(t, carry):
        cols = at(t, LANES)
        got = mm(normed[:, cols], grad_pre[...], TN).astype(BF16)
        gi_sum[t] = got.reshape(gi_sum.shape[1:])
        return carry

    lax.fori_loop(0, nb, weight_grad, 0)
    core_stage(gi_sum, gi_core, s_gic)

    s_ig = slots(nb)

    def input_part(r, carry):
        i = nb - 1 - r
        rows = at(i, group)
        for k in range(1, nb):
            arrive(part_got.at[blk_from(k), i], s_ps + i * nb + k)
            arrive(stats_one.at[blk_from(k), i], s_s1 + i * nb + k)
        total = sum(part_got[q, i].astype(F32) for q in range(nb))
        row = sum(stats_one[q, i] for q in range(nb)) * (1.0 / D)
        padded[0:8, :] = row
        turned = jnp.transpose(padded[...])
        mean_one, inverse_one = fix[rows, 0:1], fix[rows, 1:2]
        mycols = at(b, part)
        hat_one = (embedded[rows, mycols].astype(F32) - mean_one) * inverse_one
        gain_sum[0:1, :] += jnp.sum(total * hat_one, axis=0, keepdims=True)
        gain_sum[1:2, :] += jnp.sum(total, axis=0, keepdims=True)
        back = (total * gain_one_own - turned[:, 0:1] - hat_one * turned[:, 1:2]) * inverse_one
        ig_send[i] = (cot[i, :, mycols].astype(F32) + back).astype(BF16)
        return carry

    lax.fori_loop(0, nb, input_part, 0)
    for k in range(1, nb):
        to = blk_peer(k)
        push(ig_send.at[to[0]], ig_got.at[b], s_ig + k, to)
    ig_got[b] = ig_send[b]

    s_tgc, s_tgz, s_tgx = slots(nz), slots(nz), slots(nb)

    def table_part(t, carry):
        picked = jnp.concatenate([index[e][0:1] for e in range(nb)], axis=1)
        hot = jnp.where(iota((step, length), 0) + t * step == picked, 1.0, 0.0).astype(BF16)
        got = mm(hot, ig_send[...].reshape(length, part)).astype(BF16)
        table_sum[t // (items // nb // step), at(t % (items // nb // step), step // rows_table)] = (
            got.reshape(step // rows_table, rows_table, part)
        )
        return carry

    lax.fori_loop(0, items // step, table_part, 0)
    core_stage(table_sum, table_core, s_tgc)

    s_lc, s_lz = slots(1), slots(nz)
    own_items = items // nb

    def count(t, carry):
        picked = column[at(t, step), 0:1]
        hit = jnp.where(iota((step, own_items), 1) + b * own_items == picked, 1.0, 0.0)
        return carry + jnp.sum(hit, axis=0, keepdims=True)

    counted = lax.fori_loop(0, length // step, count, jnp.zeros((1, own_items), F32))
    time_grad = jnp.where(low, bias_sum[0:1, :], pltpu.roll(bias_sum[1:2, :], NB, 1))
    pos_grad = jnp.where(low, pltpu.roll(bias_sum[2:3, :], NB, 1), bias_sum[3:4, :])
    halved = 0.5 * inv_length
    little[...] = jnp.zeros(little.shape, F32)
    little[0:4, :] = gain_sum[0:4, :]
    little[4:5, :] = pos_grad * halved
    little[5:6, :] = time_grad * halved
    for q in range(own_items // LANES):
        little[8 + q : 9 + q, :] = counted[:, q * LANES : (q + 1) * LANES]
    push(little, little_core, s_lc, core_peer)

    core_sum(go_sum, go_core, go_z, s_goc)
    z_stage(go_z, go_zgot, s_goz)
    core_sum(gi_sum, gi_core, gi_z, s_gic)
    z_stage(gi_z, gi_zgot, s_giz)
    arrive(little_core, s_lc)
    little_z[...] = little[...] + little_core[...]
    for k in range(1, nz):
        push(little_z, little_zgot.at[k], s_lz + k, z_peer(k))
    core_sum(table_sum, table_core, table_z, s_tgc)
    z_stage(table_z, table_zgot, s_tgz)

    for k in range(1, nb):
        arrive(gated_got.at[blk_from(k)], s_gt + k)
        arrive(outw.at[blk_from(k)], s_ox + k)
    result = embedded[at(b, group), :].astype(F32)
    for q in range(nb):
        result = result + mm(gated_got[q], outw[q].reshape(part, D))
    layer_out[...] = result.astype(BF16)

    gi_own[...] = z_sum(gi_z, gi_zgot, s_giz)
    for k in range(1, nb):
        to = blk_peer(k)
        push(gi_own.at[to[0]], gi_got.at[b], s_gix + k, to)
    gi_got[b] = gi_own[b]
    table_own[...] = z_sum(table_z, table_zgot, s_tgz)
    for k in range(1, nb):
        to = blk_peer(k)
        push(table_own.at[to[0]], table_got.at[b], s_tgx + k, to)
    table_got[b] = table_own[b]

    grad_out_out[...] = z_sum(go_z, go_zgot, s_goz)[0]
    totals = little_z[...]
    for k in range(1, nz):
        arrive(little_zgot.at[k], s_lz + k)
        totals = totals + little_zgot[k]
    little_out[...] = totals
    for k in range(1, nb):
        arrive(gi_got.at[blk_from(k)], s_gix + k)
    grad_in_out[...] = gi_got[...]
    for k in range(1, nb):
        arrive(ig_got.at[blk_from(k)], s_ig + k)
    input_out[...] = ig_got[...]
    for k in range(1, nb):
        arrive(table_got.at[blk_from(k)], s_tgx + k)
    table_out[...] = table_got[...]

    for where, *sent in pending:
        if where is None:
            copy(*sent).wait_send()
        else:
            pl.when(where)(copy(*sent).wait_send)

    def drain(i, carry):
        for k in range(1, nb):
            to = blk_peer(k)
            copy(stats.at[b, i], stats.at[b, i], s_st + i * nb + k, to).wait_send()
            copy(part_send.at[to[0], i], part_got.at[b, i], s_ps + i * nb + k, to).wait_send()
            copy(stats_one.at[b, i], stats_one.at[b, i], s_s1 + i * nb + k, to).wait_send()
        return carry

    lax.fori_loop(0, nb, drain, 0)
    assert counter[0] <= send.shape[0], counter[0]


def finish_kernel(sizes, *refs):
    nb, nz, group, items, weight_rows, tokens = sizes
    part = D // nb
    rows_table = items // (nb * nz * 2)
    (
        layer_in, input_in, table_in, grad_in_in, grad_out_in, little_in,
        proj_in, proj_out, small_in,
        moment_in, second_in, moment_out, second_out, moment_small, second_small,
        layer_out, input_grad, table_grad, counts_out, logq_out,
        new_m_in, new_s_in, new_w_in, new_m_out, new_s_out, new_w_out,
        new_m_small, new_s_small, new_w_small,
    ) = refs
    d = lax.axis_index("dp")
    layer_out[...] = layer_in[...]
    for q in range(nb):
        cols = slice(q * part, (q + 1) * part)
        input_grad[:, cols] = input_in[q].astype(F32)
        table_grad[:, cols] = table_in[q]
        for s in range(4):
            own = slice(s * D + q * part, s * D + (q + 1) * part)
            new_m_in[:, own], new_s_in[:, own], new_w_in[:, own] = adam_update(
                proj_in[:, own], grad_in_in[q, :, s * part : (s + 1) * part],
                moment_in[:, own], second_in[:, own], rate_in,
            )
    new_m_out[...], new_s_out[...], new_w_out[...] = adam_update(
        proj_out[...], grad_out_in[...], moment_out[...], second_out[...], rate_out
    )
    width = small_in.shape[1]
    shifted = pltpu.roll(little_in[0:8, :], lax.rem(LANES - d * width, LANES), 1)[0:6, 0:width]
    new_m_small[...], new_s_small[...], new_w_small[...] = adam_update(
        small_in[...], shifted, moment_small[...], second_small[...], rate_small
    )
    per_row = LANES // rows_table
    count_row = little_in[pl.ds(8 + d // per_row, 1), :]
    count_row = pltpu.roll(
        jnp.broadcast_to(count_row, (8, LANES)),
        lax.rem(LANES - lax.rem(d, per_row) * rows_table, LANES), 1,
    )[0:1, 0:rows_table]
    counts_out[...] = count_row
    logq_out[...] = jnp.log(jnp.maximum(count_row, 1.0) * (1.0 / tokens))


def fused(sizes, args):
    nb, nz, group, items, weight_rows, tokens = sizes
    nd = nz * 2
    length = nb * group
    part = D // nb
    rows_table = items // (nb * nd)
    (
        item_ids, pos_buckets, time_buckets, item_table, proj_in, proj_out, small_params, out_grad,
        moment_in, second_in, moment_out, second_out, moment_small, second_small,
    ) = args
    width = small_params.shape[1]
    shape = jax.ShapeDtypeStruct
    middle = [
        shape((group, D), BF16), shape((nb, group, part), BF16), shape((nb, rows_table, part), F32),
        shape((nb, weight_rows, 4 * part), F32), shape((weight_rows, D), F32), shape((16, LANES), F32),
    ]
    outs = [
        shape((group, D), BF16), shape((group, D), F32), shape((rows_table, D), F32),
        shape((1, rows_table), F32), shape((1, rows_table), F32),
        *[shape(proj_in.shape, F32)] * 3, *[shape(proj_out.shape, F32)] * 3,
        *[shape(small_params.shape, F32)] * 3,
    ]
    vm = pltpu.VMEM
    scratch = [
        pltpu.SemaphoreType.DMA((192,)), pltpu.SemaphoreType.DMA((192,)), pltpu.SemaphoreType.DMA((2,)),
        vm((nb, 8, group), I32),
        vm((length, LANES), I32),
        vm((LANES, group), F32),
        vm((nd, nb, rows_table, D), BF16),
        vm((nb, nd, weight_rows, 4 * part), BF16),
        vm((nb, weight_rows, 4 * part), BF16),
        vm((nb, nd, weight_rows, D), BF16),
        vm((nb, 16, LANES), BF16),
        vm((nd, 16, LANES), BF16),
        vm((nb, 16, LANES), F32),
        vm((nb, group, D), BF16),
        vm((length, D), BF16),
        vm((length, D), BF16),
        vm((length, 4 * part), F32),
        vm((length, part), F32),
        vm((length, part), BF16),
        vm((2, length, 2 * LANES), BF16),
        vm((2, length, 2 * LANES), BF16),
        vm((length, part), F32),
        vm((length, part), F32),
        vm((nb, nb, 8, group), F32),
        vm((length, LANES), F32),
        vm((nb, group, part), BF16),
        vm((nb, group, part), BF16),
        vm((2, group, part), BF16),
        vm((2, group, 2 * LANES), F32),
        vm((nb, group, part), F32),
        vm((nb, group, part), F32),
        vm((length, 4 * part), BF16),
        vm((nb, nb, group, part), BF16),
        vm((nb, nb, group, part), BF16),
        vm((nb, nb, 8, group), F32),
        vm((nb, group, part), BF16),
        vm((nb, group, part), BF16),
        vm((8, LANES), F32),
        vm((8, LANES), F32),
        vm((nb, nd, rows_table, part), BF16),
        vm((nz, nb, rows_table, part), BF16),
        vm((nz, nb, rows_table, part), BF16),
        vm((nz, nb, rows_table, part), BF16),
        vm((nb, rows_table, part), F32),
        vm((nb, rows_table, part), F32),
        vm((nb, nd, weight_rows, 4 * part), BF16),
        vm((nz, nb, weight_rows, 4 * part), BF16),
        vm((nz, nb, weight_rows, 4 * part), BF16),
        vm((nz, nb, weight_rows, 4 * part), BF16),
        vm((nb, weight_rows, 4 * part), F32),
        vm((nb, weight_rows, 4 * part), F32),
        vm((1, nd, weight_rows, D), BF16),
        vm((nz, 1, weight_rows, D), BF16),
        vm((nz, 1, weight_rows, D), BF16),
        vm((nz, 1, weight_rows, D), BF16),
        vm((16, LANES), F32), vm((16, LANES), F32), vm((16, LANES), F32), vm((nz, 16, LANES), F32),
    ]
    whole, far = pl.BlockSpec(memory_space=pltpu.VMEM), pl.BlockSpec(memory_space=pl.ANY)
    between = pl.pallas_call(
        functools.partial(fused_kernel, sizes),
        out_shape=middle,
        in_specs=[whole] * 3 + [far] + [whole] * 3 + [far],
        out_specs=[whole] * len(middle),
        scratch_shapes=scratch,
        compiler_params=pltpu.CompilerParams(
            collective_id=0, has_side_effects=True, vmem_limit_bytes=60 * 2**20
        ),
        name="hstu_step",
    )(
        item_ids, pos_buckets, time_buckets,
        item_table.reshape(nb, item_table.shape[0] // nb, D),
        proj_in, proj_out, small_params, out_grad.reshape(group, D),
    )
    got = pl.pallas_call(
        functools.partial(finish_kernel, sizes),
        out_shape=outs,
        in_specs=[whole] * (len(middle) + 9),
        out_specs=[whole] * len(outs),
        name="hstu_finish",
    )(
        *between, proj_in, proj_out, small_params,
        moment_in, second_in, moment_out, second_out, moment_small, second_small,
    )
    return (
        got[0].reshape(out_grad.shape), got[1].reshape(out_grad.shape), got[2],
        got[3].reshape(rows_table), got[4].reshape(rows_table), *got[5:],
    )


def per_device(*args):
    item_ids, item_table, proj_in, small_params = args[0], args[3], args[4], args[6]
    seq_count, group = item_ids.shape
    nb, nd = lax.axis_size("blk"), lax.axis_size("dp")
    items = item_table.shape[0] * nd
    by_heads = (
        seq_count == 1 and nd % 2 == 0 and D // nb == LANES and group % 256 == 0
        and items <= 2048 and items // (nb * nd) % 16 == 0 and proj_in.shape[0] % 16 == 0
        and small_params.shape[1] * nd == LANES and nb == 4 and nd == 8
    )
    if by_heads:
        sizes = (nb, nd // 2, group, items, proj_in.shape[0], nd * nb * group)
        return fused(sizes, args)
    return by_events(*args)


def solution(mesh):
    placed = (
        P("dp", "blk"),
        P("dp", "blk"),
        P("dp", "blk"),
        P("dp", None),
        P(("blk", "dp"), None),
        P(("blk", "dp"), None),
        P(None, ("blk", "dp")),
        P("dp", "blk", None),
        P(("blk", "dp"), None),
        P(("blk", "dp"), None),
        P(("blk", "dp"), None),
        P(("blk", "dp"), None),
        P(None, ("blk", "dp")),
        P(None, ("blk", "dp")),
    )
    return jax.shard_map(
        per_device,
        mesh=mesh,
        in_specs=placed,
        out_specs=(
            P("dp", "blk", None),
            P("dp", "blk", None),
            P(("blk", "dp"), None),
            P(("blk", "dp")),
            P(("blk", "dp")),
            P(("blk", "dp"), None),
            P(("blk", "dp"), None),
            P(("blk", "dp"), None),
            P(("blk", "dp"), None),
            P(("blk", "dp"), None),
            P(("blk", "dp"), None),
            P(None, ("blk", "dp")),
            P(None, ("blk", "dp")),
            P(None, ("blk", "dp")),
        ),
        check_vma=False,
    )
```

```python
import functools
import math

import jax
import jax.numpy as jnp
from jax import lax
from jax.experimental import pallas as pl
from jax.experimental.pallas import tpu as pltpu
from jax.sharding import PartitionSpec as P

D = 512
H = 8
HEAD = 64
NB = 64


norm_eps = 1e-05
beta_first = 0.5
beta_second = 0.5
adam_eps = 1e-08
weight_decay = 0.01
rate_in = 0.05
rate_out = 0.06
rate_small = 0.3
step_number = 3


def standardize(values):
    centered = values - jnp.mean(values, axis=-1, keepdims=True)
    inverse = lax.rsqrt(jnp.mean(centered * centered, axis=-1, keepdims=True) + norm_eps)
    return (centered * inverse, inverse)


def norm_back(grad_hat, normal_hat, inverse):
    mean_grad = jnp.mean(grad_hat, axis=-1, keepdims=True)
    mean_cross = jnp.mean(grad_hat * normal_hat, axis=-1, keepdims=True)
    return (grad_hat - mean_grad - normal_hat * mean_cross) * inverse


def silu_slope(values):
    logistic = jax.nn.sigmoid(values)
    return logistic * (1.0 + values * (1.0 - logistic))


def adam_update(weight, grad, moment, second, rate):
    new_moment = beta_first * moment + (1.0 - beta_first) * grad
    new_second = beta_second * second + (1.0 - beta_second) * grad * grad
    moment_hat = new_moment / (1.0 - beta_first**step_number)
    second_hat = new_second / (1.0 - beta_second**step_number)
    new_weight = weight - rate * (
        moment_hat / (jnp.sqrt(second_hat) + adam_eps) + weight_decay * weight
    )
    return (new_moment, new_second, new_weight)


def by_events(
    item_ids,
    pos_buckets,
    time_buckets,
    item_table,
    proj_in,
    proj_out,
    small_params,
    out_grad,
    moment_in,
    second_in,
    moment_out,
    second_out,
    moment_small,
    second_small,
):
    seq_count, group = item_ids.shape
    length = group * lax.axis_size("blk")
    devices = lax.axis_size("blk") * lax.axis_size("dp")
    items = item_table.shape[0] * lax.axis_size("dp")
    tokens = seq_count * group
    scale = HEAD ** (-0.5)
    copy_in, copy_out, copy_small = (
        lax.all_gather(proj_in.astype(jnp.bfloat16), ("blk", "dp"), axis=0, tiled=True),
        lax.all_gather(proj_out.astype(jnp.bfloat16), ("blk", "dp"), axis=0, tiled=True),
        lax.all_gather(small_params.astype(jnp.bfloat16), ("blk", "dp"), axis=1, tiled=True),
    )
    small_float = copy_small.astype(jnp.float32)
    flat_ids = item_ids.reshape(tokens)
    portion = lax.all_gather(item_table, "dp", axis=0, tiled=True)
    hot = (flat_ids[:, None] == jnp.arange(portion.shape[0], dtype=jnp.int32)[None, :]).astype(
        jnp.bfloat16
    )
    embedded = jnp.dot(hot, portion, preferred_element_type=jnp.float32)
    hat_one, inverse_one = standardize(embedded)
    normed = (hat_one * small_float[0] + small_float[1]).astype(jnp.bfloat16)
    projected = jnp.dot(normed, copy_in, preferred_element_type=jnp.float32)
    activated = jax.nn.silu(projected)
    gate_u = activated[:, :D]
    rounded = activated[:, D:].astype(jnp.bfloat16)
    values = rounded[:, :D].reshape(seq_count, group, H, HEAD)
    queries = rounded[:, D : 2 * D].reshape(seq_count, group, H, HEAD)
    keys_own = rounded[:, 2 * D :].reshape(seq_count, group, H, HEAD)
    pos_table = small_float[4].reshape(H, NB)
    time_table = small_float[5].reshape(H, NB)
    buckets = jnp.arange(NB, dtype=jnp.int32)
    time_hot = (time_buckets[:, :, None] == buckets).astype(jnp.float32)
    query_bias = jnp.einsum("scb,hb->shc", time_hot, time_table)
    query_first = lax.axis_index("blk") * group
    query_pos = query_first + jnp.arange(group, dtype=jnp.int32)
    query_last = query_first + group - 1
    pos_sent = pos_buckets.astype(jnp.bfloat16)

    def tile_scores(key_blk, bucket_blk, key_start):
        pos_hot = (bucket_blk.astype(jnp.int32)[:, :, None] == buckets).astype(jnp.float32)
        key_bias = jnp.einsum("sjb,hb->shj", pos_hot, pos_table)
        raw_scores = (
            jnp.einsum("sihd,sjhd->shij", queries, key_blk, preferred_element_type=jnp.float32)
            * scale
        )
        raw_scores = raw_scores + query_bias[:, :, :, None] + key_bias[:, :, None, :]
        key_pos = key_start + jnp.arange(key_blk.shape[1], dtype=jnp.int32)
        allowed = (query_pos[:, None] >= key_pos[None, :])[None, None]
        return (raw_scores, allowed, pos_hot)

    attend_init = jnp.zeros((seq_count, group, H, HEAD), jnp.float32)
    running = attend_init
    key_part = lax.all_gather(keys_own, "blk", axis=1, tiled=True)
    value_part = lax.all_gather(values, "blk", axis=1, tiled=True)
    bucket_part = lax.all_gather(pos_sent, "blk", axis=1, tiled=True)
    span = key_part.shape[1]
    rows_blk = math.gcd(span, 512)

    def fold_step(carried, block_idx):
        key_start = block_idx * rows_blk
        key_blk = lax.dynamic_slice_in_dim(key_part, key_start, rows_blk, 1)
        value_blk = lax.dynamic_slice_in_dim(value_part, key_start, rows_blk, 1)
        bucket_blk = lax.dynamic_slice_in_dim(bucket_part, key_start, rows_blk, 1)

        def fold_compute(current):
            raw_scores, allowed, pos_hot = tile_scores(key_blk, bucket_blk, key_start)
            weights = jnp.where(allowed, jax.nn.silu(raw_scores) / length, 0.0).astype(jnp.bfloat16)
            return current + jnp.einsum(
                "shij,sjhd->sihd", weights, value_blk, preferred_element_type=jnp.float32
            )

        return (
            lax.cond(key_start <= query_last, fold_compute, lambda current: current, carried),
            None,
        )

    running, _ = lax.scan(fold_step, running, jnp.arange(span // rows_blk, dtype=jnp.int32))
    attended = running
    attended = attended.reshape(tokens, D)
    hat_two, inverse_two = standardize(attended)
    normed_two = hat_two * small_float[2] + small_float[3]
    gated = (normed_two * gate_u).astype(jnp.bfloat16)
    result = embedded + jnp.dot(gated, copy_out, preferred_element_type=jnp.float32)
    layer_out = result.astype(jnp.bfloat16).reshape(seq_count, group, D)
    cotangent = out_grad.reshape(tokens, D)
    grad_out_weight = jnp.einsum("td,te->de", gated, cotangent, preferred_element_type=jnp.float32)
    grad_gated = jnp.einsum("te,de->td", cotangent, copy_out, preferred_element_type=jnp.float32)
    grad_u = grad_gated * normed_two
    grad_norm_two = grad_gated * gate_u
    grad_gain_two = jnp.sum(grad_norm_two * hat_two, axis=0)
    grad_shift_two = jnp.sum(grad_norm_two, axis=0)
    grad_attended = norm_back(grad_norm_two * small_float[2], hat_two, inverse_two).astype(
        jnp.bfloat16
    )
    grad_attended = grad_attended.reshape(seq_count, group, H, HEAD)
    key_whole, value_whole, bucket_whole = (
        lax.all_gather(keys_own, "blk", axis=1, tiled=True),
        lax.all_gather(values, "blk", axis=1, tiled=True),
        lax.all_gather(pos_sent, "blk", axis=1, tiled=True),
    )
    rows_back = math.gcd(length, 512)

    def back_step(carried, block_idx):
        grad_query, grad_pos, grad_qbias = carried
        key_start = block_idx * rows_back
        key_blk = lax.dynamic_slice_in_dim(key_whole, key_start, rows_back, 1)
        value_blk = lax.dynamic_slice_in_dim(value_whole, key_start, rows_back, 1)
        bucket_blk = lax.dynamic_slice_in_dim(bucket_whole, key_start, rows_back, 1)

        def back_compute(operand):
            raw_scores, allowed, pos_hot = tile_scores(key_blk, bucket_blk, key_start)
            grad_weights = jnp.einsum(
                "sihd,sjhd->shij", grad_attended, value_blk, preferred_element_type=jnp.float32
            )
            grad_raw = jnp.where(
                allowed, grad_weights / length * silu_slope(raw_scores), 0.0
            ).astype(jnp.bfloat16)
            grad_raw_float = grad_raw.astype(jnp.float32)
            part_query = (
                jnp.einsum("shij,sjhd->sihd", grad_raw, key_blk, preferred_element_type=jnp.float32)
                * scale
            )
            part_pos = jnp.einsum("shj,sjb->hb", jnp.sum(grad_raw_float, axis=2), pos_hot)
            part_qbias = jnp.sum(grad_raw_float, axis=3)
            weights = jnp.where(allowed, jax.nn.silu(raw_scores) / length, 0.0).astype(jnp.bfloat16)
            part_key = (
                jnp.einsum("shij,sihd->sjhd", grad_raw, queries, preferred_element_type=jnp.float32)
                * scale
            )
            part_value = jnp.einsum(
                "shij,sihd->sjhd", weights, grad_attended, preferred_element_type=jnp.float32
            )
            paired = jnp.concatenate(
                [
                    part_key.reshape(seq_count, rows_back, D),
                    part_value.reshape(seq_count, rows_back, D),
                ],
                axis=-1,
            )
            return (part_query, part_pos, part_qbias, paired)

        def skip_tile(operand):
            empty = (
                jnp.zeros((seq_count, group, H, HEAD), jnp.float32),
                jnp.zeros((H, NB), jnp.float32),
                jnp.zeros((seq_count, H, group), jnp.float32),
            )
            return empty + (jnp.zeros((seq_count, rows_back, 2 * D), jnp.float32),)

        parts = lax.cond(key_start <= query_last, back_compute, skip_tile, 0)
        summed = (grad_query + parts[0], grad_pos + parts[1], grad_qbias + parts[2])
        return (summed, parts[3])

    back_init = (
        jnp.zeros((seq_count, group, H, HEAD), jnp.float32),
        jnp.zeros((H, NB), jnp.float32),
        jnp.zeros((seq_count, H, group), jnp.float32),
    )
    (grad_query, grad_pos_table, grad_qbias), stacked = lax.scan(
        back_step, back_init, jnp.arange(length // rows_back, dtype=jnp.int32)
    )
    kv_terms = stacked.transpose(1, 0, 2, 3).reshape(seq_count, length, 2 * D)
    kv_own = lax.psum_scatter(kv_terms, "blk", scatter_dimension=1, tiled=True)
    grad_key = kv_own[:, :, :D].reshape(tokens, D)
    grad_value = kv_own[:, :, D:].reshape(tokens, D)
    grad_time_table = jnp.einsum("shc,scb->hb", grad_qbias, time_hot)
    grad_acts = jnp.concatenate(
        [grad_u, grad_value, grad_query.reshape(tokens, D), grad_key], axis=-1
    )
    grad_pre = (grad_acts * silu_slope(projected)).astype(jnp.bfloat16)
    grad_in_weight = jnp.einsum("td,tf->df", normed, grad_pre, preferred_element_type=jnp.float32)
    grad_normed = jnp.einsum("tf,df->td", grad_pre, copy_in, preferred_element_type=jnp.float32)
    grad_gain_one = jnp.sum(grad_normed * hat_one, axis=0)
    grad_shift_one = jnp.sum(grad_normed, axis=0)
    grad_embed = cotangent.astype(jnp.float32) + norm_back(
        grad_normed * small_float[0], hat_one, inverse_one
    )
    input_grad = grad_embed.reshape(seq_count, group, D)
    grad_small = jnp.stack(
        [
            grad_gain_one,
            grad_shift_one,
            grad_gain_two,
            grad_shift_two,
            grad_pos_table.reshape(D),
            grad_time_table.reshape(D),
        ]
    )
    counts_local = jnp.sum(
        (flat_ids[:, None] == jnp.arange(items, dtype=jnp.int32)[None, :]).astype(jnp.float32),
        axis=0,
    )
    shard_in, shard_out, shard_small, item_counts = (
        lax.psum_scatter(grad_in_weight, ("blk", "dp"), scatter_dimension=0, tiled=True),
        lax.psum_scatter(grad_out_weight, ("blk", "dp"), scatter_dimension=0, tiled=True),
        lax.psum_scatter(grad_small, ("blk", "dp"), scatter_dimension=1, tiled=True),
        lax.psum_scatter(counts_local, ("blk", "dp"), scatter_dimension=0, tiled=True),
    )
    grad_rounded = grad_embed.astype(jnp.bfloat16)
    hot = (
        flat_ids[:, None]
        == jnp.arange(items // devices * lax.axis_size(("blk", "dp")), dtype=jnp.int32)[None, :]
    ).astype(jnp.bfloat16)
    table_grad = lax.psum_scatter(
        jnp.einsum("tr,td->rd", hot, grad_rounded, preferred_element_type=jnp.float32),
        ("blk", "dp"),
        scatter_dimension=0,
        tiled=True,
    )
    log_q = jnp.log(jnp.maximum(item_counts, 1.0) / (seq_count * lax.axis_size("dp") * length))
    new_moment_in, new_second_in, new_proj_in = adam_update(
        proj_in, shard_in, moment_in, second_in, rate_in
    )
    new_moment_out, new_second_out, new_proj_out = adam_update(
        proj_out, shard_out, moment_out, second_out, rate_out
    )
    new_moment_small, new_second_small, new_small = adam_update(
        small_params, shard_small, moment_small, second_small, rate_small
    )
    return (
        layer_out,
        input_grad,
        table_grad,
        item_counts,
        log_q,
        new_moment_in,
        new_second_in,
        new_proj_in,
        new_moment_out,
        new_second_out,
        new_proj_out,
        new_moment_small,
        new_second_small,
        new_small,
    )


MESH = pl.DeviceIdType.MESH
F32, BF16, I32 = jnp.float32, jnp.bfloat16, jnp.int32
LANES = 128
NN = (((1,), (0,)), ((), ()))
NT = (((1,), (1,)), ((), ()))
TN = (((0,), (0,)), ((), ()))


def mm(lhs, rhs, dims=NN):
    return lax.dot_general(lhs, rhs, dims, preferred_element_type=F32)


def iota(shape, dim):
    return lax.broadcasted_iota(I32, shape, dim)


def at(index, size):
    return pl.ds(pl.multiple_of(index * size, size), size)


def fused_kernel(sizes, *refs):
    nb, nz, group, items, weight_rows, tokens = sizes
    nd = nz * 2
    length = nb * group
    part = D // nb
    rows_table = items // (nb * nd)
    (
        ids_in, pos_in, time_in, table_in, proj_in, proj_out, small_in, out_grad_in,
        layer_out, input_out, table_out, grad_in_out, grad_out_out, little_out,
        send, recv, local,
        index, own_index, column, own_column, padded, table, weight, weight_send, outw,
        small, small_all, cot,
        embedded, normed, projected, gate, value, query, key, attended,
        grad_gated, stats, fix, gated_send, gated_got, grad_att, dq, dk, dv,
        grad_pre, part_send, part_core, part_x, part_got, stats_one, ig_send, ig_got,
        bias_sum, gain_sum, table_acc,
        table_sum, table_core, table_z, table_got,
        gi_sum, gi_core, gi_z, gi_got,
        go_sum, go_core, go_z, go_got,
        little, little_parts, little_all, little_got,
    ) = refs
    b = lax.axis_index("blk")
    d = lax.axis_index("dp")
    y, x, z, core = b // 2, b % 2, d // 2, d % 2
    other, off_y, off_x = 1 - core, 1 - y, 1 - x
    v = core * 2 + x
    home = core == y
    away = core != y

    counter = [0]

    def slots(count):
        base = counter[0]
        counter[0] += count
        return base

    def copy(src, dst, slot, target, landing=None):
        return pltpu.make_async_remote_copy(
            src_ref=src, dst_ref=dst, send_sem=send.at[slot],
            recv_sem=recv.at[slot if landing is None else landing],
            device_id={"blk": target[0], "dp": target[1]}, device_id_type=MESH,
        )

    def blk_peer(k):
        return (lax.rem(b + k, nb), d)

    def blk_from(k):
        return lax.rem(b + nb - k, nb)

    def z_to(k):
        return lax.rem(z + k, nz)

    def z_from(k):
        return lax.rem(z + nz - k, nz)

    def z_peer(k):
        return (b, z_to(k) * 2 + core)

    core_peer = (b, z * 2 + other)
    x_peer, y_peer = (y * 2 + off_x, d), (off_y * 2 + x, d)
    partner = (off_y * 2 + x, z * 2 + other)

    def row_peer(k):
        w = lax.rem(v + k, nb)
        return w, (y * 2 + w % 2, z * 2 + w // 2)

    def row_from(k):
        return lax.rem(v + nb - k, nb)

    pending = []

    def push(src, dst, slot, target, landing=None, where=None):
        def start():
            copy(src, dst, slot, target, landing).start()

        if where is None:
            start()
        else:
            pl.when(where)(start)
        pending.append((where, src, dst, slot, target))

    near = (z + 1 - 2 * (z % 2), 2 - z // 2, 3 * (1 - z // 2))
    steps = [(kr, kz) for kz in range(nz) for kr in range(nb) if kr + kz > 0]

    def slab(kr, kz):
        w, at_z = lax.rem(v + kr, nb), z_to(kz)
        return w, at_z, (y * 2 + w % 2, at_z * 2 + w // 2)

    def slab_from(kr, kz):
        return row_from(kr), z_from(kz)

    def arrive(dst, slot, where=None):
        wait = copy(dst, dst, slot, core_peer).wait_recv
        if where is None:
            wait()
        else:
            pl.when(where)(wait)

    table_load = pltpu.make_async_copy(table_in, table.at[d], local.at[0])
    table_load.start()
    cot_load = pltpu.make_async_copy(out_grad_in, cot.at[b], local.at[1])
    pl.when(home)(cot_load.start)
    own_index[...] = jnp.concatenate(
        [ids_in[...], pos_in[...], time_in[...], jnp.zeros((5, group), I32)], axis=0
    )

    @pl.when(home)
    def keep_index():
        index[b] = own_index[...]

    own_rows = proj_in[...].astype(BF16)
    for q in range(nb):
        weight_send[q] = jnp.concatenate(
            [own_rows[:, s * D + q * part : s * D + (q + 1) * part] for s in range(4)], axis=1
        )
    weight[y, x, z, core] = weight_send[v]
    outw[b, d] = proj_out[...].astype(BF16)
    width = small_in.shape[1]
    spread = (iota((width, LANES), 1) == iota((width, LANES), 0) + d * width).astype(F32)
    small_pad = jnp.concatenate([small_in[...], jnp.zeros((10, width), F32)], axis=0)
    small[y, x, z, core] = mm(small_pad.astype(BF16), spread.astype(BF16)).astype(BF16)

    barrier = pltpu.get_barrier_semaphore()
    peers = [slab(*k)[2] for k in steps]
    peers += [(off_y * 2 + x, z_to(kz) * 2 + c) for kz in range(nz) for c in range(2)]
    peers += [(off_y * 2 + off_x, z * 2 + c) for c in range(2)]
    for target in peers:
        pl.semaphore_signal(
            barrier, inc=1, device_id={"blk": target[0], "dp": target[1]}, device_id_type=MESH
        )
    pl.semaphore_wait(barrier, len(peers))

    table_load.wait()
    s_tz, s_tx, s_tc = slots(nz), slots(nz * nb), slots(nz * nb)
    for n in range(nz - 1):
        push(table.at[d, b], table.at[d, b], s_tz + n, (b, near[n] * 2 + core), s_tz + z)
    push(table.at[d], table.at[d], s_tc, core_peer, s_tc + z * nb)
    s_index, s_w, s_s = slots(nb), slots(nb * nz), slots(nb * nz)
    for k in range(nb):
        to = (core * 2 + (x + k % 2) % 2, z * 2 + (core + k // 2) % 2)
        push(own_index, index.at[b], s_index + k, to, s_index + b, away if k == 0 else None)
    for kr, kz in steps:
        w, at_z, to = slab(kr, kz)
        push(weight_send.at[w], weight.at[y, x, z, core], s_w + kz * nb + kr, to)
    for kr, kz in steps:
        w, at_z, to = slab(kr, kz)
        push(small.at[y, x, z, core], small.at[y, x, z, core], s_s + kz * nb + kr, to)
    s_g = slots(8)
    halves = (slice(0, group // 2), slice(group // 2, group))
    v_x, v_core, v_cross = core * 2 + off_x, other * 2 + x, other * 2 + off_x

    def cot_half(owner, n):
        return cot.at[owner, halves[n]]

    def cross_over():
        for n in range(2):
            push(out_grad_in.at[halves[n]], cot_half(b, n), s_g + n, partner, None, away)
        pl.when(home)(cot_load.wait)

    def own_half(n, where):
        push(cot_half(v, n), cot_half(v, n), s_g + 2 + n, x_peer, None, where)
        push(cot_half(v, n), cot_half(v, n), s_g + 4 + n, core_peer, None, where)

    def pass_on(n):
        arrive(cot_half(v_x, n), s_g + 2 + n)
        push(cot_half(v_x, n), cot_half(v_x, n), s_g + 6 + n, core_peer)

    s_wc, s_oz = slots(3 * nz), slots(nz)
    sides, opposite, second = (y, y, core), (off_y, off_y, other), (y_peer, y_peer, core_peer)

    def shard_of(n, side, at_z):
        if n == 2:
            return outw.at[b, at_z * 2 + side]
        return (weight, small)[n].at[side, :, at_z]

    def shard_next(n, kz):
        at_z = z_from(kz)
        if n == 2 and kz > 0:
            arrive(outw.at[b, at_z * 2 + core], s_oz + kz)
        for kr in range(nb):
            if n < 2 and kr + kz > 0:
                w = row_from(kr)
                arrive((weight, small)[n].at[y, w % 2, at_z, w // 2], (s_w, s_s)[n] + kz * nb + kr)
        ref = shard_of(n, sides[n], at_z)
        push(ref, ref, s_wc + n * nz + kz, second[n])

    def shards_end(n):
        for kz in range(nz):
            arrive(shard_of(n, opposite[n], z_from(kz)), s_wc + n * nz + kz)

    for i in range(nb):
        arrive(index.at[i], s_index + i, jnp.logical_or(away, b != i))
    padded[...] = jnp.zeros(padded.shape, F32)

    def to_column(e, carry):
        padded[0:8, :] = index[e].astype(F32)
        column[at(e, group), :] = jnp.transpose(padded[...]).astype(I32)
        return carry

    lax.fori_loop(0, nb, to_column, 0)
    padded[0:8, :] = own_index[...].astype(F32)
    own_column[...] = jnp.transpose(padded[...]).astype(I32)

    step = 256

    def table_over_z(n):
        shard = near[n] * 2 + core
        arrive(table.at[shard, b], s_tz + near[n])
        for m in range(1, nb):
            push(
                table.at[shard, b], table.at[shard, b], s_tx + n * nb + m, blk_peer(m),
                s_tx + near[n] * nb + m,
            )
        push(
            table.at[shard, b], table.at[shard, b], s_tc + (n + 1) * nb, core_peer,
            s_tc + near[n] * nb,
        )

    def table_over_blk(n):
        shard = near[n] * 2 + core
        for m in range(1, nb):
            quarter = table.at[shard, blk_from(m)]
            arrive(quarter, s_tx + near[n] * nb + m)
            push(quarter, quarter, s_tc + (n + 1) * nb + m, core_peer, s_tc + near[n] * nb + m)

    def table_over_core(n):
        shard = near[n] * 2 + other
        arrive(table.at[shard, b], s_tc + near[n] * nb)
        for m in range(1, nb):
            arrive(table.at[shard, blk_from(m)], s_tc + near[n] * nb + m)

    def picked_rows(rows, at_z, step=step):
        picked = column[rows, 0:1] - at_z * (items // nz)
        hot = jnp.where(iota((step, items // nz), 1) == picked, 1.0, 0.0).astype(BF16)
        return mm(hot, table[pl.ds(at_z * 2, 2)].reshape(items // nz, D)).astype(BF16)

    def look_up(at_z, first):
        def body(t, carry):
            rows = at(t, group)
            found = picked_rows(rows, at_z, group)
            embedded[rows, :] = found if first else embedded[rows, :] + found
            return carry

        lax.fori_loop(0, nb, body, 0)

    table_over_z(0)
    table_over_z(1)
    arrive(table.at[z * 2 + other], s_tc + z * nb)
    look_up(z, True)
    table_over_z(2)
    for k in range(1, nz):
        push(outw.at[b, d], outw.at[b, d], s_oz + k, z_peer(k))
    shard_next(0, 0)
    shard_next(0, 1)
    table_over_blk(0)
    table_over_blk(1)
    shard_next(0, 3)
    shard_next(0, 2)
    for kz in range(nz):
        shard_next(1, kz)
    cross_over()
    table_over_core(0)
    look_up(near[0], False)
    own_half(0, home)
    own_half(1, home)
    table_over_blk(2)
    table_over_core(1)
    look_up(near[1], False)
    for kz in range(nz):
        shard_next(2, kz)
    table_over_core(2)
    shards_end(0)
    shards_end(1)

    lane = iota((1, LANES), 1)
    for q in range(nb):
        total = sum(small[q // 2, q % 2, r // 2, r % 2].astype(F32) for r in range(nd))
        small_all[q] = total
    gain_one = jnp.concatenate([small_all[q][0:1] for q in range(nb)], axis=1)
    shift_one = jnp.concatenate([small_all[q][1:2] for q in range(nb)], axis=1)
    mine = small_all[v]
    gain_one_own = mine[0:1]
    gain_two, shift_two = mine[2:3], mine[3:4]
    pos_row, time_row = mine[4:5], mine[5:6]
    low = lane < NB
    pos_rows = (0.5 * pltpu.roll(pos_row, NB, 1), 0.5 * pos_row)
    time_rows = (0.5 * time_row, 0.5 * pltpu.roll(time_row, NB, 1))
    masks = (low, lane >= NB)

    def embed(t, carry):
        rows = at(t, step)
        found = embedded[rows, :] + picked_rows(rows, near[2])
        embedded[rows, :] = found
        found = found.astype(F32)
        mean = jnp.mean(found, axis=1, keepdims=True)
        centered = found - mean
        inverse = lax.rsqrt(jnp.mean(centered * centered, axis=1, keepdims=True) + norm_eps)
        fix[rows, :] = jnp.where(lane == 0, mean, inverse)
        ready = (centered * inverse * gain_one + shift_one).astype(BF16)
        normed[rows, :] = ready
        raw = mm(ready, weight[...].reshape(D, 4 * part))
        projected[rows, :] = raw
        act = raw * (0.5 + 0.5 * jnp.tanh(0.5 * raw))
        gate[rows, :] = act[:, 0:part]
        value[rows, :] = act[:, part : 2 * part].astype(BF16)
        queries = act[:, 2 * part : 3 * part].astype(BF16).astype(F32) * (0.5 * HEAD**-0.5)
        keys = act[:, 3 * part :].astype(BF16)
        time_hot = jnp.where(lane == column[rows, 2:3], 1.0, 0.0)
        pos_hot = jnp.where(lane == column[rows, 1:2] + NB, 1.0, 0.0)
        for h in range(2):
            query[h, rows, 0:LANES] = jnp.where(masks[h], queries, 0.0).astype(BF16)
            query[h, rows, LANES:] = jnp.where(low, time_hot, pos_rows[h]).astype(BF16)
            key[h, rows, 0:LANES] = keys
            key[h, rows, LANES:] = jnp.where(low, time_rows[h], pos_hot).astype(BF16)
        return carry

    lax.fori_loop(0, length // step // 2, embed, 0)
    shards_end(2)
    s_oy, s_ox = slots(1), slots(2)
    push(outw.at[b], outw.at[b], s_oy, y_peer)
    for n in range(2):
        arrive(cot_half(v, n), s_g + n, away)
        own_half(n, away)
    lax.fori_loop(length // step // 2, length // step, embed, 0)

    s_st = slots(nb * nb)
    inv_length = 1.0 / length

    def forward(r, carry):
        i = nb - 1 - r
        rows = at(i, group)
        dq[...] = jnp.zeros(dq.shape, F32)

        def tile(j, masked):
            cols = at(j, group)
            for h in range(2):
                x = mm(query[h, rows, :], key[h, cols, :], NT)
                w = x + x * jnp.tanh(x)
                if masked:
                    w = jnp.where(iota(w.shape, 0) >= iota(w.shape, 1), w, 0.0)
                dq[h, :, 0:LANES] += mm(w.astype(BF16), value[cols, :])

        def full(j, inner):
            tile(j, False)
            return inner

        lax.fori_loop(0, i, full, 0)
        tile(i, True)
        att = jnp.where(low, dq[0, :, 0:LANES], dq[1, :, 0:LANES]) * inv_length
        attended[rows, :] = att

        @pl.when(r == 1)
        def cotangents():
            pass_on(0)
            pass_on(1)

        return carry

    lax.fori_loop(0, nb, forward, 0)
    arrive(outw.at[off_y * 2 + x], s_oy)
    out_rows = outw[v].reshape(part, D)
    for n in range(2):
        arrive(cot_half(v_core, n), s_g + 4 + n)
        arrive(cot_half(v_cross, n), s_g + 6 + n)

    def statistics(r, carry):
        i = nb - 1 - r
        rows = at(i, group)
        att = attended[rows, :]
        gg = mm(cot[i], out_rows, NT)
        grad_gated[rows, :] = gg
        g = gg * gate[rows, :] * gain_two
        mean = jnp.mean(att, axis=1, keepdims=True)
        centered = att - mean
        square = jnp.sum(centered * centered, axis=1, keepdims=True)
        sum_g = jnp.sum(g, axis=1, keepdims=True)
        sum_ga = jnp.sum(g * centered, axis=1, keepdims=True)
        packed = jnp.where(
            lane == 0, mean, jnp.where(lane == 1, square, jnp.where(lane == 2, sum_g, sum_ga))
        )
        packed = jnp.transpose(packed)
        stats[v, i] = jnp.concatenate(
            [packed[0:4, 0 : group // 2], packed[0:4, group // 2 :]], axis=0
        )
        for k in range(1, nb):
            copy(stats.at[v, i], stats.at[v, i], s_st + i * nb + k, row_peer(k)[1]).start()
        return carry

    lax.fori_loop(0, nb, statistics, 0)

    push(outw.at[v], outw.at[v], s_ox, x_peer)

    s_pc, s_px, s_s1, s_gt = slots(nb), slots(nb), slots(nb * nb), slots(nb)
    dk[...] = jnp.zeros(dk.shape, F32)
    dv[...] = jnp.zeros(dv.shape, F32)
    bias_sum[...] = jnp.zeros(bias_sum.shape, F32)
    gain_sum[...] = jnp.zeros(gain_sum.shape, F32)

    def backward(r, carry):
        i = nb - 1 - r
        rows = at(i, group)
        for k in range(1, nb):
            arrive(stats.at[row_from(k), i], s_st + i * nb + k)
        every = [jnp.concatenate([stats[q, i, 0:4], stats[q, i, 4:8]], axis=1) for q in range(nb)]
        mean = sum(s[0:1] for s in every) * (1.0 / nb)
        square = sum(s[1:2] + part * (s[0:1] - mean) * (s[0:1] - mean) for s in every)
        inverse = lax.rsqrt(square * (1.0 / D) + norm_eps)
        mean_g = sum(s[2:3] for s in every) * (1.0 / D)
        cross = inverse * sum(s[3:4] + (s[0:1] - mean) * s[2:3] for s in every) * (1.0 / D)
        padded[0:1, :] = mean
        padded[1:2, :] = inverse
        padded[2:3, :] = mean_g
        padded[3:4, :] = cross
        turned = jnp.transpose(padded[...])
        inverse = turned[:, 1:2]
        hat = (attended[rows, :] - turned[:, 0:1]) * inverse
        normal = hat * gain_two + shift_two
        gated_send[i] = (normal * gate[rows, :]).astype(BF16)

        @pl.when(jnp.logical_or(away, i != b))
        def send_gated():
            copy(gated_send.at[i], gated_got.at[v], s_gt + i, (i, z * 2 + y), s_gt + v).start()

        @pl.when(jnp.logical_and(home, i == b))
        def keep_gated():
            gated_got[v] = gated_send[i]

        gg = grad_gated[rows, :]
        grad_u = gg * normal
        grad_norm = gg * gate[rows, :]
        gain_sum[2:3, :] += jnp.sum(grad_norm * hat, axis=0, keepdims=True)
        gain_sum[3:4, :] += jnp.sum(grad_norm, axis=0, keepdims=True)
        ga = (grad_norm * gain_two - turned[:, 2:3] - hat * turned[:, 3:4]) * inverse
        for h in range(2):
            grad_att[h] = jnp.where(masks[h], ga, 0.0).astype(BF16)
        dq[...] = jnp.zeros(dq.shape, F32)

        def tile(j, masked):
            cols = at(j, group)
            for h in range(2):
                x = mm(key[h, cols, :], query[h, rows, :], NT)
                t = jnp.tanh(x)
                u = 1.0 + t
                w = x * u
                slope = u * (1.0 + x * (1.0 - t))
                if masked:
                    allowed = iota(w.shape, 0) <= iota(w.shape, 1)
                    w = jnp.where(allowed, w, 0.0)
                    slope = jnp.where(allowed, slope, 0.0)
                dw = mm(value[cols, :], grad_att[h], NT)
                graw = (dw * slope).astype(BF16)
                dv[j] += mm(w.astype(BF16), grad_att[h])
                back = mm(graw, query[h, rows, :])
                dk[j] += back[:, 0:LANES]
                bias_sum[h : h + 1, :] += jnp.sum(back[:, LANES:], axis=0, keepdims=True)
                dq[h] += mm(graw, key[h, cols, :], TN)

        def full(j, inner):
            tile(j, False)
            return inner

        lax.fori_loop(0, i, full, 0)
        tile(i, True)
        for h in range(2):
            bias_sum[2 + h : 3 + h, :] += jnp.sum(dq[h, :, LANES:], axis=0, keepdims=True)
        grad_q = jnp.where(low, dq[0, :, 0:LANES], dq[1, :, 0:LANES]) * (
            0.5 * inv_length * HEAD**-0.5
        )
        raw = projected[rows, :]
        logistic = 0.5 + 0.5 * jnp.tanh(0.5 * raw)
        slope = logistic * (1.0 + raw * (1.0 - logistic))
        acts = jnp.concatenate([grad_u, dv[i] * inv_length, grad_q, dk[i] * inv_length], axis=1)
        pre = (acts * slope).astype(BF16)
        grad_pre[rows, :] = pre
        partial = mm(pre, weight[...].reshape(D, 4 * part), NT)
        scaled = partial * gain_one
        first = jnp.sum(scaled, axis=1, keepdims=True)
        mean_one, inverse_one = fix[rows, 0:1], fix[rows, 1:2]
        hat_one = (embedded[rows, :].astype(F32) - mean_one) * inverse_one
        second = jnp.sum(scaled * hat_one, axis=1, keepdims=True)
        turned = jnp.transpose(jnp.where(lane == 0, first, second))
        stats_one[v, i] = jnp.concatenate(
            [turned[n : n + 1, at_lane : at_lane + LANES] for n in range(2) for at_lane in range(0, group, LANES)],
            axis=0,
        )
        for q in range(nb):
            part_send[i, q] = partial[:, q * part : (q + 1) * part].astype(BF16)
        core_part(i).start()
        for k in range(1, nb):
            copy(stats_one.at[v, i], stats_one.at[v, i], s_s1 + i * nb + k, row_peer(k)[1]).start()

        @pl.when(r > 0)
        def previous():
            over_x(i + 1)

        return carry

    def core_part(i):
        half = part_send.at[i, pl.ds(other * 2, 2)]
        return copy(half, part_core.at[i], s_pc + i, core_peer)

    def x_part(i):
        return copy(part_x.at[i], part_got.at[i], s_px + i, x_peer)

    def over_x(i):
        core_part(i).wait_recv()
        both = part_send[i, v_x].astype(F32) + part_core[i, off_x].astype(F32)
        part_x[i] = both.astype(BF16)
        x_part(i).start()

    lax.fori_loop(0, nb, backward, 0)
    over_x(0)
    arrive(outw.at[v_x], s_ox)
    push(outw.at[v_x], outw.at[v_x], s_ox + 1, core_peer)

    def gi_half(side, k):
        return gi_sum.at[side, :, k]

    def table_half(side, k):
        return table_sum.at[side, :, k]

    def go_half(side, k):
        return go_sum.at[k, side]

    order = (near[2], near[1], near[0], z)

    def y_stage(half, landing, base):
        for n, k in enumerate(order):
            push(half(off_y, k), landing.at[k], base + n, y_peer)

    def y_sum(half, landing, outgoing, base, n):
        k = order[n]
        arrive(landing.at[k], base + n)
        outgoing[k] = (half(y, k)[...].astype(F32) + landing[k].astype(F32)).astype(BF16)

    def owner_stage(outgoing, landing, base, n):
        k = order[n]
        for w in range(nb):
            to = (y * 2 + w % 2, k * 2 + w // 2)
            own = n == nz - 1
            push(
                outgoing.at[k, w % 2, w // 2], landing.at[v, z], base + n * nb + w, to,
                base + z * nb + v, v != w if own else None,
            )
        if own:
            landing[v, z] = outgoing[z, x, core]

    def owner_sum(landing, base, result):
        for n, k in enumerate(order):
            for w in range(nb):
                arrive(landing.at[w, k], base + k * nb + w, v != w if n == nz - 1 else None)
        for q in range(nb):
            result[q] = sum(landing[q, k].astype(F32) for k in range(nz))

    s_gic, s_gio = slots(nz), slots(nz * nb)
    s_goc, s_goz = slots(nz), slots(nz)

    gated_all = gated_send[...].reshape(length, part)
    go_sum[...] = mm(gated_all, cot[...].reshape(length, D), TN).astype(BF16).reshape(go_sum.shape)
    y_stage(go_half, go_core, s_goc)

    def weight_grad(t, carry):
        cols = at(t, LANES)
        got = mm(normed[:, cols], grad_pre[...], TN).astype(BF16)
        gi_sum[t // 2, t % 2] = got.reshape(gi_sum.shape[2:])
        return carry

    lax.fori_loop(0, nb, weight_grad, 0)
    y_stage(gi_half, gi_core, s_gic)

    s_ig = slots(nb)

    def input_part(r, carry):
        i = nb - 1 - r
        rows = at(i, group)
        x_part(i).wait_recv()
        for k in range(1, nb):
            arrive(stats_one.at[row_from(k), i], s_s1 + i * nb + k)
        total = (
            part_send[i, v].astype(F32) + part_core[i, x].astype(F32) + part_got[i].astype(F32)
        )
        row = sum(stats_one[q, i] for q in range(nb)) * (1.0 / D)
        row = jnp.concatenate(
            [
                jnp.concatenate([row[n * 4 + m : n * 4 + m + 1] for m in range(4)], axis=1)
                for n in range(2)
            ],
            axis=0,
        )
        padded[0:2, :] = row
        turned = jnp.transpose(padded[...])
        mean_one, inverse_one = fix[rows, 0:1], fix[rows, 1:2]
        mycols = at(v, part)
        hat_one = (embedded[rows, mycols].astype(F32) - mean_one) * inverse_one
        gain_sum[0:1, :] += jnp.sum(total * hat_one, axis=0, keepdims=True)
        gain_sum[1:2, :] += jnp.sum(total, axis=0, keepdims=True)
        back = (total * gain_one_own - turned[:, 0:1] - hat_one * turned[:, 1:2]) * inverse_one
        ig_send[i] = (cot[i, :, mycols].astype(F32) + back).astype(BF16)
        return carry

    s_tgc, s_tgo = slots(nz), slots(nz * nb)

    def gi_over(n):
        y_sum(gi_half, gi_core, gi_z, s_gic, n)
        owner_stage(gi_z, gi_got, s_gio, n)

    def table_rows(i, t):
        hot = jnp.where(iota((group, group), 0) + t * group == index[i][0:1], 1.0, 0.0)
        return mm(hot.astype(BF16), ig_send[i])

    def table_add(i, first):
        def add(t, carry):
            rows = at(t, group)
            got = table_rows(i, t)
            table_acc[rows, :] = got if first else table_acc[rows, :] + got
            return carry

        lax.fori_loop(0, items // group, add, 0)

    def table_part(t, carry):
        got = (table_acc[at(t, group), :] + table_rows(0, t)).astype(BF16)
        table_sum[t // 2, t % 2] = got.reshape(table_sum.shape[2:])
        return carry

    for r in range(nb - 1):
        input_part(r, 0)
        table_add(nb - 1 - r, r == 0)
        if r == 1:
            gi_over(0)
            gi_over(1)
        if r == 2:
            gi_over(2)
    input_part(nb - 1, 0)
    lax.fori_loop(off_y * 2, off_y * 2 + 2, table_part, 0)
    y_stage(table_half, table_core, s_tgc)
    for k in range(nb):
        i = lax.rem(b + k, nb)
        push(ig_send.at[i], ig_got.at[v], s_ig + k, (i, z * 2 + y), s_ig + v, away if k == 0 else None)

    @pl.when(home)
    def keep_input():
        ig_got[v] = ig_send[b]

    lax.fori_loop(y * 2, y * 2 + 2, table_part, 0)
    gi_over(3)
    for n in range(nz):
        y_sum(go_half, go_core, go_z, s_goc, n)
    for k in range(nz):
        push(go_z.at[z_to(k)], go_got.at[z], s_goz + k, (v, z_to(k) * 2 + y), None, away if k == 0 else None)

    @pl.when(home)
    def keep_rows():
        go_got[z] = go_z[z]


    s_l, s_lx = slots(nd), slots(1)
    own_items = items // nb

    def count(t, carry):
        picked = column[at(t, step), 0:1]
        hit = jnp.where(iota((step, own_items), 1) + v * own_items == picked, 1.0, 0.0)
        return carry + jnp.sum(hit, axis=0, keepdims=True)

    counted = lax.fori_loop(0, length // step, count, jnp.zeros((1, own_items), F32))
    time_grad = jnp.where(low, bias_sum[0:1, :], pltpu.roll(bias_sum[1:2, :], NB, 1))
    pos_grad = jnp.where(low, pltpu.roll(bias_sum[2:3, :], NB, 1), bias_sum[3:4, :])
    halved = 0.5 * inv_length
    little[...] = jnp.zeros(little.shape, F32)
    little[0:4, :] = gain_sum[0:4, :]
    little[4:5, :] = pos_grad * halved
    little[5:6, :] = time_grad * halved
    for q in range(own_items // LANES):
        little[8 + q : 9 + q, :] = counted[:, q * LANES : (q + 1) * LANES]
    columns = [(ky, kz) for kz in range(nz) for ky in range(2) if ky + kz > 0]
    for ky, kz in columns:
        to = (lax.rem(y + ky, 2) * 2 + x, z_to(kz) * 2 + core)
        push(little, little_parts.at[kz * 2 + ky], s_l + kz * 2 + ky, to)
    def from_row(landing, base):
        for w in range(nb):
            arrive(landing.at[w], base + w, jnp.logical_or(away, v != w))

    from_row(gated_got, s_gt)
    arrive(outw.at[other * 2 + off_x], s_ox + 1)

    def finish_layer(t, carry):
        rows = at(t, step)
        hot = jnp.where(iota((step, items), 1) == own_column[rows, 0:1], 1.0, 0.0).astype(BF16)
        result = mm(hot, table[...].reshape(items, D))
        for q in range(nb):
            result = result + mm(gated_got[q, rows, :], outw[q].reshape(part, D))
        layer_out[rows, :] = result.astype(BF16)
        return carry

    lax.fori_loop(0, group // step, finish_layer, 0)

    for n in range(nz):
        y_sum(table_half, table_core, table_z, s_tgc, n)
        owner_stage(table_z, table_got, s_tgo, n)
    totals = little[...]
    for ky, kz in columns:
        arrive(little_parts.at[kz * 2 + ky], s_l + kz * 2 + ky)
        totals = totals + little_parts[kz * 2 + ky]
    little_all[...] = totals
    push(little_all, little_got, s_lx, core_peer)

    owner_sum(gi_got, s_gio, grad_in_out)
    for k in range(nz):
        arrive(go_got.at[z_from(k)], s_goz + k, away if k == 0 else None)
    grad_out_out[...] = sum(go_got[k].astype(F32) for k in range(nz))
    from_row(ig_got, s_ig)
    input_out[...] = ig_got[...]
    arrive(little_got, s_lx)

    @pl.when(home)
    def keep_own():
        little_out[...] = little_all[...]

    @pl.when(away)
    def take_peers():
        little_out[...] = little_got[...]

    owner_sum(table_got, s_tgo, table_out)

    for where, *sent in pending:
        if where is None:
            copy(*sent).wait_send()
        else:
            pl.when(where)(copy(*sent).wait_send)

    def drain(i, carry):
        for k in range(1, nb):
            to = row_peer(k)[1]
            copy(stats.at[v, i], stats.at[v, i], s_st + i * nb + k, to).wait_send()
            copy(stats_one.at[v, i], stats_one.at[v, i], s_s1 + i * nb + k, to).wait_send()
        core_part(i).wait_send()
        x_part(i).wait_send()
        sent_gated = copy(gated_send.at[i], gated_got.at[v], s_gt + i, (i, z * 2 + y), s_gt + v)
        pl.when(jnp.logical_or(away, i != b))(sent_gated.wait_send)
        return carry

    lax.fori_loop(0, nb, drain, 0)
    assert counter[0] <= send.shape[0], counter[0]


def finish_kernel(sizes, *refs):
    nb, nz, group, items, weight_rows, tokens = sizes
    part = D // nb
    rows_table = items // (nb * nz * 2)
    (
        layer_in, input_in, table_in, grad_in_in, grad_out_in, little_in,
        proj_in, proj_out, small_in,
        moment_in, second_in, moment_out, second_out, moment_small, second_small,
        layer_out, input_grad, table_grad, counts_out, logq_out,
        new_m_in, new_s_in, new_w_in, new_m_out, new_s_out, new_w_out,
        new_m_small, new_s_small, new_w_small,
    ) = refs
    d = lax.axis_index("dp")
    layer_out[...] = layer_in[...]
    for q in range(nb):
        cols = slice(q * part, (q + 1) * part)
        input_grad[:, cols] = input_in[q].astype(F32)
        table_grad[:, cols] = table_in[q]
        for s in range(4):
            own = slice(s * D + q * part, s * D + (q + 1) * part)
            new_m_in[:, own], new_s_in[:, own], new_w_in[:, own] = adam_update(
                proj_in[:, own], grad_in_in[q, :, s * part : (s + 1) * part],
                moment_in[:, own], second_in[:, own], rate_in,
            )
    new_m_out[...], new_s_out[...], new_w_out[...] = adam_update(
        proj_out[...], grad_out_in[...], moment_out[...], second_out[...], rate_out
    )
    width = small_in.shape[1]
    shifted = pltpu.roll(little_in[0:8, :], lax.rem(LANES - d * width, LANES), 1)[0:6, 0:width]
    new_m_small[...], new_s_small[...], new_w_small[...] = adam_update(
        small_in[...], shifted, moment_small[...], second_small[...], rate_small
    )
    per_row = LANES // rows_table
    count_row = little_in[pl.ds(8 + d // per_row, 1), :]
    count_row = pltpu.roll(
        jnp.broadcast_to(count_row, (8, LANES)),
        lax.rem(LANES - lax.rem(d, per_row) * rows_table, LANES), 1,
    )[0:1, 0:rows_table]
    counts_out[...] = count_row
    logq_out[...] = jnp.log(jnp.maximum(count_row, 1.0) * (1.0 / tokens))


def fused(sizes, args):
    nb, nz, group, items, weight_rows, tokens = sizes
    nd = nz * 2
    length = nb * group
    part = D // nb
    rows_table = items // (nb * nd)
    (
        item_ids, pos_buckets, time_buckets, item_table, proj_in, proj_out, small_params, out_grad,
        moment_in, second_in, moment_out, second_out, moment_small, second_small,
    ) = args
    width = small_params.shape[1]
    shape = jax.ShapeDtypeStruct
    middle = [
        shape((group, D), BF16), shape((nb, group, part), BF16), shape((nb, rows_table, part), F32),
        shape((nb, weight_rows, 4 * part), F32), shape((weight_rows, D), F32), shape((16, LANES), F32),
    ]
    outs = [
        shape((group, D), BF16), shape((group, D), F32), shape((rows_table, D), F32),
        shape((1, rows_table), F32), shape((1, rows_table), F32),
        *[shape(proj_in.shape, F32)] * 3, *[shape(proj_out.shape, F32)] * 3,
        *[shape(small_params.shape, F32)] * 3,
    ]
    vm = pltpu.VMEM
    scratch = [
        pltpu.SemaphoreType.DMA((256,)), pltpu.SemaphoreType.DMA((256,)), pltpu.SemaphoreType.DMA((2,)),
        vm((nb, 8, group), I32),
        vm((8, group), I32),
        vm((length, LANES), I32),
        vm((group, LANES), I32),
        vm((LANES, group), F32),
        vm((nd, nb, rows_table, D), BF16),
        vm((2, 2, nz, 2, weight_rows, 4 * part), BF16),
        vm((nb, weight_rows, 4 * part), BF16),
        vm((nb, nd, weight_rows, D), BF16),
        vm((2, 2, nz, 2, 16, LANES), BF16),
        vm((nb, 16, LANES), F32),
        vm((nb, group, D), BF16),
        vm((length, D), BF16),
        vm((length, D), BF16),
        vm((length, 4 * part), F32),
        vm((length, part), F32),
        vm((length, part), BF16),
        vm((2, length, 2 * LANES), BF16),
        vm((2, length, 2 * LANES), BF16),
        vm((length, part), F32),
        vm((length, part), F32),
        vm((nb, nb, 8, group // 2), F32),
        vm((length, LANES), F32),
        vm((nb, group, part), BF16),
        vm((nb, group, part), BF16),
        vm((2, group, part), BF16),
        vm((2, group, 2 * LANES), F32),
        vm((nb, group, part), F32),
        vm((nb, group, part), F32),
        vm((length, 4 * part), BF16),
        vm((nb, nb, group, part), BF16),
        vm((nb, 2, group, part), BF16),
        vm((nb, group, part), BF16),
        vm((nb, group, part), BF16),
        vm((nb, nb, 8, LANES), F32),
        vm((nb, group, part), BF16),
        vm((nb, group, part), BF16),
        vm((8, LANES), F32),
        vm((8, LANES), F32),
        vm((items, part), F32),
        vm((2, 2, nz, 2, rows_table, part), BF16),
        *[vm((nz, 2, 2, rows_table, part), BF16)] * 2,
        vm((nb, nz, rows_table, part), BF16),
        vm((2, 2, nz, 2, weight_rows, 4 * part), BF16),
        *[vm((nz, 2, 2, weight_rows, 4 * part), BF16)] * 2,
        vm((nb, nz, weight_rows, 4 * part), BF16),
        vm((nz, 2, weight_rows, D), BF16),
        *[vm((nz, weight_rows, D), BF16)] * 3,
        vm((16, LANES), F32),
        vm((nd, 16, LANES), F32),
        *[vm((16, LANES), F32)] * 2,
    ]
    whole, far = pl.BlockSpec(memory_space=pltpu.VMEM), pl.BlockSpec(memory_space=pl.ANY)
    between = pl.pallas_call(
        functools.partial(fused_kernel, sizes),
        out_shape=middle,
        in_specs=[whole] * 3 + [far] + [whole] * 3 + [far],
        out_specs=[whole] * len(middle),
        scratch_shapes=scratch,
        compiler_params=pltpu.CompilerParams(
            collective_id=0, has_side_effects=True, vmem_limit_bytes=60 * 2**20
        ),
        name="hstu_step",
    )(
        item_ids, pos_buckets, time_buckets,
        item_table.reshape(nb, item_table.shape[0] // nb, D),
        proj_in, proj_out, small_params, out_grad.reshape(group, D),
    )
    got = pl.pallas_call(
        functools.partial(finish_kernel, sizes),
        out_shape=outs,
        in_specs=[whole] * (len(middle) + 9),
        out_specs=[whole] * len(outs),
        name="hstu_finish",
    )(
        *between, proj_in, proj_out, small_params,
        moment_in, second_in, moment_out, second_out, moment_small, second_small,
    )
    return (
        got[0].reshape(out_grad.shape), got[1].reshape(out_grad.shape), got[2],
        got[3].reshape(rows_table), got[4].reshape(rows_table), *got[5:],
    )


def per_device(*args):
    item_ids, item_table, proj_in, small_params = args[0], args[3], args[4], args[6]
    seq_count, group = item_ids.shape
    nb, nd = lax.axis_size("blk"), lax.axis_size("dp")
    items = item_table.shape[0] * nd
    by_heads = (
        seq_count == 1 and nd % 2 == 0 and D // nb == LANES and group % 256 == 0
        and items == 2048 and proj_in.shape[0] % 16 == 0
        and small_params.shape[1] * nd == LANES and nb == 4 and nd == 8
    )
    if by_heads:
        sizes = (nb, nd // 2, group, items, proj_in.shape[0], nd * nb * group)
        return fused(sizes, args)
    return by_events(*args)


def solution(mesh):
    placed = (
        P("dp", "blk"),
        P("dp", "blk"),
        P("dp", "blk"),
        P("dp", None),
        P(("blk", "dp"), None),
        P(("blk", "dp"), None),
        P(None, ("blk", "dp")),
        P("dp", "blk", None),
        P(("blk", "dp"), None),
        P(("blk", "dp"), None),
        P(("blk", "dp"), None),
        P(("blk", "dp"), None),
        P(None, ("blk", "dp")),
        P(None, ("blk", "dp")),
    )
    return jax.shard_map(
        per_device,
        mesh=mesh,
        in_specs=placed,
        out_specs=(
            P("dp", "blk", None),
            P("dp", "blk", None),
            P(("blk", "dp"), None),
            P(("blk", "dp")),
            P(("blk", "dp")),
            P(("blk", "dp"), None),
            P(("blk", "dp"), None),
            P(("blk", "dp"), None),
            P(("blk", "dp"), None),
            P(("blk", "dp"), None),
            P(("blk", "dp"), None),
            P(None, ("blk", "dp")),
            P(None, ("blk", "dp")),
            P(None, ("blk", "dp")),
        ),
        check_vma=False,
    )
```

```python
import functools
import math

import jax
import jax.numpy as jnp
from jax import lax
from jax.experimental import pallas as pl
from jax.experimental.pallas import tpu as pltpu
from jax.sharding import PartitionSpec as P

D = 512
H = 8
HEAD = 64
NB = 64


norm_eps = 1e-05
beta_first = 0.5
beta_second = 0.5
adam_eps = 1e-08
weight_decay = 0.01
rate_in = 0.05
rate_out = 0.06
rate_small = 0.3
step_number = 3


def standardize(values):
    centered = values - jnp.mean(values, axis=-1, keepdims=True)
    inverse = lax.rsqrt(jnp.mean(centered * centered, axis=-1, keepdims=True) + norm_eps)
    return (centered * inverse, inverse)


def norm_back(grad_hat, normal_hat, inverse):
    mean_grad = jnp.mean(grad_hat, axis=-1, keepdims=True)
    mean_cross = jnp.mean(grad_hat * normal_hat, axis=-1, keepdims=True)
    return (grad_hat - mean_grad - normal_hat * mean_cross) * inverse


def silu_slope(values):
    logistic = jax.nn.sigmoid(values)
    return logistic * (1.0 + values * (1.0 - logistic))


def adam_update(weight, grad, moment, second, rate):
    new_moment = beta_first * moment + (1.0 - beta_first) * grad
    new_second = beta_second * second + (1.0 - beta_second) * grad * grad
    moment_hat = new_moment / (1.0 - beta_first**step_number)
    second_hat = new_second / (1.0 - beta_second**step_number)
    new_weight = weight - rate * (
        moment_hat / (jnp.sqrt(second_hat) + adam_eps) + weight_decay * weight
    )
    return (new_moment, new_second, new_weight)


def by_events(
    item_ids,
    pos_buckets,
    time_buckets,
    item_table,
    proj_in,
    proj_out,
    small_params,
    out_grad,
    moment_in,
    second_in,
    moment_out,
    second_out,
    moment_small,
    second_small,
):
    seq_count, group = item_ids.shape
    length = group * lax.axis_size("blk")
    devices = lax.axis_size("blk") * lax.axis_size("dp")
    items = item_table.shape[0] * lax.axis_size("dp")
    tokens = seq_count * group
    scale = HEAD ** (-0.5)
    copy_in, copy_out, copy_small = (
        lax.all_gather(proj_in.astype(jnp.bfloat16), ("blk", "dp"), axis=0, tiled=True),
        lax.all_gather(proj_out.astype(jnp.bfloat16), ("blk", "dp"), axis=0, tiled=True),
        lax.all_gather(small_params.astype(jnp.bfloat16), ("blk", "dp"), axis=1, tiled=True),
    )
    small_float = copy_small.astype(jnp.float32)
    flat_ids = item_ids.reshape(tokens)
    portion = lax.all_gather(item_table, "dp", axis=0, tiled=True)
    hot = (flat_ids[:, None] == jnp.arange(portion.shape[0], dtype=jnp.int32)[None, :]).astype(
        jnp.bfloat16
    )
    embedded = jnp.dot(hot, portion, preferred_element_type=jnp.float32)
    hat_one, inverse_one = standardize(embedded)
    normed = (hat_one * small_float[0] + small_float[1]).astype(jnp.bfloat16)
    projected = jnp.dot(normed, copy_in, preferred_element_type=jnp.float32)
    activated = jax.nn.silu(projected)
    gate_u = activated[:, :D]
    rounded = activated[:, D:].astype(jnp.bfloat16)
    values = rounded[:, :D].reshape(seq_count, group, H, HEAD)
    queries = rounded[:, D : 2 * D].reshape(seq_count, group, H, HEAD)
    keys_own = rounded[:, 2 * D :].reshape(seq_count, group, H, HEAD)
    pos_table = small_float[4].reshape(H, NB)
    time_table = small_float[5].reshape(H, NB)
    buckets = jnp.arange(NB, dtype=jnp.int32)
    time_hot = (time_buckets[:, :, None] == buckets).astype(jnp.float32)
    query_bias = jnp.einsum("scb,hb->shc", time_hot, time_table)
    query_first = lax.axis_index("blk") * group
    query_pos = query_first + jnp.arange(group, dtype=jnp.int32)
    query_last = query_first + group - 1
    pos_sent = pos_buckets.astype(jnp.bfloat16)

    def tile_scores(key_blk, bucket_blk, key_start):
        pos_hot = (bucket_blk.astype(jnp.int32)[:, :, None] == buckets).astype(jnp.float32)
        key_bias = jnp.einsum("sjb,hb->shj", pos_hot, pos_table)
        raw_scores = (
            jnp.einsum("sihd,sjhd->shij", queries, key_blk, preferred_element_type=jnp.float32)
            * scale
        )
        raw_scores = raw_scores + query_bias[:, :, :, None] + key_bias[:, :, None, :]
        key_pos = key_start + jnp.arange(key_blk.shape[1], dtype=jnp.int32)
        allowed = (query_pos[:, None] >= key_pos[None, :])[None, None]
        return (raw_scores, allowed, pos_hot)

    attend_init = jnp.zeros((seq_count, group, H, HEAD), jnp.float32)
    running = attend_init
    key_part = lax.all_gather(keys_own, "blk", axis=1, tiled=True)
    value_part = lax.all_gather(values, "blk", axis=1, tiled=True)
    bucket_part = lax.all_gather(pos_sent, "blk", axis=1, tiled=True)
    span = key_part.shape[1]
    rows_blk = math.gcd(span, 512)

    def fold_step(carried, block_idx):
        key_start = block_idx * rows_blk
        key_blk = lax.dynamic_slice_in_dim(key_part, key_start, rows_blk, 1)
        value_blk = lax.dynamic_slice_in_dim(value_part, key_start, rows_blk, 1)
        bucket_blk = lax.dynamic_slice_in_dim(bucket_part, key_start, rows_blk, 1)

        def fold_compute(current):
            raw_scores, allowed, pos_hot = tile_scores(key_blk, bucket_blk, key_start)
            weights = jnp.where(allowed, jax.nn.silu(raw_scores) / length, 0.0).astype(jnp.bfloat16)
            return current + jnp.einsum(
                "shij,sjhd->sihd", weights, value_blk, preferred_element_type=jnp.float32
            )

        return (
            lax.cond(key_start <= query_last, fold_compute, lambda current: current, carried),
            None,
        )

    running, _ = lax.scan(fold_step, running, jnp.arange(span // rows_blk, dtype=jnp.int32))
    attended = running
    attended = attended.reshape(tokens, D)
    hat_two, inverse_two = standardize(attended)
    normed_two = hat_two * small_float[2] + small_float[3]
    gated = (normed_two * gate_u).astype(jnp.bfloat16)
    result = embedded + jnp.dot(gated, copy_out, preferred_element_type=jnp.float32)
    layer_out = result.astype(jnp.bfloat16).reshape(seq_count, group, D)
    cotangent = out_grad.reshape(tokens, D)
    grad_out_weight = jnp.einsum("td,te->de", gated, cotangent, preferred_element_type=jnp.float32)
    grad_gated = jnp.einsum("te,de->td", cotangent, copy_out, preferred_element_type=jnp.float32)
    grad_u = grad_gated * normed_two
    grad_norm_two = grad_gated * gate_u
    grad_gain_two = jnp.sum(grad_norm_two * hat_two, axis=0)
    grad_shift_two = jnp.sum(grad_norm_two, axis=0)
    grad_attended = norm_back(grad_norm_two * small_float[2], hat_two, inverse_two).astype(
        jnp.bfloat16
    )
    grad_attended = grad_attended.reshape(seq_count, group, H, HEAD)
    key_whole, value_whole, bucket_whole = (
        lax.all_gather(keys_own, "blk", axis=1, tiled=True),
        lax.all_gather(values, "blk", axis=1, tiled=True),
        lax.all_gather(pos_sent, "blk", axis=1, tiled=True),
    )
    rows_back = math.gcd(length, 512)

    def back_step(carried, block_idx):
        grad_query, grad_pos, grad_qbias = carried
        key_start = block_idx * rows_back
        key_blk = lax.dynamic_slice_in_dim(key_whole, key_start, rows_back, 1)
        value_blk = lax.dynamic_slice_in_dim(value_whole, key_start, rows_back, 1)
        bucket_blk = lax.dynamic_slice_in_dim(bucket_whole, key_start, rows_back, 1)

        def back_compute(operand):
            raw_scores, allowed, pos_hot = tile_scores(key_blk, bucket_blk, key_start)
            grad_weights = jnp.einsum(
                "sihd,sjhd->shij", grad_attended, value_blk, preferred_element_type=jnp.float32
            )
            grad_raw = jnp.where(
                allowed, grad_weights / length * silu_slope(raw_scores), 0.0
            ).astype(jnp.bfloat16)
            grad_raw_float = grad_raw.astype(jnp.float32)
            part_query = (
                jnp.einsum("shij,sjhd->sihd", grad_raw, key_blk, preferred_element_type=jnp.float32)
                * scale
            )
            part_pos = jnp.einsum("shj,sjb->hb", jnp.sum(grad_raw_float, axis=2), pos_hot)
            part_qbias = jnp.sum(grad_raw_float, axis=3)
            weights = jnp.where(allowed, jax.nn.silu(raw_scores) / length, 0.0).astype(jnp.bfloat16)
            part_key = (
                jnp.einsum("shij,sihd->sjhd", grad_raw, queries, preferred_element_type=jnp.float32)
                * scale
            )
            part_value = jnp.einsum(
                "shij,sihd->sjhd", weights, grad_attended, preferred_element_type=jnp.float32
            )
            paired = jnp.concatenate(
                [
                    part_key.reshape(seq_count, rows_back, D),
                    part_value.reshape(seq_count, rows_back, D),
                ],
                axis=-1,
            )
            return (part_query, part_pos, part_qbias, paired)

        def skip_tile(operand):
            empty = (
                jnp.zeros((seq_count, group, H, HEAD), jnp.float32),
                jnp.zeros((H, NB), jnp.float32),
                jnp.zeros((seq_count, H, group), jnp.float32),
            )
            return empty + (jnp.zeros((seq_count, rows_back, 2 * D), jnp.float32),)

        parts = lax.cond(key_start <= query_last, back_compute, skip_tile, 0)
        summed = (grad_query + parts[0], grad_pos + parts[1], grad_qbias + parts[2])
        return (summed, parts[3])

    back_init = (
        jnp.zeros((seq_count, group, H, HEAD), jnp.float32),
        jnp.zeros((H, NB), jnp.float32),
        jnp.zeros((seq_count, H, group), jnp.float32),
    )
    (grad_query, grad_pos_table, grad_qbias), stacked = lax.scan(
        back_step, back_init, jnp.arange(length // rows_back, dtype=jnp.int32)
    )
    kv_terms = stacked.transpose(1, 0, 2, 3).reshape(seq_count, length, 2 * D)
    kv_own = lax.psum_scatter(kv_terms, "blk", scatter_dimension=1, tiled=True)
    grad_key = kv_own[:, :, :D].reshape(tokens, D)
    grad_value = kv_own[:, :, D:].reshape(tokens, D)
    grad_time_table = jnp.einsum("shc,scb->hb", grad_qbias, time_hot)
    grad_acts = jnp.concatenate(
        [grad_u, grad_value, grad_query.reshape(tokens, D), grad_key], axis=-1
    )
    grad_pre = (grad_acts * silu_slope(projected)).astype(jnp.bfloat16)
    grad_in_weight = jnp.einsum("td,tf->df", normed, grad_pre, preferred_element_type=jnp.float32)
    grad_normed = jnp.einsum("tf,df->td", grad_pre, copy_in, preferred_element_type=jnp.float32)
    grad_gain_one = jnp.sum(grad_normed * hat_one, axis=0)
    grad_shift_one = jnp.sum(grad_normed, axis=0)
    grad_embed = cotangent.astype(jnp.float32) + norm_back(
        grad_normed * small_float[0], hat_one, inverse_one
    )
    input_grad = grad_embed.reshape(seq_count, group, D)
    grad_small = jnp.stack(
        [
            grad_gain_one,
            grad_shift_one,
            grad_gain_two,
            grad_shift_two,
            grad_pos_table.reshape(D),
            grad_time_table.reshape(D),
        ]
    )
    counts_local = jnp.sum(
        (flat_ids[:, None] == jnp.arange(items, dtype=jnp.int32)[None, :]).astype(jnp.float32),
        axis=0,
    )
    shard_in, shard_out, shard_small, item_counts = (
        lax.psum_scatter(grad_in_weight, ("blk", "dp"), scatter_dimension=0, tiled=True),
        lax.psum_scatter(grad_out_weight, ("blk", "dp"), scatter_dimension=0, tiled=True),
        lax.psum_scatter(grad_small, ("blk", "dp"), scatter_dimension=1, tiled=True),
        lax.psum_scatter(counts_local, ("blk", "dp"), scatter_dimension=0, tiled=True),
    )
    grad_rounded = grad_embed.astype(jnp.bfloat16)
    hot = (
        flat_ids[:, None]
        == jnp.arange(items // devices * lax.axis_size(("blk", "dp")), dtype=jnp.int32)[None, :]
    ).astype(jnp.bfloat16)
    table_grad = lax.psum_scatter(
        jnp.einsum("tr,td->rd", hot, grad_rounded, preferred_element_type=jnp.float32),
        ("blk", "dp"),
        scatter_dimension=0,
        tiled=True,
    )
    log_q = jnp.log(jnp.maximum(item_counts, 1.0) / (seq_count * lax.axis_size("dp") * length))
    new_moment_in, new_second_in, new_proj_in = adam_update(
        proj_in, shard_in, moment_in, second_in, rate_in
    )
    new_moment_out, new_second_out, new_proj_out = adam_update(
        proj_out, shard_out, moment_out, second_out, rate_out
    )
    new_moment_small, new_second_small, new_small = adam_update(
        small_params, shard_small, moment_small, second_small, rate_small
    )
    return (
        layer_out,
        input_grad,
        table_grad,
        item_counts,
        log_q,
        new_moment_in,
        new_second_in,
        new_proj_in,
        new_moment_out,
        new_second_out,
        new_proj_out,
        new_moment_small,
        new_second_small,
        new_small,
    )


MESH = pl.DeviceIdType.MESH
F32, BF16, I32 = jnp.float32, jnp.bfloat16, jnp.int32
LANES = 128
NN = (((1,), (0,)), ((), ()))
NT = (((1,), (1,)), ((), ()))
TN = (((0,), (0,)), ((), ()))


def mm(lhs, rhs, dims=NN):
    return lax.dot_general(lhs, rhs, dims, preferred_element_type=F32)


def iota(shape, dim):
    return lax.broadcasted_iota(I32, shape, dim)


def at(index, size):
    return pl.ds(pl.multiple_of(index * size, size), size)


def fused_kernel(sizes, *refs):
    nb, nz, group, items, weight_rows, tokens = sizes
    nd = nz * 2
    length = nb * group
    part = D // nb
    rows_table = items // (nb * nd)
    (
        ids_in, pos_in, time_in, table_in, proj_in, proj_out, small_in, out_grad_in,
        layer_out, input_out, table_out, grad_in_out, grad_out_out, little_out,
        send, recv, local,
        index, own_index, column, own_column, padded, table, weight, weight_send, outw,
        small, small_all, cot,
        embedded, normed, projected, gate, value, query, key, attended,
        grad_gated, stats, fix, gated_send, gated_got, grad_att, dq, dk, dv,
        grad_pre, part_send, part_core, part_x, part_got, stats_one, ig_send, ig_got,
        bias_sum, gain_sum, table_acc,
        table_sum, table_core, table_z, table_got,
        gi_sum, gi_core, gi_z, gi_got,
        go_sum, go_core, go_z, go_got,
        little, little_parts, little_all, little_got,
    ) = refs
    b = lax.axis_index("blk")
    d = lax.axis_index("dp")
    y, x, z, core = b // 2, b % 2, d // 2, d % 2
    other, off_y, off_x = 1 - core, 1 - y, 1 - x
    v = core * 2 + x
    home = core == y
    away = core != y

    counter = [0]

    def slots(count):
        base = counter[0]
        counter[0] += count
        return base

    def copy(src, dst, slot, target, landing=None):
        return pltpu.make_async_remote_copy(
            src_ref=src, dst_ref=dst, send_sem=send.at[slot],
            recv_sem=recv.at[slot if landing is None else landing],
            device_id={"blk": target[0], "dp": target[1]}, device_id_type=MESH,
        )

    def blk_peer(k):
        return (lax.rem(b + k, nb), d)

    def blk_from(k):
        return lax.rem(b + nb - k, nb)

    def z_to(k):
        return lax.rem(z + k, nz)

    def z_from(k):
        return lax.rem(z + nz - k, nz)

    def z_peer(k):
        return (b, z_to(k) * 2 + core)

    core_peer = (b, z * 2 + other)
    x_peer, y_peer = (y * 2 + off_x, d), (off_y * 2 + x, d)
    partner = (off_y * 2 + x, z * 2 + other)

    def row_peer(k):
        w = lax.rem(v + k, nb)
        return w, (y * 2 + w % 2, z * 2 + w // 2)

    def row_from(k):
        return lax.rem(v + nb - k, nb)

    pending = []

    def push(src, dst, slot, target, landing=None, where=None):
        def start():
            copy(src, dst, slot, target, landing).start()

        if where is None:
            start()
        else:
            pl.when(where)(start)
        pending.append((where, src, dst, slot, target))

    near = (z + 1 - 2 * (z % 2), 2 - z // 2, 3 * (1 - z // 2))
    steps = [(kr, kz) for kz in range(nz) for kr in range(nb) if kr + kz > 0]

    def slab(kr, kz):
        w, at_z = lax.rem(v + kr, nb), z_to(kz)
        return w, at_z, (y * 2 + w % 2, at_z * 2 + w // 2)

    def slab_from(kr, kz):
        return row_from(kr), z_from(kz)

    def arrive(dst, slot, where=None):
        wait = copy(dst, dst, slot, core_peer).wait_recv
        if where is None:
            wait()
        else:
            pl.when(where)(wait)

    table_load = pltpu.make_async_copy(table_in, table.at[d], local.at[0])
    table_load.start()
    cot_load = pltpu.make_async_copy(out_grad_in, cot.at[b], local.at[1])
    pl.when(home)(cot_load.start)
    own_index[...] = jnp.concatenate(
        [ids_in[...], pos_in[...], time_in[...], jnp.zeros((5, group), I32)], axis=0
    )

    @pl.when(home)
    def keep_index():
        index[b] = own_index[...]

    own_rows = proj_in[...].astype(BF16)
    for q in range(nb):
        weight_send[q] = jnp.concatenate(
            [own_rows[:, s * D + q * part : s * D + (q + 1) * part] for s in range(4)], axis=1
        )
    weight[y, x, z, core] = weight_send[v]
    outw[b, d] = proj_out[...].astype(BF16)
    width = small_in.shape[1]
    spread = (iota((width, LANES), 1) == iota((width, LANES), 0) + d * width).astype(F32)
    small_pad = jnp.concatenate([small_in[...], jnp.zeros((10, width), F32)], axis=0)
    small[y, x, z, core] = mm(small_pad.astype(BF16), spread.astype(BF16)).astype(BF16)

    barrier = pltpu.get_barrier_semaphore()
    peers = [slab(*k)[2] for k in steps]
    peers += [(off_y * 2 + x, z_to(kz) * 2 + c) for kz in range(nz) for c in range(2)]
    peers += [(off_y * 2 + off_x, z * 2 + c) for c in range(2)]
    for target in peers:
        pl.semaphore_signal(
            barrier, inc=1, device_id={"blk": target[0], "dp": target[1]}, device_id_type=MESH
        )
    pl.semaphore_wait(barrier, len(peers))

    table_load.wait()
    s_tz, s_tx, s_tc = slots(nz), slots(nz * nb), slots(nz * nb)
    for n in range(nz - 1):
        push(table.at[d, b], table.at[d, b], s_tz + n, (b, near[n] * 2 + core), s_tz + z)
    push(table.at[d], table.at[d], s_tc, core_peer, s_tc + z * nb)
    s_index, s_w, s_s = slots(nb), slots(nb * nz), slots(nb * nz)
    for k in range(nb):
        to = (core * 2 + (x + k % 2) % 2, z * 2 + (core + k // 2) % 2)
        push(own_index, index.at[b], s_index + k, to, s_index + b, away if k == 0 else None)
    for kr, kz in steps:
        w, at_z, to = slab(kr, kz)
        push(small.at[y, x, z, core], small.at[y, x, z, core], s_s + kz * nb + kr, to)
    for kr, kz in steps:
        w, at_z, to = slab(kr, kz)
        push(weight_send.at[w], weight.at[y, x, z, core], s_w + kz * nb + kr, to)
    s_g = slots(8)
    halves = (slice(0, group // 2), slice(group // 2, group))
    v_x, v_core, v_cross = core * 2 + off_x, other * 2 + x, other * 2 + off_x

    def cot_half(owner, n):
        return cot.at[owner, halves[n]]

    def cross_over():
        for n in range(2):
            push(out_grad_in.at[halves[n]], cot_half(b, n), s_g + n, partner, None, away)
        pl.when(home)(cot_load.wait)

    def own_half(n, where):
        push(cot_half(v, n), cot_half(v, n), s_g + 2 + n, x_peer, None, where)
        push(cot_half(v, n), cot_half(v, n), s_g + 4 + n, core_peer, None, where)

    def pass_on(n):
        arrive(cot_half(v_x, n), s_g + 2 + n)
        push(cot_half(v_x, n), cot_half(v_x, n), s_g + 6 + n, core_peer)

    s_wc, s_oz = slots(3 * nz), slots(nz)
    sides, opposite, second = (y, y, core), (off_y, off_y, other), (y_peer, y_peer, core_peer)

    def shard_of(n, side, at_z):
        if n == 2:
            return outw.at[b, at_z * 2 + side]
        return (weight, small)[n].at[side, :, at_z]

    def shard_next(n, kz):
        at_z = z_from(kz)
        if n == 2 and kz > 0:
            arrive(outw.at[b, at_z * 2 + core], s_oz + kz)
        for kr in range(nb):
            if n < 2 and kr + kz > 0:
                w = row_from(kr)
                arrive((weight, small)[n].at[y, w % 2, at_z, w // 2], (s_w, s_s)[n] + kz * nb + kr)
        ref = shard_of(n, sides[n], at_z)
        push(ref, ref, s_wc + n * nz + kz, second[n])

    def shards_end(n):
        for kz in range(nz):
            arrive(shard_of(n, opposite[n], z_from(kz)), s_wc + n * nz + kz)

    for i in range(nb):
        arrive(index.at[i], s_index + i, jnp.logical_or(away, b != i))
    padded[...] = jnp.zeros(padded.shape, F32)

    def to_column(e, carry):
        padded[0:8, :] = index[e].astype(F32)
        column[at(e, group), :] = jnp.transpose(padded[...]).astype(I32)
        return carry

    lax.fori_loop(0, nb, to_column, 0)
    padded[0:8, :] = own_index[...].astype(F32)
    own_column[...] = jnp.transpose(padded[...]).astype(I32)

    step = 256

    def table_over_z(n):
        shard = near[n] * 2 + core
        arrive(table.at[shard, b], s_tz + near[n])
        for m in range(1, nb):
            push(
                table.at[shard, b], table.at[shard, b], s_tx + n * nb + m, blk_peer(m),
                s_tx + near[n] * nb + m,
            )
        push(
            table.at[shard, b], table.at[shard, b], s_tc + (n + 1) * nb, core_peer,
            s_tc + near[n] * nb,
        )

    def table_over_blk(n):
        shard = near[n] * 2 + core
        for m in range(1, nb):
            quarter = table.at[shard, blk_from(m)]
            arrive(quarter, s_tx + near[n] * nb + m)
            push(quarter, quarter, s_tc + (n + 1) * nb + m, core_peer, s_tc + near[n] * nb + m)

    def table_over_core(n):
        shard = near[n] * 2 + other
        arrive(table.at[shard, b], s_tc + near[n] * nb)
        for m in range(1, nb):
            arrive(table.at[shard, blk_from(m)], s_tc + near[n] * nb + m)

    def picked_rows(rows, at_z, step=step):
        picked = column[rows, 0:1] - at_z * (items // nz)
        hot = jnp.where(iota((step, items // nz), 1) == picked, 1.0, 0.0).astype(BF16)
        return mm(hot, table[pl.ds(at_z * 2, 2)].reshape(items // nz, D)).astype(BF16)

    def look_up(at_z, first):
        def body(t, carry):
            rows = at(t, group)
            found = picked_rows(rows, at_z, group)
            embedded[rows, :] = found if first else embedded[rows, :] + found
            return carry

        lax.fori_loop(0, nb, body, 0)

    table_over_z(0)
    table_over_z(1)
    arrive(table.at[z * 2 + other], s_tc + z * nb)
    look_up(z, True)
    table_over_z(2)
    for k in range(1, nz):
        push(outw.at[b, d], outw.at[b, d], s_oz + k, z_peer(k))
    for kz in range(nz):
        shard_next(1, kz)
    shard_next(0, 0)
    shard_next(0, 1)
    table_over_blk(0)
    table_over_blk(1)
    shard_next(0, 3)
    shard_next(0, 2)
    cross_over()
    table_over_core(0)
    look_up(near[0], False)
    own_half(0, home)
    own_half(1, home)
    table_over_blk(2)
    table_over_core(1)
    look_up(near[1], False)
    for kz in range(nz):
        shard_next(2, kz)
    table_over_core(2)
    shards_end(0)
    shards_end(1)

    lane = iota((1, LANES), 1)
    for q in range(nb):
        total = sum(small[q // 2, q % 2, r // 2, r % 2].astype(F32) for r in range(nd))
        small_all[q] = total
    gain_one = jnp.concatenate([small_all[q][0:1] for q in range(nb)], axis=1)
    shift_one = jnp.concatenate([small_all[q][1:2] for q in range(nb)], axis=1)
    mine = small_all[v]
    gain_one_own = mine[0:1]
    gain_two, shift_two = mine[2:3], mine[3:4]
    pos_row, time_row = mine[4:5], mine[5:6]
    low = lane < NB
    pos_rows = (0.5 * pltpu.roll(pos_row, NB, 1), 0.5 * pos_row)
    time_rows = (0.5 * time_row, 0.5 * pltpu.roll(time_row, NB, 1))
    masks = (low, lane >= NB)

    def embed(t, carry):
        rows = at(t, group)
        found = embedded[rows, :] + picked_rows(rows, near[2], group)
        embedded[rows, :] = found
        found = found.astype(F32)
        mean = jnp.mean(found, axis=1, keepdims=True)
        centered = found - mean
        inverse = lax.rsqrt(jnp.mean(centered * centered, axis=1, keepdims=True) + norm_eps)
        fix[rows, :] = jnp.where(lane == 0, mean, inverse)
        ready = (centered * inverse * gain_one + shift_one).astype(BF16)
        normed[rows, :] = ready
        raw = mm(ready, weight[...].reshape(D, 4 * part))
        projected[rows, :] = raw
        act = raw * (0.5 + 0.5 * jnp.tanh(0.5 * raw))
        gate[rows, :] = act[:, 0:part]
        value[rows, :] = act[:, part : 2 * part].astype(BF16)
        queries = act[:, 2 * part : 3 * part].astype(BF16).astype(F32) * (0.5 * HEAD**-0.5)
        keys = act[:, 3 * part :].astype(BF16)
        time_hot = jnp.where(lane == column[rows, 2:3], 1.0, 0.0)
        pos_hot = jnp.where(lane == column[rows, 1:2] + NB, 1.0, 0.0)
        for h in range(2):
            query[h, rows, 0:LANES] = jnp.where(masks[h], queries, 0.0).astype(BF16)
            query[h, rows, LANES:] = jnp.where(low, time_hot, pos_rows[h]).astype(BF16)
            key[h, rows, 0:LANES] = keys
            key[h, rows, LANES:] = jnp.where(low, time_rows[h], pos_hot).astype(BF16)
        return carry

    lax.fori_loop(0, nb // 2, embed, 0)
    shards_end(2)
    s_oy, s_ox = slots(1), slots(2)
    push(outw.at[b], outw.at[b], s_oy, y_peer)
    for n in range(2):
        arrive(cot_half(v, n), s_g + n, away)
        own_half(n, away)
    lax.fori_loop(nb // 2, nb, embed, 0)

    s_st = slots(nb * nb)
    inv_length = 1.0 / length

    def forward(r, carry):
        i = nb - 1 - r
        rows = at(i, group)
        dq[...] = jnp.zeros(dq.shape, F32)

        def tile(j, masked):
            cols = at(j, group)
            for h in range(2):
                x = mm(query[h, rows, :], key[h, cols, :], NT)
                w = x + x * jnp.tanh(x)
                if masked:
                    w = jnp.where(iota(w.shape, 0) >= iota(w.shape, 1), w, 0.0)
                dq[h, :, 0:LANES] += mm(w.astype(BF16), value[cols, :])

        def full(j, inner):
            tile(j, False)
            return inner

        lax.fori_loop(0, i, full, 0)
        tile(i, True)
        att = jnp.where(low, dq[0, :, 0:LANES], dq[1, :, 0:LANES]) * inv_length
        attended[rows, :] = att

        @pl.when(r == 1)
        def cotangents():
            pass_on(0)
            pass_on(1)

        return carry

    lax.fori_loop(0, nb, forward, 0)
    arrive(outw.at[off_y * 2 + x], s_oy)
    out_rows = outw[v].reshape(part, D)
    for n in range(2):
        arrive(cot_half(v_core, n), s_g + 4 + n)
        arrive(cot_half(v_cross, n), s_g + 6 + n)

    def statistics(r, carry):
        i = nb - 1 - r
        rows = at(i, group)
        att = attended[rows, :]
        gg = mm(cot[i], out_rows, NT)
        grad_gated[rows, :] = gg
        g = gg * gate[rows, :] * gain_two
        mean = jnp.mean(att, axis=1, keepdims=True)
        centered = att - mean
        square = jnp.sum(centered * centered, axis=1, keepdims=True)
        sum_g = jnp.sum(g, axis=1, keepdims=True)
        sum_ga = jnp.sum(g * centered, axis=1, keepdims=True)
        packed = jnp.where(
            lane == 0, mean, jnp.where(lane == 1, square, jnp.where(lane == 2, sum_g, sum_ga))
        )
        packed = jnp.transpose(packed)
        stats[v, i] = jnp.concatenate(
            [packed[0:4, 0 : group // 2], packed[0:4, group // 2 :]], axis=0
        )
        for k in range(1, nb):
            copy(stats.at[v, i], stats.at[v, i], s_st + i * nb + k, row_peer(k)[1]).start()
        return carry

    lax.fori_loop(0, nb, statistics, 0)

    push(outw.at[v], outw.at[v], s_ox, x_peer)

    s_pc, s_px, s_s1, s_gt = slots(nb), slots(nb), slots(nb * nb), slots(nb)
    dk[...] = jnp.zeros(dk.shape, F32)
    dv[...] = jnp.zeros(dv.shape, F32)
    bias_sum[...] = jnp.zeros(bias_sum.shape, F32)
    gain_sum[...] = jnp.zeros(gain_sum.shape, F32)

    def backward(r, carry):
        i = nb - 1 - r
        rows = at(i, group)
        for k in range(1, nb):
            arrive(stats.at[row_from(k), i], s_st + i * nb + k)
        every = [jnp.concatenate([stats[q, i, 0:4], stats[q, i, 4:8]], axis=1) for q in range(nb)]
        mean = sum(s[0:1] for s in every) * (1.0 / nb)
        square = sum(s[1:2] + part * (s[0:1] - mean) * (s[0:1] - mean) for s in every)
        inverse = lax.rsqrt(square * (1.0 / D) + norm_eps)
        mean_g = sum(s[2:3] for s in every) * (1.0 / D)
        cross = inverse * sum(s[3:4] + (s[0:1] - mean) * s[2:3] for s in every) * (1.0 / D)
        padded[0:1, :] = mean
        padded[1:2, :] = inverse
        padded[2:3, :] = mean_g
        padded[3:4, :] = cross
        turned = jnp.transpose(padded[...])
        inverse = turned[:, 1:2]
        hat = (attended[rows, :] - turned[:, 0:1]) * inverse
        normal = hat * gain_two + shift_two
        gated_send[i] = (normal * gate[rows, :]).astype(BF16)

        @pl.when(jnp.logical_or(away, i != b))
        def send_gated():
            copy(gated_send.at[i], gated_got.at[v], s_gt + i, (i, z * 2 + y), s_gt + v).start()

        @pl.when(jnp.logical_and(home, i == b))
        def keep_gated():
            gated_got[v] = gated_send[i]

        gg = grad_gated[rows, :]
        grad_u = gg * normal
        grad_norm = gg * gate[rows, :]
        gain_sum[2:3, :] += jnp.sum(grad_norm * hat, axis=0, keepdims=True)
        gain_sum[3:4, :] += jnp.sum(grad_norm, axis=0, keepdims=True)
        ga = (grad_norm * gain_two - turned[:, 2:3] - hat * turned[:, 3:4]) * inverse
        for h in range(2):
            grad_att[h] = jnp.where(masks[h], ga, 0.0).astype(BF16)
        dq[...] = jnp.zeros(dq.shape, F32)

        def tile(j, masked):
            cols = at(j, group)
            for h in range(2):
                x = mm(key[h, cols, :], query[h, rows, :], NT)
                t = jnp.tanh(x)
                u = 1.0 + t
                w = x * u
                slope = u + w * (1.0 - t)
                if masked:
                    allowed = iota(w.shape, 0) <= iota(w.shape, 1)
                    w = jnp.where(allowed, w, 0.0)
                    slope = jnp.where(allowed, slope, 0.0)
                dw = mm(value[cols, :], grad_att[h], NT)
                graw = (dw * slope).astype(BF16)
                dv[j] += mm(w.astype(BF16), grad_att[h])
                back = mm(graw, query[h, rows, :])
                dk[j] += back[:, 0:LANES]
                bias_sum[h : h + 1, :] += jnp.sum(back[:, LANES:], axis=0, keepdims=True)
                dq[h] += mm(graw, key[h, cols, :], TN)

        def full(j, inner):
            tile(j, False)
            return inner

        lax.fori_loop(0, i, full, 0)
        tile(i, True)
        for h in range(2):
            bias_sum[2 + h : 3 + h, :] += jnp.sum(dq[h, :, LANES:], axis=0, keepdims=True)
        grad_q = jnp.where(low, dq[0, :, 0:LANES], dq[1, :, 0:LANES]) * (
            0.5 * inv_length * HEAD**-0.5
        )
        raw = projected[rows, :]
        logistic = 0.5 + 0.5 * jnp.tanh(0.5 * raw)
        slope = logistic * (1.0 + raw * (1.0 - logistic))
        acts = jnp.concatenate([grad_u, dv[i] * inv_length, grad_q, dk[i] * inv_length], axis=1)
        pre = (acts * slope).astype(BF16)
        grad_pre[rows, :] = pre
        partial = mm(pre, weight[...].reshape(D, 4 * part), NT)
        scaled = partial * gain_one
        first = jnp.sum(scaled, axis=1, keepdims=True)
        mean_one, inverse_one = fix[rows, 0:1], fix[rows, 1:2]
        hat_one = (embedded[rows, :].astype(F32) - mean_one) * inverse_one
        second = jnp.sum(scaled * hat_one, axis=1, keepdims=True)
        turned = jnp.transpose(jnp.where(lane == 0, first, second))
        stats_one[v, i] = jnp.concatenate(
            [turned[n : n + 1, at_lane : at_lane + LANES] for n in range(2) for at_lane in range(0, group, LANES)],
            axis=0,
        )
        for q in range(nb):
            part_send[i, q] = partial[:, q * part : (q + 1) * part].astype(BF16)
        core_part(i).start()
        for k in range(1, nb):
            copy(stats_one.at[v, i], stats_one.at[v, i], s_s1 + i * nb + k, row_peer(k)[1]).start()

        @pl.when(r > 0)
        def previous():
            over_x(i + 1)

        return carry

    def core_part(i):
        half = part_send.at[i, pl.ds(other * 2, 2)]
        return copy(half, part_core.at[i], s_pc + i, core_peer)

    def x_part(i):
        return copy(part_x.at[i], part_got.at[i], s_px + i, x_peer)

    def over_x(i):
        core_part(i).wait_recv()
        both = part_send[i, v_x].astype(F32) + part_core[i, off_x].astype(F32)
        part_x[i] = both.astype(BF16)
        x_part(i).start()

    lax.fori_loop(0, nb, backward, 0)
    over_x(0)
    arrive(outw.at[v_x], s_ox)
    push(outw.at[v_x], outw.at[v_x], s_ox + 1, core_peer)

    def gi_half(side, k):
        return gi_sum.at[side, :, k]

    def table_half(side, k):
        return table_sum.at[side, :, k]

    def go_half(side, k):
        return go_sum.at[k, side]

    order = (near[2], near[1], near[0], z)

    def y_stage(half, landing, base):
        for n, k in enumerate(order):
            push(half(off_y, k), landing.at[k], base + n, y_peer)

    def y_sum(half, landing, outgoing, base, n):
        k = order[n]
        arrive(landing.at[k], base + n)
        outgoing[k] = (half(y, k)[...].astype(F32) + landing[k].astype(F32)).astype(BF16)

    def owner_stage(outgoing, landing, base, n):
        k = order[n]
        for w in range(nb):
            to = (y * 2 + w % 2, k * 2 + w // 2)
            own = n == nz - 1
            push(
                outgoing.at[k, w % 2, w // 2], landing.at[v, z], base + n * nb + w, to,
                base + z * nb + v, v != w if own else None,
            )
        if own:
            landing[v, z] = outgoing[z, x, core]

    def owner_sum(landing, base, result):
        for n, k in enumerate(order):
            for w in range(nb):
                arrive(landing.at[w, k], base + k * nb + w, v != w if n == nz - 1 else None)
        for q in range(nb):
            result[q] = sum(landing[q, k].astype(F32) for k in range(nz))

    s_gic, s_gio = slots(nz), slots(nz * nb)
    s_goc, s_goz = slots(nz), slots(nz)

    gated_all = gated_send[...].reshape(length, part)
    go_sum[...] = mm(gated_all, cot[...].reshape(length, D), TN).astype(BF16).reshape(go_sum.shape)
    y_stage(go_half, go_core, s_goc)

    def weight_grad(t, carry):
        cols = at(t, LANES)
        got = mm(normed[:, cols], grad_pre[...], TN).astype(BF16)
        gi_sum[t // 2, t % 2] = got.reshape(gi_sum.shape[2:])
        return carry

    lax.fori_loop(0, nb, weight_grad, 0)
    y_stage(gi_half, gi_core, s_gic)

    s_ig = slots(nb)

    def input_part(r, carry):
        i = nb - 1 - r
        rows = at(i, group)
        x_part(i).wait_recv()
        for k in range(1, nb):
            arrive(stats_one.at[row_from(k), i], s_s1 + i * nb + k)
        total = (
            part_send[i, v].astype(F32) + part_core[i, x].astype(F32) + part_got[i].astype(F32)
        )
        row = sum(stats_one[q, i] for q in range(nb)) * (1.0 / D)
        row = jnp.concatenate(
            [
                jnp.concatenate([row[n * 4 + m : n * 4 + m + 1] for m in range(4)], axis=1)
                for n in range(2)
            ],
            axis=0,
        )
        padded[0:2, :] = row
        turned = jnp.transpose(padded[...])
        mean_one, inverse_one = fix[rows, 0:1], fix[rows, 1:2]
        mycols = at(v, part)
        hat_one = (embedded[rows, mycols].astype(F32) - mean_one) * inverse_one
        gain_sum[0:1, :] += jnp.sum(total * hat_one, axis=0, keepdims=True)
        gain_sum[1:2, :] += jnp.sum(total, axis=0, keepdims=True)
        back = (total * gain_one_own - turned[:, 0:1] - hat_one * turned[:, 1:2]) * inverse_one
        ig_send[i] = (cot[i, :, mycols].astype(F32) + back).astype(BF16)
        return carry

    s_tgc, s_tgo = slots(nz), slots(nz * nb)

    def gi_over(n):
        y_sum(gi_half, gi_core, gi_z, s_gic, n)
        owner_stage(gi_z, gi_got, s_gio, n)

    def table_rows(i, t):
        hot = jnp.where(iota((group, group), 0) + t * group == index[i][0:1], 1.0, 0.0)
        return mm(hot.astype(BF16), ig_send[i])

    def table_add(i, first):
        def add(t, carry):
            rows = at(t, group)
            got = table_rows(i, t)
            table_acc[rows, :] = got if first else table_acc[rows, :] + got
            return carry

        lax.fori_loop(0, items // group, add, 0)

    def table_part(t, carry):
        got = (table_acc[at(t, group), :] + table_rows(0, t)).astype(BF16)
        table_sum[t // 2, t % 2] = got.reshape(table_sum.shape[2:])
        return carry

    for r in range(nb - 1):
        input_part(r, 0)
        table_add(nb - 1 - r, r == 0)
        if r == 1:
            gi_over(0)
            gi_over(1)
        if r == 2:
            gi_over(2)
    input_part(nb - 1, 0)
    lax.fori_loop(off_y * 2, off_y * 2 + 2, table_part, 0)
    y_stage(table_half, table_core, s_tgc)
    for k in range(nb):
        i = lax.rem(b + k, nb)
        push(ig_send.at[i], ig_got.at[v], s_ig + k, (i, z * 2 + y), s_ig + v, away if k == 0 else None)

    @pl.when(home)
    def keep_input():
        ig_got[v] = ig_send[b]

    lax.fori_loop(y * 2, y * 2 + 2, table_part, 0)
    gi_over(3)
    for n in range(nz):
        y_sum(go_half, go_core, go_z, s_goc, n)
    for k in range(nz):
        push(go_z.at[z_to(k)], go_got.at[z], s_goz + k, (v, z_to(k) * 2 + y), None, away if k == 0 else None)

    @pl.when(home)
    def keep_rows():
        go_got[z] = go_z[z]


    s_l, s_lx = slots(nd), slots(1)
    own_items = items // nb

    def count(t, carry):
        picked = column[at(t, step), 0:1]
        hit = jnp.where(iota((step, own_items), 1) + v * own_items == picked, 1.0, 0.0)
        return carry + jnp.sum(hit, axis=0, keepdims=True)

    counted = lax.fori_loop(0, length // step, count, jnp.zeros((1, own_items), F32))
    time_grad = jnp.where(low, bias_sum[0:1, :], pltpu.roll(bias_sum[1:2, :], NB, 1))
    pos_grad = jnp.where(low, pltpu.roll(bias_sum[2:3, :], NB, 1), bias_sum[3:4, :])
    halved = 0.5 * inv_length
    little[...] = jnp.zeros(little.shape, F32)
    little[0:4, :] = gain_sum[0:4, :]
    little[4:5, :] = pos_grad * halved
    little[5:6, :] = time_grad * halved
    for q in range(own_items // LANES):
        little[8 + q : 9 + q, :] = counted[:, q * LANES : (q + 1) * LANES]
    columns = [(ky, kz) for kz in range(nz) for ky in range(2) if ky + kz > 0]
    for ky, kz in columns:
        to = (lax.rem(y + ky, 2) * 2 + x, z_to(kz) * 2 + core)
        push(little, little_parts.at[kz * 2 + ky], s_l + kz * 2 + ky, to)
    def from_row(landing, base):
        for w in range(nb):
            arrive(landing.at[w], base + w, jnp.logical_or(away, v != w))

    from_row(gated_got, s_gt)
    arrive(outw.at[other * 2 + off_x], s_ox + 1)

    def finish_layer(t, carry):
        rows = at(t, step)
        hot = jnp.where(iota((step, items), 1) == own_column[rows, 0:1], 1.0, 0.0).astype(BF16)
        result = mm(hot, table[...].reshape(items, D))
        for q in range(nb):
            result = result + mm(gated_got[q, rows, :], outw[q].reshape(part, D))
        layer_out[rows, :] = result.astype(BF16)
        return carry

    lax.fori_loop(0, group // step, finish_layer, 0)

    for n in range(nz):
        y_sum(table_half, table_core, table_z, s_tgc, n)
        owner_stage(table_z, table_got, s_tgo, n)
    totals = little[...]
    for ky, kz in columns:
        arrive(little_parts.at[kz * 2 + ky], s_l + kz * 2 + ky)
        totals = totals + little_parts[kz * 2 + ky]
    little_all[...] = totals
    push(little_all, little_got, s_lx, core_peer)

    owner_sum(gi_got, s_gio, grad_in_out)
    for k in range(nz):
        arrive(go_got.at[z_from(k)], s_goz + k, away if k == 0 else None)
    grad_out_out[...] = sum(go_got[k].astype(F32) for k in range(nz))
    from_row(ig_got, s_ig)
    input_out[...] = ig_got[...]
    arrive(little_got, s_lx)

    @pl.when(home)
    def keep_own():
        little_out[...] = little_all[...]

    @pl.when(away)
    def take_peers():
        little_out[...] = little_got[...]

    owner_sum(table_got, s_tgo, table_out)

    for where, *sent in pending:
        if where is None:
            copy(*sent).wait_send()
        else:
            pl.when(where)(copy(*sent).wait_send)

    def drain(i, carry):
        for k in range(1, nb):
            to = row_peer(k)[1]
            copy(stats.at[v, i], stats.at[v, i], s_st + i * nb + k, to).wait_send()
            copy(stats_one.at[v, i], stats_one.at[v, i], s_s1 + i * nb + k, to).wait_send()
        core_part(i).wait_send()
        x_part(i).wait_send()
        sent_gated = copy(gated_send.at[i], gated_got.at[v], s_gt + i, (i, z * 2 + y), s_gt + v)
        pl.when(jnp.logical_or(away, i != b))(sent_gated.wait_send)
        return carry

    lax.fori_loop(0, nb, drain, 0)
    assert counter[0] <= send.shape[0], counter[0]


def finish_kernel(sizes, *refs):
    nb, nz, group, items, weight_rows, tokens = sizes
    part = D // nb
    rows_table = items // (nb * nz * 2)
    (
        layer_in, input_in, table_in, grad_in_in, grad_out_in, little_in,
        proj_in, proj_out, small_in,
        moment_in, second_in, moment_out, second_out, moment_small, second_small,
        layer_out, input_grad, table_grad, counts_out, logq_out,
        new_m_in, new_s_in, new_w_in, new_m_out, new_s_out, new_w_out,
        new_m_small, new_s_small, new_w_small,
    ) = refs
    d = lax.axis_index("dp")
    layer_out[...] = layer_in[...]
    for q in range(nb):
        cols = slice(q * part, (q + 1) * part)
        input_grad[:, cols] = input_in[q].astype(F32)
        table_grad[:, cols] = table_in[q]
        for s in range(4):
            own = slice(s * D + q * part, s * D + (q + 1) * part)
            new_m_in[:, own], new_s_in[:, own], new_w_in[:, own] = adam_update(
                proj_in[:, own], grad_in_in[q, :, s * part : (s + 1) * part],
                moment_in[:, own], second_in[:, own], rate_in,
            )
    new_m_out[...], new_s_out[...], new_w_out[...] = adam_update(
        proj_out[...], grad_out_in[...], moment_out[...], second_out[...], rate_out
    )
    width = small_in.shape[1]
    shifted = pltpu.roll(little_in[0:8, :], lax.rem(LANES - d * width, LANES), 1)[0:6, 0:width]
    new_m_small[...], new_s_small[...], new_w_small[...] = adam_update(
        small_in[...], shifted, moment_small[...], second_small[...], rate_small
    )
    per_row = LANES // rows_table
    count_row = little_in[pl.ds(8 + d // per_row, 1), :]
    count_row = pltpu.roll(
        jnp.broadcast_to(count_row, (8, LANES)),
        lax.rem(LANES - lax.rem(d, per_row) * rows_table, LANES), 1,
    )[0:1, 0:rows_table]
    counts_out[...] = count_row
    logq_out[...] = jnp.log(jnp.maximum(count_row, 1.0) * (1.0 / tokens))


def fused(sizes, args):
    nb, nz, group, items, weight_rows, tokens = sizes
    nd = nz * 2
    length = nb * group
    part = D // nb
    rows_table = items // (nb * nd)
    (
        item_ids, pos_buckets, time_buckets, item_table, proj_in, proj_out, small_params, out_grad,
        moment_in, second_in, moment_out, second_out, moment_small, second_small,
    ) = args
    width = small_params.shape[1]
    shape = jax.ShapeDtypeStruct
    middle = [
        shape((group, D), BF16), shape((nb, group, part), BF16), shape((nb, rows_table, part), F32),
        shape((nb, weight_rows, 4 * part), F32), shape((weight_rows, D), F32), shape((16, LANES), F32),
    ]
    outs = [
        shape((group, D), BF16), shape((group, D), F32), shape((rows_table, D), F32),
        shape((1, rows_table), F32), shape((1, rows_table), F32),
        *[shape(proj_in.shape, F32)] * 3, *[shape(proj_out.shape, F32)] * 3,
        *[shape(small_params.shape, F32)] * 3,
    ]
    vm = pltpu.VMEM
    scratch = [
        pltpu.SemaphoreType.DMA((256,)), pltpu.SemaphoreType.DMA((256,)), pltpu.SemaphoreType.DMA((2,)),
        vm((nb, 8, group), I32),
        vm((8, group), I32),
        vm((length, LANES), I32),
        vm((group, LANES), I32),
        vm((LANES, group), F32),
        vm((nd, nb, rows_table, D), BF16),
        vm((2, 2, nz, 2, weight_rows, 4 * part), BF16),
        vm((nb, weight_rows, 4 * part), BF16),
        vm((nb, nd, weight_rows, D), BF16),
        vm((2, 2, nz, 2, 16, LANES), BF16),
        vm((nb, 16, LANES), F32),
        vm((nb, group, D), BF16),
        vm((length, D), BF16),
        vm((length, D), BF16),
        vm((length, 4 * part), F32),
        vm((length, part), F32),
        vm((length, part), BF16),
        vm((2, length, 2 * LANES), BF16),
        vm((2, length, 2 * LANES), BF16),
        vm((length, part), F32),
        vm((length, part), F32),
        vm((nb, nb, 8, group // 2), F32),
        vm((length, LANES), F32),
        vm((nb, group, part), BF16),
        vm((nb, group, part), BF16),
        vm((2, group, part), BF16),
        vm((2, group, 2 * LANES), F32),
        vm((nb, group, part), F32),
        vm((nb, group, part), F32),
        vm((length, 4 * part), BF16),
        vm((nb, nb, group, part), BF16),
        vm((nb, 2, group, part), BF16),
        vm((nb, group, part), BF16),
        vm((nb, group, part), BF16),
        vm((nb, nb, 8, LANES), F32),
        vm((nb, group, part), BF16),
        vm((nb, group, part), BF16),
        vm((8, LANES), F32),
        vm((8, LANES), F32),
        vm((items, part), F32),
        vm((2, 2, nz, 2, rows_table, part), BF16),
        *[vm((nz, 2, 2, rows_table, part), BF16)] * 2,
        vm((nb, nz, rows_table, part), BF16),
        vm((2, 2, nz, 2, weight_rows, 4 * part), BF16),
        *[vm((nz, 2, 2, weight_rows, 4 * part), BF16)] * 2,
        vm((nb, nz, weight_rows, 4 * part), BF16),
        vm((nz, 2, weight_rows, D), BF16),
        *[vm((nz, weight_rows, D), BF16)] * 3,
        vm((16, LANES), F32),
        vm((nd, 16, LANES), F32),
        *[vm((16, LANES), F32)] * 2,
    ]
    whole, far = pl.BlockSpec(memory_space=pltpu.VMEM), pl.BlockSpec(memory_space=pl.ANY)
    between = pl.pallas_call(
        functools.partial(fused_kernel, sizes),
        out_shape=middle,
        in_specs=[whole] * 3 + [far] + [whole] * 3 + [far],
        out_specs=[whole] * len(middle),
        scratch_shapes=scratch,
        compiler_params=pltpu.CompilerParams(
            collective_id=0, has_side_effects=True, vmem_limit_bytes=60 * 2**20
        ),
        name="hstu_step",
    )(
        item_ids, pos_buckets, time_buckets,
        item_table.reshape(nb, item_table.shape[0] // nb, D),
        proj_in, proj_out, small_params, out_grad.reshape(group, D),
    )
    got = pl.pallas_call(
        functools.partial(finish_kernel, sizes),
        out_shape=outs,
        in_specs=[whole] * (len(middle) + 9),
        out_specs=[whole] * len(outs),
        name="hstu_finish",
    )(
        *between, proj_in, proj_out, small_params,
        moment_in, second_in, moment_out, second_out, moment_small, second_small,
    )
    return (
        got[0].reshape(out_grad.shape), got[1].reshape(out_grad.shape), got[2],
        got[3].reshape(rows_table), got[4].reshape(rows_table), *got[5:],
    )


def per_device(*args):
    item_ids, item_table, proj_in, small_params = args[0], args[3], args[4], args[6]
    seq_count, group = item_ids.shape
    nb, nd = lax.axis_size("blk"), lax.axis_size("dp")
    items = item_table.shape[0] * nd
    by_heads = (
        seq_count == 1 and nd % 2 == 0 and D // nb == LANES and group % 256 == 0
        and items == 2048 and proj_in.shape[0] % 16 == 0
        and small_params.shape[1] * nd == LANES and nb == 4 and nd == 8
    )
    if by_heads:
        sizes = (nb, nd // 2, group, items, proj_in.shape[0], nd * nb * group)
        return fused(sizes, args)
    return by_events(*args)


def solution(mesh):
    placed = (
        P("dp", "blk"),
        P("dp", "blk"),
        P("dp", "blk"),
        P("dp", None),
        P(("blk", "dp"), None),
        P(("blk", "dp"), None),
        P(None, ("blk", "dp")),
        P("dp", "blk", None),
        P(("blk", "dp"), None),
        P(("blk", "dp"), None),
        P(("blk", "dp"), None),
        P(("blk", "dp"), None),
        P(None, ("blk", "dp")),
        P(None, ("blk", "dp")),
    )
    return jax.shard_map(
        per_device,
        mesh=mesh,
        in_specs=placed,
        out_specs=(
            P("dp", "blk", None),
            P("dp", "blk", None),
            P(("blk", "dp"), None),
            P(("blk", "dp")),
            P(("blk", "dp")),
            P(("blk", "dp"), None),
            P(("blk", "dp"), None),
            P(("blk", "dp"), None),
            P(("blk", "dp"), None),
            P(("blk", "dp"), None),
            P(("blk", "dp"), None),
            P(None, ("blk", "dp")),
            P(None, ("blk", "dp")),
            P(None, ("blk", "dp")),
        ),
        check_vma=False,
    )
```

```python
import functools
import math

import jax
import jax.numpy as jnp
from jax import lax
from jax.experimental import pallas as pl
from jax.experimental.pallas import tpu as pltpu
from jax.sharding import PartitionSpec as P

D = 512
H = 8
HEAD = 64
NB = 64


norm_eps = 1e-05
beta_first = 0.5
beta_second = 0.5
adam_eps = 1e-08
weight_decay = 0.01
rate_in = 0.05
rate_out = 0.06
rate_small = 0.3
step_number = 3


def standardize(values):
    centered = values - jnp.mean(values, axis=-1, keepdims=True)
    inverse = lax.rsqrt(jnp.mean(centered * centered, axis=-1, keepdims=True) + norm_eps)
    return (centered * inverse, inverse)


def norm_back(grad_hat, normal_hat, inverse):
    mean_grad = jnp.mean(grad_hat, axis=-1, keepdims=True)
    mean_cross = jnp.mean(grad_hat * normal_hat, axis=-1, keepdims=True)
    return (grad_hat - mean_grad - normal_hat * mean_cross) * inverse


def silu_slope(values):
    logistic = jax.nn.sigmoid(values)
    return logistic * (1.0 + values * (1.0 - logistic))


def adam_update(weight, grad, moment, second, rate):
    new_moment = beta_first * moment + (1.0 - beta_first) * grad
    new_second = beta_second * second + (1.0 - beta_second) * grad * grad
    moment_hat = new_moment / (1.0 - beta_first**step_number)
    second_hat = new_second / (1.0 - beta_second**step_number)
    new_weight = weight - rate * (
        moment_hat / (jnp.sqrt(second_hat) + adam_eps) + weight_decay * weight
    )
    return (new_moment, new_second, new_weight)


def by_events(
    item_ids,
    pos_buckets,
    time_buckets,
    item_table,
    proj_in,
    proj_out,
    small_params,
    out_grad,
    moment_in,
    second_in,
    moment_out,
    second_out,
    moment_small,
    second_small,
):
    seq_count, group = item_ids.shape
    length = group * lax.axis_size("blk")
    devices = lax.axis_size("blk") * lax.axis_size("dp")
    items = item_table.shape[0] * lax.axis_size("dp")
    tokens = seq_count * group
    scale = HEAD ** (-0.5)
    copy_in, copy_out, copy_small = (
        lax.all_gather(proj_in.astype(jnp.bfloat16), ("blk", "dp"), axis=0, tiled=True),
        lax.all_gather(proj_out.astype(jnp.bfloat16), ("blk", "dp"), axis=0, tiled=True),
        lax.all_gather(small_params.astype(jnp.bfloat16), ("blk", "dp"), axis=1, tiled=True),
    )
    small_float = copy_small.astype(jnp.float32)
    flat_ids = item_ids.reshape(tokens)
    portion = lax.all_gather(item_table, "dp", axis=0, tiled=True)
    hot = (flat_ids[:, None] == jnp.arange(portion.shape[0], dtype=jnp.int32)[None, :]).astype(
        jnp.bfloat16
    )
    embedded = jnp.dot(hot, portion, preferred_element_type=jnp.float32)
    hat_one, inverse_one = standardize(embedded)
    normed = (hat_one * small_float[0] + small_float[1]).astype(jnp.bfloat16)
    projected = jnp.dot(normed, copy_in, preferred_element_type=jnp.float32)
    activated = jax.nn.silu(projected)
    gate_u = activated[:, :D]
    rounded = activated[:, D:].astype(jnp.bfloat16)
    values = rounded[:, :D].reshape(seq_count, group, H, HEAD)
    queries = rounded[:, D : 2 * D].reshape(seq_count, group, H, HEAD)
    keys_own = rounded[:, 2 * D :].reshape(seq_count, group, H, HEAD)
    pos_table = small_float[4].reshape(H, NB)
    time_table = small_float[5].reshape(H, NB)
    buckets = jnp.arange(NB, dtype=jnp.int32)
    time_hot = (time_buckets[:, :, None] == buckets).astype(jnp.float32)
    query_bias = jnp.einsum("scb,hb->shc", time_hot, time_table)
    query_first = lax.axis_index("blk") * group
    query_pos = query_first + jnp.arange(group, dtype=jnp.int32)
    query_last = query_first + group - 1
    pos_sent = pos_buckets.astype(jnp.bfloat16)

    def tile_scores(key_blk, bucket_blk, key_start):
        pos_hot = (bucket_blk.astype(jnp.int32)[:, :, None] == buckets).astype(jnp.float32)
        key_bias = jnp.einsum("sjb,hb->shj", pos_hot, pos_table)
        raw_scores = (
            jnp.einsum("sihd,sjhd->shij", queries, key_blk, preferred_element_type=jnp.float32)
            * scale
        )
        raw_scores = raw_scores + query_bias[:, :, :, None] + key_bias[:, :, None, :]
        key_pos = key_start + jnp.arange(key_blk.shape[1], dtype=jnp.int32)
        allowed = (query_pos[:, None] >= key_pos[None, :])[None, None]
        return (raw_scores, allowed, pos_hot)

    attend_init = jnp.zeros((seq_count, group, H, HEAD), jnp.float32)
    running = attend_init
    key_part = lax.all_gather(keys_own, "blk", axis=1, tiled=True)
    value_part = lax.all_gather(values, "blk", axis=1, tiled=True)
    bucket_part = lax.all_gather(pos_sent, "blk", axis=1, tiled=True)
    span = key_part.shape[1]
    rows_blk = math.gcd(span, 512)

    def fold_step(carried, block_idx):
        key_start = block_idx * rows_blk
        key_blk = lax.dynamic_slice_in_dim(key_part, key_start, rows_blk, 1)
        value_blk = lax.dynamic_slice_in_dim(value_part, key_start, rows_blk, 1)
        bucket_blk = lax.dynamic_slice_in_dim(bucket_part, key_start, rows_blk, 1)

        def fold_compute(current):
            raw_scores, allowed, pos_hot = tile_scores(key_blk, bucket_blk, key_start)
            weights = jnp.where(allowed, jax.nn.silu(raw_scores) / length, 0.0).astype(jnp.bfloat16)
            return current + jnp.einsum(
                "shij,sjhd->sihd", weights, value_blk, preferred_element_type=jnp.float32
            )

        return (
            lax.cond(key_start <= query_last, fold_compute, lambda current: current, carried),
            None,
        )

    running, _ = lax.scan(fold_step, running, jnp.arange(span // rows_blk, dtype=jnp.int32))
    attended = running
    attended = attended.reshape(tokens, D)
    hat_two, inverse_two = standardize(attended)
    normed_two = hat_two * small_float[2] + small_float[3]
    gated = (normed_two * gate_u).astype(jnp.bfloat16)
    result = embedded + jnp.dot(gated, copy_out, preferred_element_type=jnp.float32)
    layer_out = result.astype(jnp.bfloat16).reshape(seq_count, group, D)
    cotangent = out_grad.reshape(tokens, D)
    grad_out_weight = jnp.einsum("td,te->de", gated, cotangent, preferred_element_type=jnp.float32)
    grad_gated = jnp.einsum("te,de->td", cotangent, copy_out, preferred_element_type=jnp.float32)
    grad_u = grad_gated * normed_two
    grad_norm_two = grad_gated * gate_u
    grad_gain_two = jnp.sum(grad_norm_two * hat_two, axis=0)
    grad_shift_two = jnp.sum(grad_norm_two, axis=0)
    grad_attended = norm_back(grad_norm_two * small_float[2], hat_two, inverse_two).astype(
        jnp.bfloat16
    )
    grad_attended = grad_attended.reshape(seq_count, group, H, HEAD)
    key_whole, value_whole, bucket_whole = (
        lax.all_gather(keys_own, "blk", axis=1, tiled=True),
        lax.all_gather(values, "blk", axis=1, tiled=True),
        lax.all_gather(pos_sent, "blk", axis=1, tiled=True),
    )
    rows_back = math.gcd(length, 512)

    def back_step(carried, block_idx):
        grad_query, grad_pos, grad_qbias = carried
        key_start = block_idx * rows_back
        key_blk = lax.dynamic_slice_in_dim(key_whole, key_start, rows_back, 1)
        value_blk = lax.dynamic_slice_in_dim(value_whole, key_start, rows_back, 1)
        bucket_blk = lax.dynamic_slice_in_dim(bucket_whole, key_start, rows_back, 1)

        def back_compute(operand):
            raw_scores, allowed, pos_hot = tile_scores(key_blk, bucket_blk, key_start)
            grad_weights = jnp.einsum(
                "sihd,sjhd->shij", grad_attended, value_blk, preferred_element_type=jnp.float32
            )
            grad_raw = jnp.where(
                allowed, grad_weights / length * silu_slope(raw_scores), 0.0
            ).astype(jnp.bfloat16)
            grad_raw_float = grad_raw.astype(jnp.float32)
            part_query = (
                jnp.einsum("shij,sjhd->sihd", grad_raw, key_blk, preferred_element_type=jnp.float32)
                * scale
            )
            part_pos = jnp.einsum("shj,sjb->hb", jnp.sum(grad_raw_float, axis=2), pos_hot)
            part_qbias = jnp.sum(grad_raw_float, axis=3)
            weights = jnp.where(allowed, jax.nn.silu(raw_scores) / length, 0.0).astype(jnp.bfloat16)
            part_key = (
                jnp.einsum("shij,sihd->sjhd", grad_raw, queries, preferred_element_type=jnp.float32)
                * scale
            )
            part_value = jnp.einsum(
                "shij,sihd->sjhd", weights, grad_attended, preferred_element_type=jnp.float32
            )
            paired = jnp.concatenate(
                [
                    part_key.reshape(seq_count, rows_back, D),
                    part_value.reshape(seq_count, rows_back, D),
                ],
                axis=-1,
            )
            return (part_query, part_pos, part_qbias, paired)

        def skip_tile(operand):
            empty = (
                jnp.zeros((seq_count, group, H, HEAD), jnp.float32),
                jnp.zeros((H, NB), jnp.float32),
                jnp.zeros((seq_count, H, group), jnp.float32),
            )
            return empty + (jnp.zeros((seq_count, rows_back, 2 * D), jnp.float32),)

        parts = lax.cond(key_start <= query_last, back_compute, skip_tile, 0)
        summed = (grad_query + parts[0], grad_pos + parts[1], grad_qbias + parts[2])
        return (summed, parts[3])

    back_init = (
        jnp.zeros((seq_count, group, H, HEAD), jnp.float32),
        jnp.zeros((H, NB), jnp.float32),
        jnp.zeros((seq_count, H, group), jnp.float32),
    )
    (grad_query, grad_pos_table, grad_qbias), stacked = lax.scan(
        back_step, back_init, jnp.arange(length // rows_back, dtype=jnp.int32)
    )
    kv_terms = stacked.transpose(1, 0, 2, 3).reshape(seq_count, length, 2 * D)
    kv_own = lax.psum_scatter(kv_terms, "blk", scatter_dimension=1, tiled=True)
    grad_key = kv_own[:, :, :D].reshape(tokens, D)
    grad_value = kv_own[:, :, D:].reshape(tokens, D)
    grad_time_table = jnp.einsum("shc,scb->hb", grad_qbias, time_hot)
    grad_acts = jnp.concatenate(
        [grad_u, grad_value, grad_query.reshape(tokens, D), grad_key], axis=-1
    )
    grad_pre = (grad_acts * silu_slope(projected)).astype(jnp.bfloat16)
    grad_in_weight = jnp.einsum("td,tf->df", normed, grad_pre, preferred_element_type=jnp.float32)
    grad_normed = jnp.einsum("tf,df->td", grad_pre, copy_in, preferred_element_type=jnp.float32)
    grad_gain_one = jnp.sum(grad_normed * hat_one, axis=0)
    grad_shift_one = jnp.sum(grad_normed, axis=0)
    grad_embed = cotangent.astype(jnp.float32) + norm_back(
        grad_normed * small_float[0], hat_one, inverse_one
    )
    input_grad = grad_embed.reshape(seq_count, group, D)
    grad_small = jnp.stack(
        [
            grad_gain_one,
            grad_shift_one,
            grad_gain_two,
            grad_shift_two,
            grad_pos_table.reshape(D),
            grad_time_table.reshape(D),
        ]
    )
    counts_local = jnp.sum(
        (flat_ids[:, None] == jnp.arange(items, dtype=jnp.int32)[None, :]).astype(jnp.float32),
        axis=0,
    )
    shard_in, shard_out, shard_small, item_counts = (
        lax.psum_scatter(grad_in_weight, ("blk", "dp"), scatter_dimension=0, tiled=True),
        lax.psum_scatter(grad_out_weight, ("blk", "dp"), scatter_dimension=0, tiled=True),
        lax.psum_scatter(grad_small, ("blk", "dp"), scatter_dimension=1, tiled=True),
        lax.psum_scatter(counts_local, ("blk", "dp"), scatter_dimension=0, tiled=True),
    )
    grad_rounded = grad_embed.astype(jnp.bfloat16)
    hot = (
        flat_ids[:, None]
        == jnp.arange(items // devices * lax.axis_size(("blk", "dp")), dtype=jnp.int32)[None, :]
    ).astype(jnp.bfloat16)
    table_grad = lax.psum_scatter(
        jnp.einsum("tr,td->rd", hot, grad_rounded, preferred_element_type=jnp.float32),
        ("blk", "dp"),
        scatter_dimension=0,
        tiled=True,
    )
    log_q = jnp.log(jnp.maximum(item_counts, 1.0) / (seq_count * lax.axis_size("dp") * length))
    new_moment_in, new_second_in, new_proj_in = adam_update(
        proj_in, shard_in, moment_in, second_in, rate_in
    )
    new_moment_out, new_second_out, new_proj_out = adam_update(
        proj_out, shard_out, moment_out, second_out, rate_out
    )
    new_moment_small, new_second_small, new_small = adam_update(
        small_params, shard_small, moment_small, second_small, rate_small
    )
    return (
        layer_out,
        input_grad,
        table_grad,
        item_counts,
        log_q,
        new_moment_in,
        new_second_in,
        new_proj_in,
        new_moment_out,
        new_second_out,
        new_proj_out,
        new_moment_small,
        new_second_small,
        new_small,
    )


MESH = pl.DeviceIdType.MESH
F32, BF16, I32 = jnp.float32, jnp.bfloat16, jnp.int32
LANES = 128
NN = (((1,), (0,)), ((), ()))
NT = (((1,), (1,)), ((), ()))
TN = (((0,), (0,)), ((), ()))


def mm(lhs, rhs, dims=NN):
    return lax.dot_general(lhs, rhs, dims, preferred_element_type=F32)


def iota(shape, dim):
    return lax.broadcasted_iota(I32, shape, dim)


def at(index, size):
    return pl.ds(pl.multiple_of(index * size, size), size)


def fused_kernel(sizes, *refs):
    nb, nz, group, items, weight_rows, tokens = sizes
    nd = nz * 2
    length = nb * group
    part = D // nb
    rows_table = items // (nb * nd)
    (
        ids_in, pos_in, time_in, table_in, proj_in, proj_out, small_in, out_grad_in,
        layer_out, input_out, table_out, grad_in_out, grad_out_out, little_out,
        send, recv, local,
        index, own_index, column, own_column, padded, table, weight, weight_send, outw,
        small, small_all, cot,
        embedded, normed, projected, gate, value, query, key, attended,
        grad_gated, stats, fix, gated_send, gated_got, grad_att, dq, dk, dv,
        grad_pre, part_send, part_core, part_x, part_got, stats_one, ig_send, ig_got,
        bias_sum, gain_sum, table_acc,
        table_sum, table_core, table_z, table_got,
        gi_sum, gi_core, gi_z, gi_got,
        go_sum, go_core, go_z, go_got,
        little, little_parts, little_all, little_got,
    ) = refs
    b = lax.axis_index("blk")
    d = lax.axis_index("dp")
    y, x, z, core = b // 2, b % 2, d // 2, d % 2
    other, off_y, off_x = 1 - core, 1 - y, 1 - x
    v = core * 2 + x
    home = core == y
    away = core != y

    counter = [0]

    def slots(count):
        base = counter[0]
        counter[0] += count
        return base

    def copy(src, dst, slot, target, landing=None):
        return pltpu.make_async_remote_copy(
            src_ref=src, dst_ref=dst, send_sem=send.at[slot],
            recv_sem=recv.at[slot if landing is None else landing],
            device_id={"blk": target[0], "dp": target[1]}, device_id_type=MESH,
        )

    def blk_peer(k):
        return (lax.rem(b + k, nb), d)

    def blk_from(k):
        return lax.rem(b + nb - k, nb)

    def z_to(k):
        return lax.rem(z + k, nz)

    def z_from(k):
        return lax.rem(z + nz - k, nz)

    def z_peer(k):
        return (b, z_to(k) * 2 + core)

    core_peer = (b, z * 2 + other)
    x_peer, y_peer = (y * 2 + off_x, d), (off_y * 2 + x, d)
    partner = (off_y * 2 + x, z * 2 + other)

    def row_peer(k):
        w = lax.rem(v + k, nb)
        return w, (y * 2 + w % 2, z * 2 + w // 2)

    def row_from(k):
        return lax.rem(v + nb - k, nb)

    pending = []

    def push(src, dst, slot, target, landing=None, where=None):
        def start():
            copy(src, dst, slot, target, landing).start()

        if where is None:
            start()
        else:
            pl.when(where)(start)
        pending.append((where, src, dst, slot, target))

    near = (z + 1 - 2 * (z % 2), 2 - z // 2, 3 * (1 - z // 2))
    steps = [(kr, kz) for kz in range(nz) for kr in range(nb) if kr + kz > 0]

    def slab(kr, kz):
        w, at_z = lax.rem(v + kr, nb), z_to(kz)
        return w, at_z, (y * 2 + w % 2, at_z * 2 + w // 2)

    def slab_from(kr, kz):
        return row_from(kr), z_from(kz)

    def arrive(dst, slot, where=None):
        wait = copy(dst, dst, slot, core_peer).wait_recv
        if where is None:
            wait()
        else:
            pl.when(where)(wait)

    table_load = pltpu.make_async_copy(table_in, table.at[d], local.at[0])
    table_load.start()
    cot_load = pltpu.make_async_copy(out_grad_in, cot.at[b], local.at[1])
    pl.when(home)(cot_load.start)
    own_index[...] = jnp.concatenate(
        [ids_in[...], pos_in[...], time_in[...], jnp.zeros((5, group), I32)], axis=0
    )

    @pl.when(home)
    def keep_index():
        index[b] = own_index[...]

    own_rows = proj_in[...].astype(BF16)
    for q in range(nb):
        weight_send[q] = jnp.concatenate(
            [own_rows[:, s * D + q * part : s * D + (q + 1) * part] for s in range(4)], axis=1
        )
    weight[y, x, z, core] = weight_send[v]
    outw[b, d] = proj_out[...].astype(BF16)
    width = small_in.shape[1]
    spread = (iota((width, LANES), 1) == iota((width, LANES), 0) + d * width).astype(F32)
    small_pad = jnp.concatenate([small_in[...], jnp.zeros((10, width), F32)], axis=0)
    small[y, x, z, core] = mm(small_pad.astype(BF16), spread.astype(BF16)).astype(BF16)

    barrier = pltpu.get_barrier_semaphore()
    peers = [slab(*k)[2] for k in steps]
    peers += [(off_y * 2 + x, z_to(kz) * 2 + c) for kz in range(nz) for c in range(2)]
    peers += [(off_y * 2 + off_x, z * 2 + c) for c in range(2)]
    for target in peers:
        pl.semaphore_signal(
            barrier, inc=1, device_id={"blk": target[0], "dp": target[1]}, device_id_type=MESH
        )
    pl.semaphore_wait(barrier, len(peers))

    table_load.wait()
    s_tz, s_tx, s_tc = slots(nz), slots(nz * nb), slots(nz * nb)
    for n in range(nz - 1):
        push(table.at[d, b], table.at[d, b], s_tz + n, (b, near[n] * 2 + core), s_tz + z)
    push(table.at[d], table.at[d], s_tc, core_peer, s_tc + z * nb)
    s_index, s_w, s_s = slots(nb), slots(nb * nz), slots(nb * nz)
    for k in range(nb):
        to = (core * 2 + (x + k % 2) % 2, z * 2 + (core + k // 2) % 2)
        push(own_index, index.at[b], s_index + k, to, s_index + b, away if k == 0 else None)
    for kr, kz in steps:
        w, at_z, to = slab(kr, kz)
        push(small.at[y, x, z, core], small.at[y, x, z, core], s_s + kz * nb + kr, to)
    for kr, kz in steps:
        w, at_z, to = slab(kr, kz)
        push(weight_send.at[w], weight.at[y, x, z, core], s_w + kz * nb + kr, to)
    s_g = slots(8)
    halves = (slice(0, group // 2), slice(group // 2, group))
    v_x, v_core, v_cross = core * 2 + off_x, other * 2 + x, other * 2 + off_x

    def cot_half(owner, n):
        return cot.at[owner, halves[n]]

    def cross_over():
        for n in range(2):
            push(out_grad_in.at[halves[n]], cot_half(b, n), s_g + n, partner, None, away)
        pl.when(home)(cot_load.wait)

    def own_half(n, where):
        push(cot_half(v, n), cot_half(v, n), s_g + 2 + n, x_peer, None, where)
        push(cot_half(v, n), cot_half(v, n), s_g + 4 + n, core_peer, None, where)

    def pass_on(n):
        arrive(cot_half(v_x, n), s_g + 2 + n)
        push(cot_half(v_x, n), cot_half(v_x, n), s_g + 6 + n, core_peer)

    s_wc, s_oz = slots(3 * nz), slots(nz)
    sides, opposite, second = (y, y, core), (off_y, off_y, other), (y_peer, y_peer, core_peer)

    def shard_of(n, side, at_z):
        if n == 2:
            return outw.at[b, at_z * 2 + side]
        return (weight, small)[n].at[side, :, at_z]

    def shard_next(n, kz):
        at_z = z_from(kz)
        if n == 2 and kz > 0:
            arrive(outw.at[b, at_z * 2 + core], s_oz + kz)
        for kr in range(nb):
            if n < 2 and kr + kz > 0:
                w = row_from(kr)
                arrive((weight, small)[n].at[y, w % 2, at_z, w // 2], (s_w, s_s)[n] + kz * nb + kr)
        ref = shard_of(n, sides[n], at_z)
        push(ref, ref, s_wc + n * nz + kz, second[n])

    def shards_end(n):
        for kz in range(nz):
            arrive(shard_of(n, opposite[n], z_from(kz)), s_wc + n * nz + kz)

    for i in range(nb):
        arrive(index.at[i], s_index + i, jnp.logical_or(away, b != i))
    padded[...] = jnp.zeros(padded.shape, F32)

    def to_column(e, carry):
        padded[0:8, :] = index[e].astype(F32)
        column[at(e, group), :] = jnp.transpose(padded[...]).astype(I32)
        return carry

    lax.fori_loop(0, nb, to_column, 0)
    padded[0:8, :] = own_index[...].astype(F32)
    own_column[...] = jnp.transpose(padded[...]).astype(I32)

    step = 256

    def table_over_z(n):
        shard = near[n] * 2 + core
        arrive(table.at[shard, b], s_tz + near[n])
        for m in range(1, nb):
            push(
                table.at[shard, b], table.at[shard, b], s_tx + n * nb + m, blk_peer(m),
                s_tx + near[n] * nb + m,
            )
        push(
            table.at[shard, b], table.at[shard, b], s_tc + (n + 1) * nb, core_peer,
            s_tc + near[n] * nb,
        )

    def table_over_blk(n):
        shard = near[n] * 2 + core
        for m in range(1, nb):
            quarter = table.at[shard, blk_from(m)]
            arrive(quarter, s_tx + near[n] * nb + m)
            push(quarter, quarter, s_tc + (n + 1) * nb + m, core_peer, s_tc + near[n] * nb + m)

    def table_over_core(n):
        shard = near[n] * 2 + other
        arrive(table.at[shard, b], s_tc + near[n] * nb)
        for m in range(1, nb):
            arrive(table.at[shard, blk_from(m)], s_tc + near[n] * nb + m)

    def picked_rows(rows, at_z, step=step):
        picked = column[rows, 0:1] - at_z * (items // nz)
        hot = jnp.where(iota((step, items // nz), 1) == picked, 1.0, 0.0).astype(BF16)
        return mm(hot, table[pl.ds(at_z * 2, 2)].reshape(items // nz, D)).astype(BF16)

    def look_up(at_z, first):
        def body(t, carry):
            rows = at(t, 2 * group)
            found = picked_rows(rows, at_z, 2 * group)
            embedded[rows, :] = found if first else embedded[rows, :] + found
            return carry

        lax.fori_loop(0, nb // 2, body, 0)

    table_over_z(0)
    table_over_z(1)
    arrive(table.at[z * 2 + other], s_tc + z * nb)
    look_up(z, True)
    table_over_z(2)
    for k in range(1, nz):
        push(outw.at[b, d], outw.at[b, d], s_oz + k, z_peer(k))
    for kz in range(nz):
        shard_next(1, kz)
    shard_next(0, 0)
    shard_next(0, 1)
    table_over_blk(0)
    table_over_blk(1)
    shard_next(0, 3)
    shard_next(0, 2)
    cross_over()
    table_over_core(0)
    look_up(near[0], False)
    own_half(0, home)
    own_half(1, home)
    table_over_blk(2)
    table_over_core(1)
    look_up(near[1], False)
    for kz in range(nz):
        shard_next(2, kz)
    table_over_core(2)
    shards_end(0)
    shards_end(1)

    lane = iota((1, LANES), 1)
    for q in range(nb):
        total = sum(small[q // 2, q % 2, r // 2, r % 2].astype(F32) for r in range(nd))
        small_all[q] = total
    gain_one = jnp.concatenate([small_all[q][0:1] for q in range(nb)], axis=1)
    shift_one = jnp.concatenate([small_all[q][1:2] for q in range(nb)], axis=1)
    mine = small_all[v]
    gain_one_own = mine[0:1]
    gain_two, shift_two = mine[2:3], mine[3:4]
    pos_row, time_row = mine[4:5], mine[5:6]
    low = lane < NB
    pos_rows = (0.5 * pltpu.roll(pos_row, NB, 1), 0.5 * pos_row)
    time_rows = (0.5 * time_row, 0.5 * pltpu.roll(time_row, NB, 1))
    masks = (low, lane >= NB)

    def embed(t, carry):
        rows = at(t, group)
        found = embedded[rows, :] + picked_rows(rows, near[2], group)
        embedded[rows, :] = found
        found = found.astype(F32)
        mean = jnp.mean(found, axis=1, keepdims=True)
        centered = found - mean
        inverse = lax.rsqrt(jnp.mean(centered * centered, axis=1, keepdims=True) + norm_eps)
        fix[rows, :] = jnp.where(lane == 0, mean, inverse)
        ready = (centered * inverse * gain_one + shift_one).astype(BF16)
        normed[rows, :] = ready
        raw = mm(ready, weight[...].reshape(D, 4 * part))
        projected[rows, :] = raw
        act = raw * (0.5 + 0.5 * jnp.tanh(0.5 * raw))
        gate[rows, :] = act[:, 0:part]
        value[rows, :] = act[:, part : 2 * part].astype(BF16)
        queries = act[:, 2 * part : 3 * part].astype(BF16).astype(F32) * (0.5 * HEAD**-0.5)
        keys = act[:, 3 * part :].astype(BF16)
        time_hot = jnp.where(lane == column[rows, 2:3], 1.0, 0.0)
        pos_hot = jnp.where(lane == column[rows, 1:2] + NB, 1.0, 0.0)
        for h in range(2):
            query[h, rows, 0:LANES] = jnp.where(masks[h], queries, 0.0).astype(BF16)
            query[h, rows, LANES:] = jnp.where(low, time_hot, pos_rows[h]).astype(BF16)
            key[h, rows, 0:LANES] = keys
            key[h, rows, LANES:] = jnp.where(low, time_rows[h], pos_hot).astype(BF16)
        return carry

    lax.fori_loop(0, nb // 2, embed, 0)
    shards_end(2)
    s_oy, s_ox = slots(1), slots(2)
    push(outw.at[b], outw.at[b], s_oy, y_peer)
    for n in range(2):
        arrive(cot_half(v, n), s_g + n, away)
        own_half(n, away)
    lax.fori_loop(nb // 2, nb, embed, 0)

    s_st = slots(nb * nb)
    inv_length = 1.0 / length

    def forward(r, carry):
        i = nb - 1 - r
        rows = at(i, group)
        dq[...] = jnp.zeros(dq.shape, F32)

        def tile(j, masked):
            cols = at(j, group)
            for h in range(2):
                x = mm(query[h, rows, :], key[h, cols, :], NT)
                w = x + x * jnp.tanh(x)
                if masked:
                    w = jnp.where(iota(w.shape, 0) >= iota(w.shape, 1), w, 0.0)
                dq[h, :, 0:LANES] += mm(w.astype(BF16), value[cols, :])

        def full(j, inner):
            tile(j, False)
            return inner

        lax.fori_loop(0, i, full, 0)
        tile(i, True)
        att = jnp.where(low, dq[0, :, 0:LANES], dq[1, :, 0:LANES]) * inv_length
        attended[rows, :] = att

        @pl.when(r == 1)
        def cotangents():
            pass_on(0)
            pass_on(1)

        return carry

    lax.fori_loop(0, nb, forward, 0)
    arrive(outw.at[off_y * 2 + x], s_oy)
    out_rows = outw[v].reshape(part, D)
    for n in range(2):
        arrive(cot_half(v_core, n), s_g + 4 + n)
        arrive(cot_half(v_cross, n), s_g + 6 + n)

    def statistics(r, carry):
        i = nb - 1 - r
        rows = at(i, group)
        att = attended[rows, :]
        gg = mm(cot[i], out_rows, NT)
        grad_gated[rows, :] = gg
        g = gg * gate[rows, :] * gain_two
        mean = jnp.mean(att, axis=1, keepdims=True)
        centered = att - mean
        square = jnp.sum(centered * centered, axis=1, keepdims=True)
        sum_g = jnp.sum(g, axis=1, keepdims=True)
        sum_ga = jnp.sum(g * centered, axis=1, keepdims=True)
        packed = jnp.where(
            lane == 0, mean, jnp.where(lane == 1, square, jnp.where(lane == 2, sum_g, sum_ga))
        )
        packed = jnp.transpose(packed)
        stats[v, i] = jnp.concatenate(
            [packed[0:4, 0 : group // 2], packed[0:4, group // 2 :]], axis=0
        )
        for k in range(1, nb):
            copy(stats.at[v, i], stats.at[v, i], s_st + i * nb + k, row_peer(k)[1]).start()
        return carry

    lax.fori_loop(0, nb, statistics, 0)

    push(outw.at[v], outw.at[v], s_ox, x_peer)

    s_pc, s_px, s_s1, s_gt = slots(nb), slots(nb), slots(nb * nb), slots(nb)
    dk[...] = jnp.zeros(dk.shape, F32)
    dv[...] = jnp.zeros(dv.shape, F32)
    bias_sum[...] = jnp.zeros(bias_sum.shape, F32)
    gain_sum[...] = jnp.zeros(gain_sum.shape, F32)

    def backward(r, carry):
        i = nb - 1 - r
        rows = at(i, group)
        for k in range(1, nb):
            arrive(stats.at[row_from(k), i], s_st + i * nb + k)
        every = [jnp.concatenate([stats[q, i, 0:4], stats[q, i, 4:8]], axis=1) for q in range(nb)]
        mean = sum(s[0:1] for s in every) * (1.0 / nb)
        square = sum(s[1:2] + part * (s[0:1] - mean) * (s[0:1] - mean) for s in every)
        inverse = lax.rsqrt(square * (1.0 / D) + norm_eps)
        mean_g = sum(s[2:3] for s in every) * (1.0 / D)
        cross = inverse * sum(s[3:4] + (s[0:1] - mean) * s[2:3] for s in every) * (1.0 / D)
        padded[0:1, :] = mean
        padded[1:2, :] = inverse
        padded[2:3, :] = mean_g
        padded[3:4, :] = cross
        turned = jnp.transpose(padded[...])
        inverse = turned[:, 1:2]
        hat = (attended[rows, :] - turned[:, 0:1]) * inverse
        normal = hat * gain_two + shift_two
        gated_send[i] = (normal * gate[rows, :]).astype(BF16)

        @pl.when(jnp.logical_or(away, i != b))
        def send_gated():
            copy(gated_send.at[i], gated_got.at[v], s_gt + i, (i, z * 2 + y), s_gt + v).start()

        @pl.when(jnp.logical_and(home, i == b))
        def keep_gated():
            gated_got[v] = gated_send[i]

        gg = grad_gated[rows, :]
        grad_u = gg * normal
        grad_norm = gg * gate[rows, :]
        gain_sum[2:3, :] += jnp.sum(grad_norm * hat, axis=0, keepdims=True)
        gain_sum[3:4, :] += jnp.sum(grad_norm, axis=0, keepdims=True)
        ga = (grad_norm * gain_two - turned[:, 2:3] - hat * turned[:, 3:4]) * inverse
        for h in range(2):
            grad_att[h] = jnp.where(masks[h], ga, 0.0).astype(BF16)
        dq[...] = jnp.zeros(dq.shape, F32)

        def tile(j, masked):
            cols = at(j, group)
            for h in range(2):
                x = mm(key[h, cols, :], query[h, rows, :], NT)
                t = jnp.tanh(x)
                u = 1.0 + t
                w = x * u
                slope = u + w * (1.0 - t)
                if masked:
                    allowed = iota(w.shape, 0) <= iota(w.shape, 1)
                    w = jnp.where(allowed, w, 0.0)
                    slope = jnp.where(allowed, slope, 0.0)
                dw = mm(value[cols, :], grad_att[h], NT)
                graw = (dw * slope).astype(BF16)
                dv[j] += mm(w.astype(BF16), grad_att[h])
                back = mm(graw, query[h, rows, :])
                dk[j] += back[:, 0:LANES]
                bias_sum[h : h + 1, :] += jnp.sum(back[:, LANES:], axis=0, keepdims=True)
                dq[h] += mm(graw, key[h, cols, :], TN)

        def full(j, inner):
            tile(j, False)
            return inner

        lax.fori_loop(0, i, full, 0)
        tile(i, True)
        for h in range(2):
            bias_sum[2 + h : 3 + h, :] += jnp.sum(dq[h, :, LANES:], axis=0, keepdims=True)
        grad_q = jnp.where(low, dq[0, :, 0:LANES], dq[1, :, 0:LANES]) * (
            0.5 * inv_length * HEAD**-0.5
        )
        raw = projected[rows, :]
        logistic = 0.5 + 0.5 * jnp.tanh(0.5 * raw)
        slope = logistic * (1.0 + raw * (1.0 - logistic))
        acts = jnp.concatenate([grad_u, dv[i] * inv_length, grad_q, dk[i] * inv_length], axis=1)
        pre = (acts * slope).astype(BF16)
        grad_pre[rows, :] = pre
        partial = mm(pre, weight[...].reshape(D, 4 * part), NT)
        scaled = partial * gain_one
        first = jnp.sum(scaled, axis=1, keepdims=True)
        mean_one, inverse_one = fix[rows, 0:1], fix[rows, 1:2]
        hat_one = (embedded[rows, :].astype(F32) - mean_one) * inverse_one
        second = jnp.sum(scaled * hat_one, axis=1, keepdims=True)
        turned = jnp.transpose(jnp.where(lane == 0, first, second))
        stats_one[v, i] = jnp.concatenate(
            [turned[n : n + 1, at_lane : at_lane + LANES] for n in range(2) for at_lane in range(0, group, LANES)],
            axis=0,
        )
        for q in range(nb):
            part_send[i, q] = partial[:, q * part : (q + 1) * part].astype(BF16)
        core_part(i).start()
        for k in range(1, nb):
            copy(stats_one.at[v, i], stats_one.at[v, i], s_s1 + i * nb + k, row_peer(k)[1]).start()

        @pl.when(r > 0)
        def previous():
            over_x(i + 1)

        return carry

    def core_part(i):
        half = part_send.at[i, pl.ds(other * 2, 2)]
        return copy(half, part_core.at[i], s_pc + i, core_peer)

    def x_part(i):
        return copy(part_x.at[i], part_got.at[i], s_px + i, x_peer)

    def over_x(i):
        core_part(i).wait_recv()
        both = part_send[i, v_x].astype(F32) + part_core[i, off_x].astype(F32)
        part_x[i] = both.astype(BF16)
        x_part(i).start()

    lax.fori_loop(0, nb, backward, 0)
    over_x(0)
    arrive(outw.at[v_x], s_ox)
    push(outw.at[v_x], outw.at[v_x], s_ox + 1, core_peer)

    def gi_half(side, k):
        return gi_sum.at[side, :, k]

    def table_half(side, k):
        return table_sum.at[side, :, k]

    def go_half(side, k):
        return go_sum.at[k, side]

    order = (near[2], near[1], near[0], z)

    def y_stage(half, landing, base):
        for n, k in enumerate(order):
            push(half(off_y, k), landing.at[k], base + n, y_peer)

    def y_sum(half, landing, outgoing, base, n):
        k = order[n]
        arrive(landing.at[k], base + n)
        outgoing[k] = (half(y, k)[...].astype(F32) + landing[k].astype(F32)).astype(BF16)

    def owner_stage(outgoing, landing, base, n):
        k = order[n]
        for w in range(nb):
            to = (y * 2 + w % 2, k * 2 + w // 2)
            own = n == nz - 1
            push(
                outgoing.at[k, w % 2, w // 2], landing.at[v, z], base + n * nb + w, to,
                base + z * nb + v, v != w if own else None,
            )
        if own:
            landing[v, z] = outgoing[z, x, core]

    def owner_sum(landing, base, result):
        for n, k in enumerate(order):
            for w in range(nb):
                arrive(landing.at[w, k], base + k * nb + w, v != w if n == nz - 1 else None)
        for q in range(nb):
            result[q] = sum(landing[q, k].astype(F32) for k in range(nz))

    s_gic, s_gio = slots(nz), slots(nz * nb)
    s_goc, s_goz = slots(nz), slots(nz)

    gated_all = gated_send[...].reshape(length, part)
    go_sum[...] = mm(gated_all, cot[...].reshape(length, D), TN).astype(BF16).reshape(go_sum.shape)
    y_stage(go_half, go_core, s_goc)

    def weight_grad(t, carry):
        cols = at(t, LANES)
        got = mm(normed[:, cols], grad_pre[...], TN).astype(BF16)
        gi_sum[t // 2, t % 2] = got.reshape(gi_sum.shape[2:])
        return carry

    lax.fori_loop(0, nb, weight_grad, 0)
    y_stage(gi_half, gi_core, s_gic)

    s_ig = slots(nb)

    def input_part(r, carry):
        i = nb - 1 - r
        rows = at(i, group)
        x_part(i).wait_recv()
        for k in range(1, nb):
            arrive(stats_one.at[row_from(k), i], s_s1 + i * nb + k)
        total = (
            part_send[i, v].astype(F32) + part_core[i, x].astype(F32) + part_got[i].astype(F32)
        )
        row = sum(stats_one[q, i] for q in range(nb)) * (1.0 / D)
        row = jnp.concatenate(
            [
                jnp.concatenate([row[n * 4 + m : n * 4 + m + 1] for m in range(4)], axis=1)
                for n in range(2)
            ],
            axis=0,
        )
        padded[0:2, :] = row
        turned = jnp.transpose(padded[...])
        mean_one, inverse_one = fix[rows, 0:1], fix[rows, 1:2]
        mycols = at(v, part)
        hat_one = (embedded[rows, mycols].astype(F32) - mean_one) * inverse_one
        gain_sum[0:1, :] += jnp.sum(total * hat_one, axis=0, keepdims=True)
        gain_sum[1:2, :] += jnp.sum(total, axis=0, keepdims=True)
        back = (total * gain_one_own - turned[:, 0:1] - hat_one * turned[:, 1:2]) * inverse_one
        ig_send[i] = (cot[i, :, mycols].astype(F32) + back).astype(BF16)
        return carry

    s_tgc, s_tgo = slots(nz), slots(nz * nb)

    def gi_over(n):
        y_sum(gi_half, gi_core, gi_z, s_gic, n)
        owner_stage(gi_z, gi_got, s_gio, n)

    def table_rows(i, t):
        hot = jnp.where(iota((group, group), 0) + t * group == index[i][0:1], 1.0, 0.0)
        return mm(hot.astype(BF16), ig_send[i])

    def table_add(i, first):
        def add(t, carry):
            rows = at(t, group)
            got = table_rows(i, t)
            table_acc[rows, :] = got if first else table_acc[rows, :] + got
            return carry

        lax.fori_loop(0, items // group, add, 0)

    def table_part(t, carry):
        got = (table_acc[at(t, group), :] + table_rows(0, t)).astype(BF16)
        table_sum[t // 2, t % 2] = got.reshape(table_sum.shape[2:])
        return carry

    for r in range(nb - 1):
        input_part(r, 0)
        table_add(nb - 1 - r, r == 0)
        if r == 1:
            gi_over(0)
            gi_over(1)
        if r == 2:
            gi_over(2)
    input_part(nb - 1, 0)
    lax.fori_loop(off_y * 2, off_y * 2 + 2, table_part, 0)
    y_stage(table_half, table_core, s_tgc)
    for k in range(nb):
        i = lax.rem(b + k, nb)
        push(ig_send.at[i], ig_got.at[v], s_ig + k, (i, z * 2 + y), s_ig + v, away if k == 0 else None)

    @pl.when(home)
    def keep_input():
        ig_got[v] = ig_send[b]

    lax.fori_loop(y * 2, y * 2 + 2, table_part, 0)
    gi_over(3)
    for n in range(nz):
        y_sum(go_half, go_core, go_z, s_goc, n)
    for k in range(nz):
        push(go_z.at[z_to(k)], go_got.at[z], s_goz + k, (v, z_to(k) * 2 + y), None, away if k == 0 else None)

    @pl.when(home)
    def keep_rows():
        go_got[z] = go_z[z]


    s_l, s_lx = slots(nd), slots(1)
    own_items = items // nb

    def count(t, carry):
        picked = column[at(t, step), 0:1]
        hit = jnp.where(iota((step, own_items), 1) + v * own_items == picked, 1.0, 0.0)
        return carry + jnp.sum(hit, axis=0, keepdims=True)

    counted = lax.fori_loop(0, length // step, count, jnp.zeros((1, own_items), F32))
    time_grad = jnp.where(low, bias_sum[0:1, :], pltpu.roll(bias_sum[1:2, :], NB, 1))
    pos_grad = jnp.where(low, pltpu.roll(bias_sum[2:3, :], NB, 1), bias_sum[3:4, :])
    halved = 0.5 * inv_length
    little[...] = jnp.zeros(little.shape, F32)
    little[0:4, :] = gain_sum[0:4, :]
    little[4:5, :] = pos_grad * halved
    little[5:6, :] = time_grad * halved
    for q in range(own_items // LANES):
        little[8 + q : 9 + q, :] = counted[:, q * LANES : (q + 1) * LANES]
    columns = [(ky, kz) for kz in range(nz) for ky in range(2) if ky + kz > 0]
    for ky, kz in columns:
        to = (lax.rem(y + ky, 2) * 2 + x, z_to(kz) * 2 + core)
        push(little, little_parts.at[kz * 2 + ky], s_l + kz * 2 + ky, to)
    def from_row(landing, base):
        for w in range(nb):
            arrive(landing.at[w], base + w, jnp.logical_or(away, v != w))

    from_row(gated_got, s_gt)
    arrive(outw.at[other * 2 + off_x], s_ox + 1)

    def finish_layer(t, carry):
        rows = at(t, step)
        hot = jnp.where(iota((step, items), 1) == own_column[rows, 0:1], 1.0, 0.0).astype(BF16)
        result = mm(hot, table[...].reshape(items, D))
        for q in range(nb):
            result = result + mm(gated_got[q, rows, :], outw[q].reshape(part, D))
        layer_out[rows, :] = result.astype(BF16)
        return carry

    lax.fori_loop(0, group // step, finish_layer, 0)

    for n in range(nz):
        y_sum(table_half, table_core, table_z, s_tgc, n)
        owner_stage(table_z, table_got, s_tgo, n)
    totals = little[...]
    for ky, kz in columns:
        arrive(little_parts.at[kz * 2 + ky], s_l + kz * 2 + ky)
        totals = totals + little_parts[kz * 2 + ky]
    little_all[...] = totals
    push(little_all, little_got, s_lx, core_peer)

    owner_sum(gi_got, s_gio, grad_in_out)
    for k in range(nz):
        arrive(go_got.at[z_from(k)], s_goz + k, away if k == 0 else None)
    grad_out_out[...] = sum(go_got[k].astype(F32) for k in range(nz))
    from_row(ig_got, s_ig)
    input_out[...] = ig_got[...]
    arrive(little_got, s_lx)

    @pl.when(home)
    def keep_own():
        little_out[...] = little_all[...]

    @pl.when(away)
    def take_peers():
        little_out[...] = little_got[...]

    owner_sum(table_got, s_tgo, table_out)

    for where, *sent in pending:
        if where is None:
            copy(*sent).wait_send()
        else:
            pl.when(where)(copy(*sent).wait_send)

    def drain(i, carry):
        for k in range(1, nb):
            to = row_peer(k)[1]
            copy(stats.at[v, i], stats.at[v, i], s_st + i * nb + k, to).wait_send()
            copy(stats_one.at[v, i], stats_one.at[v, i], s_s1 + i * nb + k, to).wait_send()
        core_part(i).wait_send()
        x_part(i).wait_send()
        sent_gated = copy(gated_send.at[i], gated_got.at[v], s_gt + i, (i, z * 2 + y), s_gt + v)
        pl.when(jnp.logical_or(away, i != b))(sent_gated.wait_send)
        return carry

    lax.fori_loop(0, nb, drain, 0)
    assert counter[0] <= send.shape[0], counter[0]


def finish_kernel(sizes, *refs):
    nb, nz, group, items, weight_rows, tokens = sizes
    part = D // nb
    rows_table = items // (nb * nz * 2)
    (
        layer_in, input_in, table_in, grad_in_in, grad_out_in, little_in,
        proj_in, proj_out, small_in,
        moment_in, second_in, moment_out, second_out, moment_small, second_small,
        layer_out, input_grad, table_grad, counts_out, logq_out,
        new_m_in, new_s_in, new_w_in, new_m_out, new_s_out, new_w_out,
        new_m_small, new_s_small, new_w_small,
    ) = refs
    d = lax.axis_index("dp")
    layer_out[...] = layer_in[...]
    for q in range(nb):
        cols = slice(q * part, (q + 1) * part)
        input_grad[:, cols] = input_in[q].astype(F32)
        table_grad[:, cols] = table_in[q]
        for s in range(4):
            own = slice(s * D + q * part, s * D + (q + 1) * part)
            new_m_in[:, own], new_s_in[:, own], new_w_in[:, own] = adam_update(
                proj_in[:, own], grad_in_in[q, :, s * part : (s + 1) * part],
                moment_in[:, own], second_in[:, own], rate_in,
            )
    new_m_out[...], new_s_out[...], new_w_out[...] = adam_update(
        proj_out[...], grad_out_in[...], moment_out[...], second_out[...], rate_out
    )
    width = small_in.shape[1]
    shifted = pltpu.roll(little_in[0:8, :], lax.rem(LANES - d * width, LANES), 1)[0:6, 0:width]
    new_m_small[...], new_s_small[...], new_w_small[...] = adam_update(
        small_in[...], shifted, moment_small[...], second_small[...], rate_small
    )
    per_row = LANES // rows_table
    count_row = little_in[pl.ds(8 + d // per_row, 1), :]
    count_row = pltpu.roll(
        jnp.broadcast_to(count_row, (8, LANES)),
        lax.rem(LANES - lax.rem(d, per_row) * rows_table, LANES), 1,
    )[0:1, 0:rows_table]
    counts_out[...] = count_row
    logq_out[...] = jnp.log(jnp.maximum(count_row, 1.0) * (1.0 / tokens))


def fused(sizes, args):
    nb, nz, group, items, weight_rows, tokens = sizes
    nd = nz * 2
    length = nb * group
    part = D // nb
    rows_table = items // (nb * nd)
    (
        item_ids, pos_buckets, time_buckets, item_table, proj_in, proj_out, small_params, out_grad,
        moment_in, second_in, moment_out, second_out, moment_small, second_small,
    ) = args
    width = small_params.shape[1]
    shape = jax.ShapeDtypeStruct
    middle = [
        shape((group, D), BF16), shape((nb, group, part), BF16), shape((nb, rows_table, part), F32),
        shape((nb, weight_rows, 4 * part), F32), shape((weight_rows, D), F32), shape((16, LANES), F32),
    ]
    outs = [
        shape((group, D), BF16), shape((group, D), F32), shape((rows_table, D), F32),
        shape((1, rows_table), F32), shape((1, rows_table), F32),
        *[shape(proj_in.shape, F32)] * 3, *[shape(proj_out.shape, F32)] * 3,
        *[shape(small_params.shape, F32)] * 3,
    ]
    vm = pltpu.VMEM
    scratch = [
        pltpu.SemaphoreType.DMA((256,)), pltpu.SemaphoreType.DMA((256,)), pltpu.SemaphoreType.DMA((2,)),
        vm((nb, 8, group), I32),
        vm((8, group), I32),
        vm((length, LANES), I32),
        vm((group, LANES), I32),
        vm((LANES, group), F32),
        vm((nd, nb, rows_table, D), BF16),
        vm((2, 2, nz, 2, weight_rows, 4 * part), BF16),
        vm((nb, weight_rows, 4 * part), BF16),
        vm((nb, nd, weight_rows, D), BF16),
        vm((2, 2, nz, 2, 16, LANES), BF16),
        vm((nb, 16, LANES), F32),
        vm((nb, group, D), BF16),
        vm((length, D), BF16),
        vm((length, D), BF16),
        vm((length, 4 * part), F32),
        vm((length, part), F32),
        vm((length, part), BF16),
        vm((2, length, 2 * LANES), BF16),
        vm((2, length, 2 * LANES), BF16),
        vm((length, part), F32),
        vm((length, part), F32),
        vm((nb, nb, 8, group // 2), F32),
        vm((length, LANES), F32),
        vm((nb, group, part), BF16),
        vm((nb, group, part), BF16),
        vm((2, group, part), BF16),
        vm((2, group, 2 * LANES), F32),
        vm((nb, group, part), F32),
        vm((nb, group, part), F32),
        vm((length, 4 * part), BF16),
        vm((nb, nb, group, part), BF16),
        vm((nb, 2, group, part), BF16),
        vm((nb, group, part), BF16),
        vm((nb, group, part), BF16),
        vm((nb, nb, 8, LANES), F32),
        vm((nb, group, part), BF16),
        vm((nb, group, part), BF16),
        vm((8, LANES), F32),
        vm((8, LANES), F32),
        vm((items, part), F32),
        vm((2, 2, nz, 2, rows_table, part), BF16),
        *[vm((nz, 2, 2, rows_table, part), BF16)] * 2,
        vm((nb, nz, rows_table, part), BF16),
        vm((2, 2, nz, 2, weight_rows, 4 * part), BF16),
        *[vm((nz, 2, 2, weight_rows, 4 * part), BF16)] * 2,
        vm((nb, nz, weight_rows, 4 * part), BF16),
        vm((nz, 2, weight_rows, D), BF16),
        *[vm((nz, weight_rows, D), BF16)] * 3,
        vm((16, LANES), F32),
        vm((nd, 16, LANES), F32),
        *[vm((16, LANES), F32)] * 2,
    ]
    whole, far = pl.BlockSpec(memory_space=pltpu.VMEM), pl.BlockSpec(memory_space=pl.ANY)
    between = pl.pallas_call(
        functools.partial(fused_kernel, sizes),
        out_shape=middle,
        in_specs=[whole] * 3 + [far] + [whole] * 3 + [far],
        out_specs=[whole] * len(middle),
        scratch_shapes=scratch,
        compiler_params=pltpu.CompilerParams(
            collective_id=0, has_side_effects=True, vmem_limit_bytes=60 * 2**20
        ),
        name="hstu_step",
    )(
        item_ids, pos_buckets, time_buckets,
        item_table.reshape(nb, item_table.shape[0] // nb, D),
        proj_in, proj_out, small_params, out_grad.reshape(group, D),
    )
    got = pl.pallas_call(
        functools.partial(finish_kernel, sizes),
        out_shape=outs,
        in_specs=[whole] * (len(middle) + 9),
        out_specs=[whole] * len(outs),
        name="hstu_finish",
    )(
        *between, proj_in, proj_out, small_params,
        moment_in, second_in, moment_out, second_out, moment_small, second_small,
    )
    return (
        got[0].reshape(out_grad.shape), got[1].reshape(out_grad.shape), got[2],
        got[3].reshape(rows_table), got[4].reshape(rows_table), *got[5:],
    )


def per_device(*args):
    item_ids, item_table, proj_in, small_params = args[0], args[3], args[4], args[6]
    seq_count, group = item_ids.shape
    nb, nd = lax.axis_size("blk"), lax.axis_size("dp")
    items = item_table.shape[0] * nd
    by_heads = (
        seq_count == 1 and nd % 2 == 0 and D // nb == LANES and group % 256 == 0
        and items == 2048 and proj_in.shape[0] % 16 == 0
        and small_params.shape[1] * nd == LANES and nb == 4 and nd == 8
    )
    if by_heads:
        sizes = (nb, nd // 2, group, items, proj_in.shape[0], nd * nb * group)
        return fused(sizes, args)
    return by_events(*args)


def solution(mesh):
    placed = (
        P("dp", "blk"),
        P("dp", "blk"),
        P("dp", "blk"),
        P("dp", None),
        P(("blk", "dp"), None),
        P(("blk", "dp"), None),
        P(None, ("blk", "dp")),
        P("dp", "blk", None),
        P(("blk", "dp"), None),
        P(("blk", "dp"), None),
        P(("blk", "dp"), None),
        P(("blk", "dp"), None),
        P(None, ("blk", "dp")),
        P(None, ("blk", "dp")),
    )
    return jax.shard_map(
        per_device,
        mesh=mesh,
        in_specs=placed,
        out_specs=(
            P("dp", "blk", None),
            P("dp", "blk", None),
            P(("blk", "dp"), None),
            P(("blk", "dp")),
            P(("blk", "dp")),
            P(("blk", "dp"), None),
            P(("blk", "dp"), None),
            P(("blk", "dp"), None),
            P(("blk", "dp"), None),
            P(("blk", "dp"), None),
            P(("blk", "dp"), None),
            P(None, ("blk", "dp")),
            P(None, ("blk", "dp")),
            P(None, ("blk", "dp")),
        ),
        check_vma=False,
    )
```
